128 devices in a mesh: row: 8 (over z, y_lo), col: 16 (over y_hi, x, core).
Axes of the slice: x: 4, y: 4 (y_hi: 2, y_lo: 2; y = y_hi * 2 + y_lo), z: 4, core: 2. Of those that a mesh axis runs over, the one named last changes fastest.
Arguments:
- spectra: bfloat16 [2048, 256, 512], P(('row', 'col')), may hold values from 0.05 to 20000
- sensor_ids: int32 [2048, 1], P(('row', 'col')), may hold values from 0 to 255, as said below
- permutation: int32 [2048], P(('row', 'col')), may hold values from 0 to 2047, as said below
- w_enc1: bfloat16 [2048, 256], replicated, may hold values from -0.125 to 0.125
- w_enc2: bfloat16 [1024, 256], replicated, may hold values from -0.1875 to 0.1875
- w_dec1: bfloat16 [256, 1024], replicated, may hold values from -0.25 to 0.25
- w_dec2: bfloat16 [256, 2048], replicated, may hold values from -0.25 to 0.25
Outputs:
- grad_enc1: float32 [2048, 256], replicated
- grad_enc2: float32 [1024, 256], replicated
- grad_dec1: float32 [256, 1024], replicated
- grad_dec2: float32 [256, 2048], replicated
The draws below stay inside these ranges and needn't reach their ends.
Inputs may be any that keep to these rules, and one draw needn't show every extreme that they name: `sensor_ids`: every sensor from 0 to 255 recorded exactly 8 windows. A permutation of all slots; the 16 windows of the ingest device with indices (a, b) go to 16 different trainers, one to each trainer whose col index c has c // 2 = a; each trainer thus receives one window from each ingest device of one row index.
All inputs are finite; a program needn't handle non-finite values.
Results may differ from the reference program's by a relative error of at most 0.004.
Values may be sent and summed in bfloat16 or wider, within the bound.
No kernel may reach another device: no remote copies, remote signals or barrier semaphores. Data moves between devices by JAX's collectives and lax.ppermute only.
A program may use at most 192 MiB of HBM per device.

```python
import math
import jax
import jax.numpy as jnp
from jax import lax

BINS = 512
CH = 256
WIN_SENSOR = 8
FRAMES = 256
WIN_DEV = 16
PER_ROW = 2
WINDOWS = 2048
SENSORS = 256


def sensor_draw(key):
    sensor_key = jax.random.fold_in(key, 11)
    order = jax.random.permutation(sensor_key, WINDOWS)
    return (order // WIN_SENSOR).astype(jnp.int32)


def draw_sensor_ids(key, part):
    return sensor_draw(key)[:, None]


def draw_spectra(key, part):
    first_key, second_key = jax.random.split(key, 2)
    loud_key = jax.random.fold_in(key, 13)
    labels = sensor_draw(key)
    position = jnp.arange(WINDOWS, dtype=jnp.float32) / WINDOWS
    sensor_gain = 10.0 ** jax.random.uniform(loud_key, (SENSORS,), jnp.float32, 0.0, 1.0)
    gain = sensor_gain[labels] * 10.0 ** position
    frame_gain = jnp.exp(jax.random.uniform(first_key, (WINDOWS, FRAMES, 1), jnp.float32, math.log(0.5), math.log(2.0)))
    texture = jnp.exp(jax.random.uniform(second_key, (WINDOWS, FRAMES, BINS), jnp.float32, math.log(0.1), math.log(10.0)))
    return (gain[:, None, None] * frame_gain * texture).astype(jnp.bfloat16)


def draw_permutation(key, part):
    col_total = WIN_DEV
    device_total = WINDOWS // WIN_DEV
    subkeys = jax.random.split(jax.random.fold_in(key, 7), 2)
    offsets = jax.random.randint(subkeys[0], (device_total,), 0, col_total)
    stored = jax.vmap(lambda single: jax.random.permutation(single, col_total))(jax.random.split(subkeys[1], device_total))
    device = jnp.arange(device_total, dtype=jnp.int32)[:, None]
    source_row = device // col_total
    source_col = device % col_total
    dest_row = stored // PER_ROW
    dest_col = source_row * PER_ROW + stored % PER_ROW
    dest_dev = dest_row * col_total + dest_col
    slot = (source_col + offsets[dest_dev]) % col_total
    return (dest_dev * col_total + slot).reshape(-1).astype(jnp.int32)


def scatter_about(rng, extent, spread, most, held_as=jnp.bfloat16):
    values = jax.random.normal(rng, extent, jnp.float32) * spread
    return jnp.minimum(jnp.maximum(values, -most), most).astype(held_as)


def setup_inputs(seed: int = 0) -> dict:
    streams_of = jax.random.split(jax.random.key(seed), 8)
    spectra = draw_spectra(jax.random.fold_in(streams_of[7], 71), 0)
    sensor_ids = draw_sensor_ids(jax.random.fold_in(streams_of[7], 71), 0)
    permutation = draw_permutation(jax.random.fold_in(streams_of[7], 71), 0)
    w_enc1 = scatter_about(streams_of[3], (4 * BINS, CH), (4 * BINS) ** -0.5, 0.125)
    w_enc2 = scatter_about(streams_of[4], (4 * CH, CH), (4 * CH) ** -0.5, 0.1875)
    w_dec1 = scatter_about(streams_of[5], (CH, 4 * CH), (2 * CH) ** -0.5, 0.25)
    w_dec2 = scatter_about(streams_of[6], (CH, 4 * BINS), (2 * CH) ** -0.5, 0.25)
    return dict(spectra=spectra, sensor_ids=sensor_ids, permutation=permutation, w_enc1=w_enc1, w_enc2=w_enc2, w_dec1=w_dec1, w_dec2=w_dec2)


EPS = 1e-05

def frame_taps(values):
    windows, length, channels = values.shape
    padded = jnp.pad(values, ((0, 0), (1, 1), (0, 0)))
    paired = padded.reshape(windows, length // 2 + 1, 2 * channels)
    return jnp.concatenate([paired[:, :-1], paired[:, 1:]], axis=2)

def fold_taps(stacked):
    windows, length, columns = stacked.shape
    channels = columns // 4
    pieces = stacked.reshape(windows, length, 4, channels)
    blank = jnp.zeros((windows, 1, channels), stacked.dtype)
    even_rows = pieces[:, :, 1] + jnp.concatenate([blank, pieces[:, :-1, 3]], axis=1)
    odd_rows = pieces[:, :, 2] + jnp.concatenate([pieces[:, 1:, 0], blank], axis=1)
    return jnp.stack([even_rows, odd_rows], axis=2).reshape(windows, 2 * length, channels)

def silu_slope(values):
    logistic = jax.nn.sigmoid(values)
    return logistic * (1.0 + values * (1.0 - logistic))

def forward_dot(values, weight):
    flat = values.reshape(-1, values.shape[-1]).astype(jnp.float32)
    result = jnp.dot(flat, weight.astype(jnp.float32), precision=lax.Precision.HIGHEST, preferred_element_type=jnp.float32)
    return result.reshape(values.shape[:-1] + (weight.shape[1],))

def backward_dot(values, weight):
    flat = values.reshape(-1, values.shape[-1]).astype(jnp.float32)
    result = jnp.dot(flat, weight.astype(jnp.float32).T, precision=lax.Precision.HIGHEST, preferred_element_type=jnp.float32)
    return result.reshape(values.shape[:-1] + (weight.shape[0],))

def weight_grad(left, right):
    left_flat = left.reshape(-1, left.shape[-1]).astype(jnp.float32)
    right_flat = right.reshape(-1, right.shape[-1]).astype(jnp.float32)
    return jnp.dot(left_flat.T, right_flat, precision=lax.Precision.HIGHEST, preferred_element_type=jnp.float32)

def group_grads(normed, w_enc1, w_enc2, w_dec1, w_dec2):
    stem_taps = frame_taps(normed)
    enc1_pre = forward_dot(stem_taps, w_enc1)
    middle = lax.optimization_barrier(jnp.mean(enc1_pre, axis=(0, 1)))
    variance = lax.optimization_barrier(jnp.mean(jnp.square(enc1_pre - middle), axis=(0, 1)))
    inverse = lax.rsqrt(variance + EPS)
    enc1_hat = (enc1_pre - middle) * inverse
    enc1_out = jax.nn.silu(enc1_hat).astype(jnp.bfloat16)
    mid_taps = frame_taps(enc1_out)
    enc2_pre = forward_dot(mid_taps, w_enc2)
    enc2_out = jax.nn.silu(enc2_pre).astype(jnp.bfloat16)
    dec1_pre = fold_taps(forward_dot(enc2_out, w_dec1))
    dec1_out = jax.nn.silu(dec1_pre).astype(jnp.bfloat16)
    rebuilt = fold_taps(forward_dot(dec1_out, w_dec2))
    delta_out = ((rebuilt - normed.astype(jnp.float32)) / WINDOWS).astype(jnp.bfloat16)
    out_taps = frame_taps(delta_out)
    grad_dec2 = weight_grad(dec1_out, out_taps)
    delta_dec1 = (backward_dot(out_taps, w_dec2) * silu_slope(dec1_pre)).astype(jnp.bfloat16)
    dec_taps = frame_taps(delta_dec1)
    grad_dec1 = weight_grad(enc2_out, dec_taps)
    delta_enc2 = (backward_dot(dec_taps, w_dec1) * silu_slope(enc2_pre)).astype(jnp.bfloat16)
    grad_enc2 = weight_grad(mid_taps, delta_enc2)
    back_enc1 = fold_taps(backward_dot(delta_enc2, w_enc2)) * silu_slope(enc1_hat)
    first_mean = lax.optimization_barrier(jnp.mean(back_enc1, axis=(0, 1)))
    second_mean = lax.optimization_barrier(jnp.mean(back_enc1 * enc1_hat, axis=(0, 1)))
    delta_enc1 = ((back_enc1 - first_mean - enc1_hat * second_mean) * inverse).astype(jnp.bfloat16)
    grad_enc1 = weight_grad(stem_taps, delta_enc1)
    return (grad_enc1, grad_enc2, grad_dec1, grad_dec2)

def reference(spectra, sensor_ids, permutation, w_enc1, w_enc2, w_dec1, w_dec2):
    groups = WINDOWS // WIN_DEV
    sensor = sensor_ids[:, 0].astype(jnp.int32)
    blocks = spectra.reshape(groups, WIN_DEV, FRAMES, BINS)

    def window_stats(block):
        log_power = jnp.log1p(block.astype(jnp.float32))
        return (lax.optimization_barrier(jnp.sum(log_power, axis=1)), lax.optimization_barrier(jnp.sum(log_power * log_power, axis=1)))
    win_sums, win_squares = lax.map(window_stats, blocks)
    win_sums = win_sums.reshape(WINDOWS, BINS)
    win_squares = win_squares.reshape(WINDOWS, BINS)
    totals = jax.ops.segment_sum(win_sums, sensor, num_segments=SENSORS)
    squares = jax.ops.segment_sum(win_squares, sensor, num_segments=SENSORS)
    counts = jax.ops.segment_sum(jnp.ones((WINDOWS,), jnp.float32), sensor, num_segments=SENSORS) * FRAMES
    center = totals / counts[:, None]
    factor = lax.rsqrt(squares / counts[:, None] - center * center + EPS)
    ranking = jnp.argsort(permutation).astype(jnp.int32).reshape(groups, WIN_DEV)

    def group_step(running, members):
        log_power = jnp.log1p(spectra[members].astype(jnp.float32))
        member_ids = sensor[members]
        normed = ((log_power - center[member_ids][:, None, :]) * factor[member_ids][:, None, :]).astype(jnp.bfloat16)
        gradients = group_grads(normed, w_enc1, w_enc2, w_dec1, w_dec2)
        return (tuple((a + b for a, b in zip(running, gradients))), None)
    starts = (jnp.zeros((4 * BINS, CH), jnp.float32), jnp.zeros((4 * CH, CH), jnp.float32), jnp.zeros((CH, 4 * CH), jnp.float32), jnp.zeros((CH, 4 * BINS), jnp.float32))
    result, _ = lax.scan(group_step, starts, ranking)
    return (result[0], result[1], result[2], result[3])
```

```python
import functools

import jax
import jax.numpy as jnp
from jax import lax
from jax.experimental import pallas as pl
from jax.experimental.pallas import tpu as pltpu
from jax.sharding import PartitionSpec as P

WIN_SENSOR = 8
EPS = 1e-05
F32 = jnp.float32
BF16 = jnp.bfloat16
LANES = 128
STEP_WINDOWS = 4
VMEM_LIMIT = 56 * 1024 * 1024


def dot(left, right):
    return jnp.dot(left, right, preferred_element_type=F32)


def dot_nt(left, right):
    return lax.dot_general(left, right, (((1,), (1,)), ((), ())), preferred_element_type=F32)


def dot_tn(left, right):
    return lax.dot_general(left, right, (((0,), (0,)), ((), ())), preferred_element_type=F32)


def split3(values):
    first = values.astype(BF16)
    rest = values - first.astype(F32)
    second = rest.astype(BF16)
    third = (rest - second.astype(F32)).astype(BF16)
    return first, second, third


def sigmoid(values):
    return 1.0 / (1.0 + jnp.exp(-values))


def shift_down(values, period):
    rows = lax.broadcasted_iota(jnp.int32, values.shape, 0) % period
    return jnp.where(rows == 0, 0.0, pltpu.roll(values, 1, 0))


def shift_up(values, period):
    total = values.shape[0]
    rows = lax.broadcasted_iota(jnp.int32, values.shape, 0) % period
    return jnp.where(rows == period - 1, 0.0, pltpu.roll(values, total - 1, 0))


def group_rank(perm_ref, window, window_dev, col_count):
    trainer = perm_ref[window] // window_dev
    per_row = 2
    return (trainer // col_count) * per_row + trainer % per_row


def sums_kernel(spec_ref, ids_ref, out_ref, acc, *, chunks):
    step = pl.program_id(0)
    windows, frames, bins = spec_ref.shape
    rows = 16

    for w in range(windows):
        def body(i, carry):
            total, square = carry
            start = pl.multiple_of(i * rows, rows)
            value = jnp.log(1.0 + spec_ref[w, pl.ds(start, rows), :].astype(F32))
            value_sq = value * value
            return (total + value[0:8] + value[8:16], square + value_sq[0:8] + value_sq[8:16])

        zero = jnp.zeros((8, bins), F32)
        total, square = lax.fori_loop(0, frames // rows, body, (zero, zero), unroll=4)
        total = jnp.sum(total, axis=0, keepdims=True)
        square = jnp.sum(square, axis=0, keepdims=True)
        pieces = [total[:, k * LANES:(k + 1) * LANES] for k in range(chunks)]
        pieces += [square[:, k * LANES:(k + 1) * LANES] for k in range(chunks)]
        start = pl.multiple_of((step * windows + w) * 2 * chunks, 2 * chunks)
        acc[pl.ds(start, 2 * chunks), :] = jnp.concatenate(pieces, axis=0)

    @pl.when(step == pl.num_programs(0) - 1)
    def _():
        count = ids_ref.shape[0]
        acc[LANES:2 * LANES, :] = jnp.zeros((LANES, LANES), F32)
        acc[LANES:LANES + count, :] = jnp.broadcast_to(ids_ref[...].astype(F32), (count, LANES))
        out_ref[:, 0:LANES] = acc[0:LANES, :].T
        out_ref[:, LANES:2 * LANES] = acc[LANES:2 * LANES, :].T


def sums_call(spectra, sensor_ids):
    windows, frames, bins = spectra.shape
    chunks = bins // LANES
    return pl.pallas_call(
        functools.partial(sums_kernel, chunks=chunks),
        grid=(windows // STEP_WINDOWS,),
        in_specs=[
            pl.BlockSpec((STEP_WINDOWS, frames, bins), lambda i: (i, 0, 0)),
            pl.BlockSpec(sensor_ids.shape, lambda i: (0, 0)),
        ],
        out_specs=pl.BlockSpec((LANES, 2 * LANES), lambda i: (0, 0)),
        out_shape=jax.ShapeDtypeStruct((LANES, 2 * LANES), F32),
        scratch_shapes=[pltpu.VMEM((2 * LANES, LANES), F32)],
        compiler_params=pltpu.CompilerParams(vmem_limit_bytes=VMEM_LIMIT),
        name="window_sums",
    )(spectra, sensor_ids)


def stats_kernel(in_ref, out_ref, *, windows, chunks, sensors, per_sensor):
    width = 2 * chunks
    data = in_ref[:, 0:LANES].T
    labels = in_ref[:, LANES:2 * LANES].T
    sensor_rows = lax.broadcasted_iota(jnp.int32, (sensors, LANES), 0).astype(F32)
    tables = [(sensor_rows == labels[w:w + 1, :]).astype(F32).astype(BF16) for w in range(windows)]
    table = jnp.concatenate(tables, axis=1)
    values = jnp.concatenate([data[w * width:(w + 1) * width, :] for w in range(windows)], axis=1)
    parts = dot_nt(jnp.concatenate(split3(values), axis=0), table)
    sums = parts[0:width] + parts[width:2 * width] + parts[2 * width:3 * width]
    center = sums[0:chunks] / per_sensor
    factor = lax.rsqrt(sums[chunks:width] / per_sensor - center * center + EPS)
    both = jnp.concatenate([center, factor], axis=0)
    back = dot(jnp.concatenate(split3(both), axis=0), table)
    back = back[0:width] + back[width:2 * width] + back[2 * width:3 * width]
    rows = jnp.concatenate([back[:, w * LANES:(w + 1) * LANES] for w in range(windows)], axis=0)
    out_ref[...] = rows.T


def stats_call(received, windows, chunks, sensors, per_sensor):
    return pl.pallas_call(
        functools.partial(stats_kernel, windows=windows, chunks=chunks, sensors=sensors, per_sensor=float(per_sensor)),
        out_shape=jax.ShapeDtypeStruct((LANES, LANES), F32),
        compiler_params=pltpu.CompilerParams(vmem_limit_bytes=VMEM_LIMIT),
        name="sensor_stats",
    )(received)


def enc1_kernel(perm_ref, spec_ref, coef_ref, w_ref, normed_ref, pre_ref, stat_ref, coef, lane, stat, *, chunks, cols, copies):
    step = pl.program_id(0)
    windows, frames, bins = spec_ref.shape
    quarter = frames // 4
    channels = w_ref.shape[1]
    all_windows = windows * pl.num_programs(0)
    width = 2 * chunks

    @pl.when(step == 0)
    def _():
        coef[...] = coef_ref[...].T

    rows = 32
    for w in range(windows):
        start = pl.multiple_of((step * windows + w) * width, width)
        both = coef[pl.ds(start, width), :]

        def body(i, carry):
            at = pl.multiple_of(i * rows, rows)
            value = jnp.log(1.0 + spec_ref[w, pl.ds(at, rows), :].astype(F32))
            for k in range(chunks):
                part = value[:, k * LANES:(k + 1) * LANES]
                lane[w % 2, k, pl.ds(at, rows), :] = (part - both[k:k + 1, :]) * both[chunks + k:chunks + k + 1, :]
            return carry

        lax.fori_loop(0, frames // rows, body, 0, unroll=2)
        for i in range(4):
            for k in range(chunks):
                picked = lane[w % 2, k, pl.ds(i, quarter, stride=4), :]
                normed_ref[i, w * quarter:(w + 1) * quarter, k * LANES:(k + 1) * LANES] = picked.astype(BF16)

    w0, w1, w2, w3 = (w_ref[k * bins:(k + 1) * bins, :] for k in range(4))
    f0, f1, f2, f3 = (normed_ref[i] for i in range(4))
    even = shift_down(dot(f3, w0), quarter) + dot(f0, w1) + dot(f1, w2) + dot(f2, w3)
    odd = dot(f1, w0) + dot(f2, w1) + dot(f3, w2) + shift_up(dot(f0, w3), quarter)
    pre_ref[0] = even
    pre_ref[1] = odd
    for w in range(windows):
        part_e = even[w * quarter:(w + 1) * quarter]
        part_o = odd[w * quarter:(w + 1) * quarter]
        mean = (jnp.sum(part_e, axis=0, keepdims=True) + jnp.sum(part_o, axis=0, keepdims=True)) / (2 * quarter)
        diff_e = part_e - mean
        diff_o = part_o - mean
        spread = (jnp.sum(diff_e * diff_e, axis=0, keepdims=True) + jnp.sum(diff_o * diff_o, axis=0, keepdims=True)) / (2 * quarter)
        place = group_rank(perm_ref, step * windows + w, all_windows, cols)
        stat[pl.ds(place, 1), 0:channels] = mean
        stat[pl.ds(place, 1), channels:2 * channels] = spread

    @pl.when(step == pl.num_programs(0) - 1)
    def _():
        for d in range(copies):
            stat_ref[d] = stat[...]


def enc1_call(permutation, spectra, coef, w_enc1, cols):
    windows, frames, bins = spectra.shape
    chunks = bins // LANES
    quarter = frames // 4
    channels = w_enc1.shape[1]
    rows = STEP_WINDOWS * quarter
    grid_spec = pltpu.PrefetchScalarGridSpec(
        num_scalar_prefetch=1,
        grid=(windows // STEP_WINDOWS,),
        in_specs=[
            pl.BlockSpec((STEP_WINDOWS, frames, bins), lambda i, p: (i, 0, 0)),
            pl.BlockSpec((LANES, LANES), lambda i, p: (0, 0)),
            pl.BlockSpec(w_enc1.shape, lambda i, p: (0, 0)),
        ],
        out_specs=[
            pl.BlockSpec((4, rows, bins), lambda i, p: (0, i, 0)),
            pl.BlockSpec((2, rows, channels), lambda i, p: (0, i, 0)),
            pl.BlockSpec((cols, windows, 2 * channels), lambda i, p: (0, 0, 0)),
        ],
        scratch_shapes=[
            pltpu.VMEM((LANES, LANES), F32),
            pltpu.VMEM((2, chunks, frames, LANES), F32),
            pltpu.VMEM((windows, 2 * channels), F32),
        ],
    )
    return pl.pallas_call(
        functools.partial(enc1_kernel, chunks=chunks, cols=cols, copies=cols),
        grid_spec=grid_spec,
        out_shape=[
            jax.ShapeDtypeStruct((4, windows * quarter, bins), BF16),
            jax.ShapeDtypeStruct((2, windows * quarter, channels), F32),
            jax.ShapeDtypeStruct((cols, windows, 2 * channels), F32),
        ],
        compiler_params=pltpu.CompilerParams(vmem_limit_bytes=VMEM_LIMIT),
        name="normalize_enc1",
    )(permutation, spectra, coef, w_enc1)


def window_rows(perm_ref, table, step, windows, quarter, all_windows, cols, first, last):
    parts = []
    for w in range(windows):
        place = group_rank(perm_ref, step * windows + w, all_windows, cols)
        parts.append(jnp.broadcast_to(table[pl.ds(place, 1), first:last], (quarter, last - first)))
    return jnp.concatenate(parts, axis=0)


def middle_kernel(perm_ref, normed_ref, pre_ref, stat_ref, v_ref, b_ref, c_ref,
                  grad_c_ref, grad_b_ref, grad_v_ref, back_ref, moment_ref, sums_ref,
                  moment, sums, *, quarter, cols, total_windows):
    step = pl.program_id(0)
    channels = v_ref.shape[1]
    bins = normed_ref.shape[2]
    rows = normed_ref.shape[1]
    windows = rows // quarter
    all_windows = windows * pl.num_programs(0)
    ch = channels

    @pl.when(step == 0)
    def _():
        means = stat_ref[:, :, 0:ch]
        mean = jnp.mean(means, axis=0)
        diff = means - mean[None]
        variance = jnp.mean(stat_ref[:, :, ch:2 * ch] + diff * diff, axis=0)
        moment[:, 0:ch] = mean
        moment[:, ch:2 * ch] = lax.rsqrt(variance + EPS)
        moment_ref[...] = moment[...]
        grad_c_ref[...] = jnp.zeros_like(grad_c_ref)
        grad_b_ref[...] = jnp.zeros_like(grad_b_ref)
        grad_v_ref[...] = jnp.zeros_like(grad_v_ref)

    mean = window_rows(perm_ref, moment, step, windows, quarter, all_windows, cols, 0, ch)
    inverse = window_rows(perm_ref, moment, step, windows, quarter, all_windows, cols, ch, 2 * ch)
    hat_e = (pre_ref[0] - mean) * inverse
    hat_o = (pre_ref[1] - mean) * inverse
    a_e = (hat_e * sigmoid(hat_e)).astype(BF16)
    a_o = (hat_o * sigmoid(hat_o)).astype(BF16)
    v0, v1, v2, v3 = (v_ref[k * ch:(k + 1) * ch, :] for k in range(4))
    pre2 = shift_down(dot(a_o, v0), quarter) + dot(a_e, v1) + dot(a_o, v2) + shift_up(dot(a_e, v3), quarter)
    gate2 = sigmoid(pre2)
    h32 = (pre2 * gate2).astype(BF16).astype(F32)
    h = h32.astype(BF16)
    b0, b1, b2, b3 = (b_ref[:, k * ch:(k + 1) * ch] for k in range(4))
    d1_e = dot(h, b1) + shift_down(dot(h, b3), quarter)
    d1_o = dot(h, b2) + shift_up(dot(h, b0), quarter)
    gate_e = sigmoid(d1_e)
    gate_o = sigmoid(d1_o)
    de32 = (d1_e * gate_e)
    do32 = (d1_o * gate_o)
    de = de32.astype(BF16)
    do = do32.astype(BF16)
    de_up = shift_up(de32, quarter).astype(BF16)
    do_down = shift_down(do32, quarter).astype(BF16)
    c0, c1, c2, c3 = (c_ref[:, k * bins:(k + 1) * bins] for k in range(4))

    def delta(rebuilt, i):
        return ((rebuilt - normed_ref[i].astype(F32)) / total_windows).astype(BF16)

    g0 = delta(dot(de, c1) + dot(do_down, c3), 0)
    g1 = delta(dot(de, c2) + dot(do, c0), 1)
    g2 = delta(dot(do, c1) + dot(de, c3), 2)
    g3 = delta(dot(do, c2) + dot(de_up, c0), 3)
    halves = bins // ch

    def add_c(k, value):
        for j in range(halves):
            at = (k * halves + j) * ch
            grad_c_ref[at:at + ch, :] += value[:, j * ch:(j + 1) * ch]

    add_c(0, dot_tn(de_up, g3) + dot_tn(do, g1))
    add_c(1, dot_tn(de, g0) + dot_tn(do, g2))
    add_c(2, dot_tn(de, g1) + dot_tn(do, g3))
    add_c(3, dot_tn(de, g2) + dot_tn(do_down, g0))
    back_e = shift_down(dot_nt(g3, c0), quarter) + dot_nt(g0, c1) + dot_nt(g1, c2) + dot_nt(g2, c3)
    back_o = dot_nt(g1, c0) + dot_nt(g2, c1) + dot_nt(g3, c2) + shift_up(dot_nt(g0, c3), quarter)
    dd_e = (back_e * (gate_e * (1.0 + d1_e * (1.0 - gate_e)))).astype(BF16)
    dd_o = (back_o * (gate_o * (1.0 + d1_o * (1.0 - gate_o)))).astype(BF16)
    h_up = shift_up(h32, quarter).astype(BF16)
    h_down = shift_down(h32, quarter).astype(BF16)
    grad_b_ref[0:ch, :] += dot_tn(h_up, dd_o)
    grad_b_ref[ch:2 * ch, :] += dot_tn(h, dd_e)
    grad_b_ref[2 * ch:3 * ch, :] += dot_tn(h, dd_o)
    grad_b_ref[3 * ch:4 * ch, :] += dot_tn(h_down, dd_e)
    back2 = shift_down(dot_nt(dd_o, b0), quarter) + dot_nt(dd_e, b1) + dot_nt(dd_o, b2) + shift_up(dot_nt(dd_e, b3), quarter)
    d2_32 = (back2 * (gate2 * (1.0 + pre2 * (1.0 - gate2)))).astype(BF16).astype(F32)
    d2 = d2_32.astype(BF16)
    d2_up = shift_up(d2_32, quarter).astype(BF16)
    d2_down = shift_down(d2_32, quarter).astype(BF16)
    grad_v_ref[0:ch, :] += dot_tn(a_o, d2_up)
    grad_v_ref[ch:2 * ch, :] += dot_tn(a_e, d2)
    grad_v_ref[2 * ch:3 * ch, :] += dot_tn(a_o, d2)
    grad_v_ref[3 * ch:4 * ch, :] += dot_tn(a_e, d2_down)
    fold_e = dot_nt(d2, v1) + shift_down(dot_nt(d2, v3), quarter)
    fold_o = dot_nt(d2, v2) + shift_up(dot_nt(d2, v0), quarter)
    gate_he = sigmoid(hat_e)
    gate_ho = sigmoid(hat_o)
    fold_e = fold_e * (gate_he * (1.0 + hat_e * (1.0 - gate_he)))
    fold_o = fold_o * (gate_ho * (1.0 + hat_o * (1.0 - gate_ho)))
    back_ref[0] = fold_e
    back_ref[1] = fold_o
    cross_e = fold_e * hat_e
    cross_o = fold_o * hat_o
    for w in range(windows):
        low, high = w * quarter, (w + 1) * quarter
        first = jnp.sum(fold_e[low:high] + fold_o[low:high], axis=0, keepdims=True)
        second = jnp.sum(cross_e[low:high] + cross_o[low:high], axis=0, keepdims=True)
        place = group_rank(perm_ref, step * windows + w, all_windows, cols)
        sums[pl.ds(place, 1), 0:ch] = first
        sums[pl.ds(place, 1), ch:2 * ch] = second

    @pl.when(step == pl.num_programs(0) - 1)
    def _():
        for d in range(cols):
            sums_ref[d] = sums[...]


def middle_call(permutation, normed, pre, stat, w_enc2, w_dec1, w_dec2, quarter, cols, total_windows):
    bins = normed.shape[2]
    channels = w_enc2.shape[1]
    windows = normed.shape[1] // quarter
    rows = STEP_WINDOWS * quarter
    whole2 = lambda i, p: (0, 0)
    whole3 = lambda i, p: (0, 0, 0)
    grid_spec = pltpu.PrefetchScalarGridSpec(
        num_scalar_prefetch=1,
        grid=(windows // STEP_WINDOWS,),
        in_specs=[
            pl.BlockSpec((4, rows, bins), lambda i, p: (0, i, 0)),
            pl.BlockSpec((2, rows, channels), lambda i, p: (0, i, 0)),
            pl.BlockSpec(stat.shape, whole3),
            pl.BlockSpec(w_enc2.shape, whole2),
            pl.BlockSpec(w_dec1.shape, whole2),
            pl.BlockSpec(w_dec2.shape, whole2),
        ],
        out_specs=[
            pl.BlockSpec((4 * bins, channels), whole2),
            pl.BlockSpec((4 * channels, channels), whole2),
            pl.BlockSpec((4 * channels, channels), whole2),
            pl.BlockSpec((2, rows, channels), lambda i, p: (0, i, 0)),
            pl.BlockSpec((windows, 2 * channels), whole2),
            pl.BlockSpec(stat.shape, whole3),
        ],
        scratch_shapes=[
            pltpu.VMEM((windows, 2 * channels), F32),
            pltpu.VMEM((windows, 2 * channels), F32),
        ],
    )
    return pl.pallas_call(
        functools.partial(middle_kernel, quarter=quarter, cols=cols, total_windows=float(total_windows)),
        grid_spec=grid_spec,
        out_shape=[
            jax.ShapeDtypeStruct((4 * bins, channels), F32),
            jax.ShapeDtypeStruct((4 * channels, channels), F32),
            jax.ShapeDtypeStruct((4 * channels, channels), F32),
            jax.ShapeDtypeStruct(pre.shape, F32),
            jax.ShapeDtypeStruct((windows, 2 * channels), F32),
            jax.ShapeDtypeStruct(stat.shape, F32),
        ],
        compiler_params=pltpu.CompilerParams(vmem_limit_bytes=VMEM_LIMIT),
        name="middle",
    )(permutation, normed, pre, stat, w_enc2, w_dec1, w_dec2)


def grad_kernel(perm_ref, normed_ref, pre_ref, back_ref, moment_ref, sums_ref, grad_ref, scale, *, quarter, cols):
    step = pl.program_id(0)
    bins = normed_ref.shape[2]
    rows = normed_ref.shape[1]
    ch = pre_ref.shape[2]
    windows = rows // quarter
    all_windows = windows * pl.num_programs(0)

    @pl.when(step == 0)
    def _():
        scale[...] = jnp.sum(sums_ref[...], axis=0) / (2.0 * quarter * cols)
        grad_ref[...] = jnp.zeros_like(grad_ref)

    pick = functools.partial(window_rows, perm_ref, step=step, windows=windows, quarter=quarter, all_windows=all_windows, cols=cols)
    mean = pick(table=moment_ref, first=0, last=ch)
    inverse = pick(table=moment_ref, first=ch, last=2 * ch)
    first = pick(table=scale, first=0, last=ch)
    second = pick(table=scale, first=ch, last=2 * ch)
    hat_e = (pre_ref[0] - mean) * inverse
    hat_o = (pre_ref[1] - mean) * inverse
    de32 = (back_ref[0] - first - hat_e * second) * inverse
    do32 = (back_ref[1] - first - hat_o * second) * inverse
    de = de32.astype(BF16)
    do = do32.astype(BF16)
    de_up = shift_up(de32, quarter).astype(BF16)
    do_down = shift_down(do32, quarter).astype(BF16)
    f0, f1, f2, f3 = (normed_ref[i] for i in range(4))
    grad_ref[0:bins, :] += dot_tn(f3, de_up) + dot_tn(f1, do)
    grad_ref[bins:2 * bins, :] += dot_tn(f0, de) + dot_tn(f2, do)
    grad_ref[2 * bins:3 * bins, :] += dot_tn(f1, de) + dot_tn(f3, do)
    grad_ref[3 * bins:4 * bins, :] += dot_tn(f2, de) + dot_tn(f0, do_down)


def grad_call(permutation, normed, pre, back, moment, sums, quarter, cols):
    bins = normed.shape[2]
    channels = pre.shape[2]
    windows = normed.shape[1] // quarter
    rows = STEP_WINDOWS * quarter
    grid_spec = pltpu.PrefetchScalarGridSpec(
        num_scalar_prefetch=1,
        grid=(windows // STEP_WINDOWS,),
        in_specs=[
            pl.BlockSpec((4, rows, bins), lambda i, p: (0, i, 0)),
            pl.BlockSpec((2, rows, channels), lambda i, p: (0, i, 0)),
            pl.BlockSpec((2, rows, channels), lambda i, p: (0, i, 0)),
            pl.BlockSpec(moment.shape, lambda i, p: (0, 0)),
            pl.BlockSpec(sums.shape, lambda i, p: (0, 0, 0)),
        ],
        out_specs=pl.BlockSpec((4 * bins, channels), lambda i, p: (0, 0)),
        scratch_shapes=[pltpu.VMEM((windows, 2 * channels), F32)],
    )
    return pl.pallas_call(
        functools.partial(grad_kernel, quarter=quarter, cols=cols),
        grid_spec=grid_spec,
        out_shape=jax.ShapeDtypeStruct((4 * bins, channels), F32),
        compiler_params=pltpu.CompilerParams(vmem_limit_bytes=VMEM_LIMIT),
        name="grad_enc1",
    )(permutation, normed, pre, back, moment, sums)


def exchange(values, axes):
    return lax.all_to_all(values, axes, split_axis=0, concat_axis=0, tiled=True)


def local(spectra, sensor_ids, permutation, w_enc1, w_enc2, w_dec1, w_dec2):
    windows, frames, bins = spectra.shape
    channels = w_enc1.shape[1]
    cols = lax.axis_size("col")
    total_windows = windows * lax.axis_size("row") * cols
    sensors = total_windows // WIN_SENSOR
    chunks = bins // LANES
    quarter = frames // 4
    both = ("row", "col")

    sums = exchange(sums_call(spectra, sensor_ids), both)
    coef = exchange(stats_call(sums, windows, chunks, sensors, WIN_SENSOR * frames), both)
    normed, pre, stat = enc1_call(permutation, spectra, coef, w_enc1, cols)
    stat = exchange(stat.reshape(cols * windows, 2 * channels), "col").reshape(cols, windows, 2 * channels)
    grad_c, grad_b, grad_v, back, moment, moments = middle_call(
        permutation, normed, pre, stat, w_enc2, w_dec1, w_dec2, quarter, cols, total_windows)
    moments = exchange(moments.reshape(cols * windows, 2 * channels), "col").reshape(cols, windows, 2 * channels)
    grad_w = grad_call(permutation, normed, pre, back, moment, moments, quarter, cols)
    grad_w, grad_v, grad_b, grad_c = lax.psum((grad_w, grad_v, grad_b, grad_c), both)
    grad_b = grad_b.reshape(4, channels, channels).transpose(1, 0, 2).reshape(channels, 4 * channels)
    grad_c = grad_c.reshape(4 * bins // channels, channels, channels).transpose(1, 0, 2).reshape(channels, 4 * bins)
    return (grad_w, grad_v, grad_b, grad_c)


def solution(mesh):
    return jax.shard_map(
        local,
        mesh=mesh,
        in_specs=(
            P(("row", "col"), None, None),
            P(("row", "col"), None),
            P(("row", "col")),
            P(),
            P(),
            P(),
            P(),
        ),
        out_specs=(P(), P(), P(), P()),
        check_vma=False,
    )
```

```python
import functools

import jax
import jax.numpy as jnp
from jax import lax
from jax.experimental import pallas as pl
from jax.experimental.pallas import tpu as pltpu
from jax.sharding import Mesh, PartitionSpec as P

WIN_SENSOR = 8
EPS = 1e-05
F32 = jnp.float32
BF16 = jnp.bfloat16
LANES = 128
STEP_WINDOWS = 4
VMEM_LIMIT = 56 * 1024 * 1024


def dot(left, right):
    return jnp.dot(left, right, preferred_element_type=F32)


def dot_nt(left, right):
    return lax.dot_general(left, right, (((1,), (1,)), ((), ())), preferred_element_type=F32)


def dot_tn(left, right):
    return lax.dot_general(left, right, (((0,), (0,)), ((), ())), preferred_element_type=F32)


def split3(values):
    first = values.astype(BF16)
    rest = values - first.astype(F32)
    second = rest.astype(BF16)
    third = (rest - second.astype(F32)).astype(BF16)
    return first, second, third


def sigmoid(values):
    return 1.0 / (1.0 + jnp.exp(-values))


def shift_down(values, period):
    rows = lax.broadcasted_iota(jnp.int32, values.shape, 0) % period
    return jnp.where(rows == 0, 0.0, pltpu.roll(values, 1, 0))


def shift_up(values, period):
    total = values.shape[0]
    rows = lax.broadcasted_iota(jnp.int32, values.shape, 0) % period
    return jnp.where(rows == period - 1, 0.0, pltpu.roll(values, total - 1, 0))


def group_rank(perm_ref, window, window_dev, col_count):
    trainer = perm_ref[window] // window_dev
    per_row = 2
    return (trainer // col_count) * per_row + trainer % per_row


def sums_kernel(spec_ref, ids_ref, out_ref, acc, *, chunks):
    step = pl.program_id(0)
    windows, frames, bins = spec_ref.shape
    rows = 16

    for w in range(windows):
        def body(i, carry):
            total, square = carry
            start = pl.multiple_of(i * rows, rows)
            value = jnp.log(1.0 + spec_ref[w, pl.ds(start, rows), :].astype(F32))
            value_sq = value * value
            return (total + value[0:8] + value[8:16], square + value_sq[0:8] + value_sq[8:16])

        zero = jnp.zeros((8, bins), F32)
        total, square = lax.fori_loop(0, frames // rows, body, (zero, zero), unroll=4)
        total = jnp.sum(total, axis=0, keepdims=True)
        square = jnp.sum(square, axis=0, keepdims=True)
        pieces = [total[:, k * LANES:(k + 1) * LANES] for k in range(chunks)]
        pieces += [square[:, k * LANES:(k + 1) * LANES] for k in range(chunks)]
        start = pl.multiple_of((step * windows + w) * 2 * chunks, 2 * chunks)
        acc[pl.ds(start, 2 * chunks), :] = jnp.concatenate(pieces, axis=0)

    @pl.when(step == pl.num_programs(0) - 1)
    def _():
        count = ids_ref.shape[0]
        acc[LANES:2 * LANES, :] = jnp.zeros((LANES, LANES), F32)
        acc[LANES:LANES + count, :] = jnp.broadcast_to(ids_ref[...].astype(F32), (count, LANES))
        out_ref[:, 0:LANES] = acc[0:LANES, :].T
        out_ref[:, LANES:2 * LANES] = acc[LANES:2 * LANES, :].T


def sums_call(spectra, sensor_ids):
    windows, frames, bins = spectra.shape
    chunks = bins // LANES
    return pl.pallas_call(
        functools.partial(sums_kernel, chunks=chunks),
        grid=(windows // STEP_WINDOWS,),
        in_specs=[
            pl.BlockSpec((STEP_WINDOWS, frames, bins), lambda i: (i, 0, 0)),
            pl.BlockSpec(sensor_ids.shape, lambda i: (0, 0)),
        ],
        out_specs=pl.BlockSpec((LANES, 2 * LANES), lambda i: (0, 0)),
        out_shape=jax.ShapeDtypeStruct((LANES, 2 * LANES), F32),
        scratch_shapes=[pltpu.VMEM((2 * LANES, LANES), F32)],
        compiler_params=pltpu.CompilerParams(vmem_limit_bytes=VMEM_LIMIT),
        name="window_sums",
    )(spectra, sensor_ids)


def stats_kernel(in_ref, out_ref, *, windows, chunks, sensors, per_sensor):
    width = 2 * chunks
    data = in_ref[:, 0:LANES].T
    labels = in_ref[:, LANES:2 * LANES].T
    sensor_rows = lax.broadcasted_iota(jnp.int32, (sensors, LANES), 0).astype(F32)
    tables = [(sensor_rows == labels[w:w + 1, :]).astype(F32).astype(BF16) for w in range(windows)]
    table = jnp.concatenate(tables, axis=1)
    values = jnp.concatenate([data[w * width:(w + 1) * width, :] for w in range(windows)], axis=1)
    parts = dot_nt(jnp.concatenate(split3(values), axis=0), table)
    sums = parts[0:width] + parts[width:2 * width] + parts[2 * width:3 * width]
    center = sums[0:chunks] / per_sensor
    factor = lax.rsqrt(sums[chunks:width] / per_sensor - center * center + EPS)
    both = jnp.concatenate([center, factor], axis=0)
    back = dot(jnp.concatenate(split3(both), axis=0), table)
    back = back[0:width] + back[width:2 * width] + back[2 * width:3 * width]
    rows = jnp.concatenate([back[:, w * LANES:(w + 1) * LANES] for w in range(windows)], axis=0)
    out_ref[...] = rows.T


def stats_call(received, windows, chunks, sensors, per_sensor):
    return pl.pallas_call(
        functools.partial(stats_kernel, windows=windows, chunks=chunks, sensors=sensors, per_sensor=float(per_sensor)),
        out_shape=jax.ShapeDtypeStruct((LANES, LANES), F32),
        compiler_params=pltpu.CompilerParams(vmem_limit_bytes=VMEM_LIMIT),
        name="sensor_stats",
    )(received)


def enc1_kernel(perm_ref, spec_ref, coef_ref, w_ref, normed_ref, pre_ref, stat_ref, coef, lane, stat, *, chunks, cols, copies):
    step = pl.program_id(0)
    windows, frames, bins = spec_ref.shape
    quarter = frames // 4
    channels = w_ref.shape[1]
    all_windows = windows * pl.num_programs(0)
    width = 2 * chunks

    @pl.when(step == 0)
    def _():
        coef[...] = coef_ref[...].T

    rows = 32
    for w in range(windows):
        start = pl.multiple_of((step * windows + w) * width, width)
        both = coef[pl.ds(start, width), :]

        def body(i, carry):
            at = pl.multiple_of(i * rows, rows)
            value = jnp.log(1.0 + spec_ref[w, pl.ds(at, rows), :].astype(F32))
            for k in range(chunks):
                part = value[:, k * LANES:(k + 1) * LANES]
                lane[w % 2, k, pl.ds(at, rows), :] = (part - both[k:k + 1, :]) * both[chunks + k:chunks + k + 1, :]
            return carry

        lax.fori_loop(0, frames // rows, body, 0, unroll=2)
        for i in range(4):
            for k in range(chunks):
                picked = lane[w % 2, k, pl.ds(i, quarter, stride=4), :]
                normed_ref[i, w * quarter:(w + 1) * quarter, k * LANES:(k + 1) * LANES] = picked.astype(BF16)

    w0, w1, w2, w3 = (w_ref[k * bins:(k + 1) * bins, :] for k in range(4))
    f0, f1, f2, f3 = (normed_ref[i] for i in range(4))
    even = shift_down(dot(f3, w0), quarter) + dot(f0, w1) + dot(f1, w2) + dot(f2, w3)
    odd = dot(f1, w0) + dot(f2, w1) + dot(f3, w2) + shift_up(dot(f0, w3), quarter)
    pre_ref[0] = even
    pre_ref[1] = odd
    for w in range(windows):
        part_e = even[w * quarter:(w + 1) * quarter]
        part_o = odd[w * quarter:(w + 1) * quarter]
        mean = (jnp.sum(part_e, axis=0, keepdims=True) + jnp.sum(part_o, axis=0, keepdims=True)) / (2 * quarter)
        diff_e = part_e - mean
        diff_o = part_o - mean
        spread = (jnp.sum(diff_e * diff_e, axis=0, keepdims=True) + jnp.sum(diff_o * diff_o, axis=0, keepdims=True)) / (2 * quarter)
        place = group_rank(perm_ref, step * windows + w, all_windows, cols)
        stat[pl.ds(place, 1), 0:channels] = mean
        stat[pl.ds(place, 1), channels:2 * channels] = spread

    @pl.when(step == pl.num_programs(0) - 1)
    def _():
        for d in range(copies):
            stat_ref[d] = stat[...]


def enc1_call(permutation, spectra, coef, w_enc1, cols):
    windows, frames, bins = spectra.shape
    chunks = bins // LANES
    quarter = frames // 4
    channels = w_enc1.shape[1]
    rows = STEP_WINDOWS * quarter
    grid_spec = pltpu.PrefetchScalarGridSpec(
        num_scalar_prefetch=1,
        grid=(windows // STEP_WINDOWS,),
        in_specs=[
            pl.BlockSpec((STEP_WINDOWS, frames, bins), lambda i, p: (i, 0, 0)),
            pl.BlockSpec((LANES, LANES), lambda i, p: (0, 0)),
            pl.BlockSpec(w_enc1.shape, lambda i, p: (0, 0)),
        ],
        out_specs=[
            pl.BlockSpec((4, rows, bins), lambda i, p: (0, i, 0)),
            pl.BlockSpec((2, rows, channels), lambda i, p: (0, i, 0)),
            pl.BlockSpec((cols, windows, 2 * channels), lambda i, p: (0, 0, 0)),
        ],
        scratch_shapes=[
            pltpu.VMEM((LANES, LANES), F32),
            pltpu.VMEM((2, chunks, frames, LANES), F32),
            pltpu.VMEM((windows, 2 * channels), F32),
        ],
    )
    return pl.pallas_call(
        functools.partial(enc1_kernel, chunks=chunks, cols=cols, copies=cols),
        grid_spec=grid_spec,
        out_shape=[
            jax.ShapeDtypeStruct((4, windows * quarter, bins), BF16),
            jax.ShapeDtypeStruct((2, windows * quarter, channels), F32),
            jax.ShapeDtypeStruct((cols, windows, 2 * channels), F32),
        ],
        compiler_params=pltpu.CompilerParams(vmem_limit_bytes=VMEM_LIMIT),
        name="normalize_enc1",
    )(permutation, spectra, coef, w_enc1)


def window_rows(perm_ref, table, step, windows, quarter, all_windows, cols, first, last):
    parts = []
    for w in range(windows):
        place = group_rank(perm_ref, step * windows + w, all_windows, cols)
        parts.append(jnp.broadcast_to(table[pl.ds(place, 1), first:last], (quarter, last - first)))
    return jnp.concatenate(parts, axis=0)


def write_halves(core_ref, grads, own_ref, send_ref):
    half = own_ref.shape[0]
    own_ref[...] = grads[pl.ds(pl.multiple_of(core_ref[0] * half, half), half), :]
    send_ref[...] = grads[pl.ds(pl.multiple_of((1 - core_ref[0]) * half, half), half), :]


def middle_kernel(perm_ref, core_ref, normed_ref, pre_ref, stat_ref, v_ref, b_ref, c_ref,
                  own_ref, send_ref, back_ref, moment_ref, sums_ref,
                  grads, moment, sums, *, quarter, cols, total_windows):
    step = pl.program_id(0)
    channels = v_ref.shape[1]
    bins = normed_ref.shape[2]
    rows = normed_ref.shape[1]
    windows = rows // quarter
    all_windows = windows * pl.num_programs(0)
    ch = channels

    @pl.when(step == 0)
    def _():
        means = stat_ref[:, :, 0:ch]
        mean = jnp.mean(means, axis=0)
        diff = means - mean[None]
        variance = jnp.mean(stat_ref[:, :, ch:2 * ch] + diff * diff, axis=0)
        moment[:, 0:ch] = mean
        moment[:, ch:2 * ch] = lax.rsqrt(variance + EPS)
        moment_ref[...] = moment[...]
        grads[...] = jnp.zeros_like(grads)

    mean = window_rows(perm_ref, moment, step, windows, quarter, all_windows, cols, 0, ch)
    inverse = window_rows(perm_ref, moment, step, windows, quarter, all_windows, cols, ch, 2 * ch)
    hat_e = (pre_ref[0] - mean) * inverse
    hat_o = (pre_ref[1] - mean) * inverse
    a_e = (hat_e * sigmoid(hat_e)).astype(BF16)
    a_o = (hat_o * sigmoid(hat_o)).astype(BF16)
    v0, v1, v2, v3 = (v_ref[k * ch:(k + 1) * ch, :] for k in range(4))
    pre2 = shift_down(dot(a_o, v0), quarter) + dot(a_e, v1) + dot(a_o, v2) + shift_up(dot(a_e, v3), quarter)
    gate2 = sigmoid(pre2)
    h32 = (pre2 * gate2).astype(BF16).astype(F32)
    h = h32.astype(BF16)
    b0, b1, b2, b3 = (b_ref[:, k * ch:(k + 1) * ch] for k in range(4))
    d1_e = dot(h, b1) + shift_down(dot(h, b3), quarter)
    d1_o = dot(h, b2) + shift_up(dot(h, b0), quarter)
    gate_e = sigmoid(d1_e)
    gate_o = sigmoid(d1_o)
    de32 = (d1_e * gate_e)
    do32 = (d1_o * gate_o)
    de = de32.astype(BF16)
    do = do32.astype(BF16)
    de_up = shift_up(de32, quarter).astype(BF16)
    do_down = shift_down(do32, quarter).astype(BF16)
    c0, c1, c2, c3 = (c_ref[:, k * bins:(k + 1) * bins] for k in range(4))

    def delta(rebuilt, i):
        return ((rebuilt - normed_ref[i].astype(F32)) / total_windows).astype(BF16)

    g0 = delta(dot(de, c1) + dot(do_down, c3), 0)
    g1 = delta(dot(de, c2) + dot(do, c0), 1)
    g2 = delta(dot(do, c1) + dot(de, c3), 2)
    g3 = delta(dot(do, c2) + dot(de_up, c0), 3)
    halves = bins // ch
    base_b = 4 * bins
    base_v = base_b + 4 * ch

    def add_c(k, value):
        for j in range(halves):
            at = (k * halves + j) * ch
            grads[at:at + ch, :] += value[:, j * ch:(j + 1) * ch]

    add_c(0, dot_tn(de_up, g3) + dot_tn(do, g1))
    add_c(1, dot_tn(de, g0) + dot_tn(do, g2))
    add_c(2, dot_tn(de, g1) + dot_tn(do, g3))
    add_c(3, dot_tn(de, g2) + dot_tn(do_down, g0))
    back_e = shift_down(dot_nt(g3, c0), quarter) + dot_nt(g0, c1) + dot_nt(g1, c2) + dot_nt(g2, c3)
    back_o = dot_nt(g1, c0) + dot_nt(g2, c1) + dot_nt(g3, c2) + shift_up(dot_nt(g0, c3), quarter)
    dd_e = (back_e * (gate_e * (1.0 + d1_e * (1.0 - gate_e)))).astype(BF16)
    dd_o = (back_o * (gate_o * (1.0 + d1_o * (1.0 - gate_o)))).astype(BF16)
    h_up = shift_up(h32, quarter).astype(BF16)
    h_down = shift_down(h32, quarter).astype(BF16)
    grads[base_b:base_b + ch, :] += dot_tn(h_up, dd_o)
    grads[base_b + ch:base_b + 2 * ch, :] += dot_tn(h, dd_e)
    grads[base_b + 2 * ch:base_b + 3 * ch, :] += dot_tn(h, dd_o)
    grads[base_b + 3 * ch:base_b + 4 * ch, :] += dot_tn(h_down, dd_e)
    back2 = shift_down(dot_nt(dd_o, b0), quarter) + dot_nt(dd_e, b1) + dot_nt(dd_o, b2) + shift_up(dot_nt(dd_e, b3), quarter)
    d2_32 = (back2 * (gate2 * (1.0 + pre2 * (1.0 - gate2)))).astype(BF16).astype(F32)
    d2 = d2_32.astype(BF16)
    d2_up = shift_up(d2_32, quarter).astype(BF16)
    d2_down = shift_down(d2_32, quarter).astype(BF16)
    grads[base_v:base_v + ch, :] += dot_tn(a_o, d2_up)
    grads[base_v + ch:base_v + 2 * ch, :] += dot_tn(a_e, d2)
    grads[base_v + 2 * ch:base_v + 3 * ch, :] += dot_tn(a_o, d2)
    grads[base_v + 3 * ch:base_v + 4 * ch, :] += dot_tn(a_e, d2_down)
    fold_e = dot_nt(d2, v1) + shift_down(dot_nt(d2, v3), quarter)
    fold_o = dot_nt(d2, v2) + shift_up(dot_nt(d2, v0), quarter)
    gate_he = sigmoid(hat_e)
    gate_ho = sigmoid(hat_o)
    fold_e = fold_e * (gate_he * (1.0 + hat_e * (1.0 - gate_he)))
    fold_o = fold_o * (gate_ho * (1.0 + hat_o * (1.0 - gate_ho)))
    back_ref[0] = fold_e
    back_ref[1] = fold_o
    cross_e = fold_e * hat_e
    cross_o = fold_o * hat_o
    for w in range(windows):
        low, high = w * quarter, (w + 1) * quarter
        first = jnp.sum(fold_e[low:high] + fold_o[low:high], axis=0, keepdims=True)
        second = jnp.sum(cross_e[low:high] + cross_o[low:high], axis=0, keepdims=True)
        place = group_rank(perm_ref, step * windows + w, all_windows, cols)
        sums[pl.ds(place, 1), 0:ch] = first
        sums[pl.ds(place, 1), ch:2 * ch] = second

    @pl.when(step == pl.num_programs(0) - 1)
    def _():
        for d in range(cols):
            sums_ref[d] = sums[...]
        write_halves(core_ref, grads, own_ref, send_ref)


def middle_call(permutation, core, normed, pre, stat, w_enc2, w_dec1, w_dec2, quarter, cols, total_windows):
    bins = normed.shape[2]
    channels = w_enc2.shape[1]
    windows = normed.shape[1] // quarter
    rows = STEP_WINDOWS * quarter
    total = 4 * bins + 8 * channels
    whole2 = lambda i, p, c: (0, 0)
    whole3 = lambda i, p, c: (0, 0, 0)
    grid_spec = pltpu.PrefetchScalarGridSpec(
        num_scalar_prefetch=2,
        grid=(windows // STEP_WINDOWS,),
        in_specs=[
            pl.BlockSpec((4, rows, bins), lambda i, p, c: (0, i, 0)),
            pl.BlockSpec((2, rows, channels), lambda i, p, c: (0, i, 0)),
            pl.BlockSpec(stat.shape, whole3),
            pl.BlockSpec(w_enc2.shape, whole2),
            pl.BlockSpec(w_dec1.shape, whole2),
            pl.BlockSpec(w_dec2.shape, whole2),
        ],
        out_specs=[
            pl.BlockSpec((total // 2, channels), whole2),
            pl.BlockSpec((total // 2, channels), whole2),
            pl.BlockSpec((2, rows, channels), lambda i, p, c: (0, i, 0)),
            pl.BlockSpec((windows, 2 * channels), whole2),
            pl.BlockSpec(stat.shape, whole3),
        ],
        scratch_shapes=[
            pltpu.VMEM((total, channels), F32),
            pltpu.VMEM((windows, 2 * channels), F32),
            pltpu.VMEM((windows, 2 * channels), F32),
        ],
    )
    return pl.pallas_call(
        functools.partial(middle_kernel, quarter=quarter, cols=cols, total_windows=float(total_windows)),
        grid_spec=grid_spec,
        out_shape=[
            jax.ShapeDtypeStruct((total // 2, channels), F32),
            jax.ShapeDtypeStruct((total // 2, channels), F32),
            jax.ShapeDtypeStruct(pre.shape, F32),
            jax.ShapeDtypeStruct((windows, 2 * channels), F32),
            jax.ShapeDtypeStruct(stat.shape, F32),
        ],
        compiler_params=pltpu.CompilerParams(vmem_limit_bytes=VMEM_LIMIT),
        name="middle",
    )(permutation, core, normed, pre, stat, w_enc2, w_dec1, w_dec2)


def grad_kernel(perm_ref, core_ref, normed_ref, pre_ref, back_ref, moment_ref, sums_ref, own_ref, send_ref, grads, scale, *, quarter, cols):
    step = pl.program_id(0)
    bins = normed_ref.shape[2]
    rows = normed_ref.shape[1]
    ch = pre_ref.shape[2]
    windows = rows // quarter
    all_windows = windows * pl.num_programs(0)

    @pl.when(step == 0)
    def _():
        scale[...] = jnp.sum(sums_ref[...], axis=0) / (2.0 * quarter * cols)
        grads[...] = jnp.zeros_like(grads)

    pick = functools.partial(window_rows, perm_ref, step=step, windows=windows, quarter=quarter, all_windows=all_windows, cols=cols)
    mean = pick(table=moment_ref, first=0, last=ch)
    inverse = pick(table=moment_ref, first=ch, last=2 * ch)
    first = pick(table=scale, first=0, last=ch)
    second = pick(table=scale, first=ch, last=2 * ch)
    hat_e = (pre_ref[0] - mean) * inverse
    hat_o = (pre_ref[1] - mean) * inverse
    de32 = (back_ref[0] - first - hat_e * second) * inverse
    do32 = (back_ref[1] - first - hat_o * second) * inverse
    de = de32.astype(BF16)
    do = do32.astype(BF16)
    de_up = shift_up(de32, quarter).astype(BF16)
    do_down = shift_down(do32, quarter).astype(BF16)
    f0, f1, f2, f3 = (normed_ref[i] for i in range(4))
    grads[0:bins, :] += dot_tn(f3, de_up) + dot_tn(f1, do)
    grads[bins:2 * bins, :] += dot_tn(f0, de) + dot_tn(f2, do)
    grads[2 * bins:3 * bins, :] += dot_tn(f1, de) + dot_tn(f3, do)
    grads[3 * bins:4 * bins, :] += dot_tn(f2, de) + dot_tn(f0, do_down)

    @pl.when(step == pl.num_programs(0) - 1)
    def _():
        write_halves(core_ref, grads, own_ref, send_ref)


def grad_call(permutation, core, normed, pre, back, moment, sums, quarter, cols):
    bins = normed.shape[2]
    channels = pre.shape[2]
    windows = normed.shape[1] // quarter
    rows = STEP_WINDOWS * quarter
    grid_spec = pltpu.PrefetchScalarGridSpec(
        num_scalar_prefetch=2,
        grid=(windows // STEP_WINDOWS,),
        in_specs=[
            pl.BlockSpec((4, rows, bins), lambda i, p, c: (0, i, 0)),
            pl.BlockSpec((2, rows, channels), lambda i, p, c: (0, i, 0)),
            pl.BlockSpec((2, rows, channels), lambda i, p, c: (0, i, 0)),
            pl.BlockSpec(moment.shape, lambda i, p, c: (0, 0)),
            pl.BlockSpec(sums.shape, lambda i, p, c: (0, 0, 0)),
        ],
        out_specs=[pl.BlockSpec((2 * bins, channels), lambda i, p, c: (0, 0))] * 2,
        scratch_shapes=[pltpu.VMEM((4 * bins, channels), F32), pltpu.VMEM((windows, 2 * channels), F32)],
    )
    return pl.pallas_call(
        functools.partial(grad_kernel, quarter=quarter, cols=cols),
        grid_spec=grid_spec,
        out_shape=[jax.ShapeDtypeStruct((2 * bins, channels), F32)] * 2,
        compiler_params=pltpu.CompilerParams(vmem_limit_bytes=VMEM_LIMIT),
        name="grad_enc1",
    )(permutation, core, normed, pre, back, moment, sums)


def swap_cores(values):
    return lax.ppermute(values, "core", [(0, 1), (1, 0)])


def exchange(values, axes):
    return lax.all_to_all(values, axes, split_axis=0, concat_axis=0, tiled=True)


def scatter_sum(own, send, axes, chips):
    total = (own + swap_cores(send)).astype(BF16)
    pieces = exchange(total, axes)
    return jnp.sum(pieces.reshape(chips, -1, own.shape[1]).astype(F32), axis=0)


def gather_rows(piece, axes, chips):
    rows, width = piece.shape
    copies = jnp.broadcast_to(piece[None], (chips, rows, width)).reshape(chips * rows, width)
    return exchange(copies, axes)


def local(spectra, sensor_ids, permutation, w_enc1, w_enc2, w_dec1, w_dec2):
    windows, frames, bins = spectra.shape
    channels = w_enc1.shape[1]
    col_axes = ("pair", "core")
    chip_axes = ("row", "pair")
    every = ("row", "pair", "core")
    cols = lax.axis_size("pair") * lax.axis_size("core")
    chips = lax.axis_size("row") * lax.axis_size("pair")
    total_windows = windows * lax.axis_size("row") * cols
    sensors = total_windows // WIN_SENSOR
    chunks = bins // LANES
    quarter = frames // 4
    core_index = lax.axis_index("core")
    core = core_index.astype(jnp.int32).reshape(1)

    sums = exchange(sums_call(spectra, sensor_ids), every)
    coef = exchange(stats_call(sums, windows, chunks, sensors, WIN_SENSOR * frames), every)
    normed, pre, stat = enc1_call(permutation, spectra, coef, w_enc1, cols)
    stat = exchange(stat.reshape(cols * windows, 2 * channels), col_axes).reshape(cols, windows, 2 * channels)
    own, send, back, moment, moments = middle_call(
        permutation, core, normed, pre, stat, w_enc2, w_dec1, w_dec2, quarter, cols, total_windows)
    moments = exchange(moments.reshape(cols * windows, 2 * channels), col_axes).reshape(cols, windows, 2 * channels)
    early = scatter_sum(own, send, chip_axes, chips)
    own, send = grad_call(permutation, core, normed, pre, back, moment, moments, quarter, cols)
    late = scatter_sum(own, send, chip_axes, chips)

    def collect(piece):
        mine = gather_rows(piece, chip_axes, chips)
        other = swap_cores(mine)
        first = jnp.where(core_index == 0, mine, other)
        second = jnp.where(core_index == 0, other, mine)
        return jnp.concatenate([first, second], axis=0)

    early = collect(early)
    grad_w = collect(late)
    grad_c = early[0:4 * bins]
    grad_b = early[4 * bins:4 * bins + 4 * channels]
    grad_v = early[4 * bins + 4 * channels:]
    grad_b = grad_b.reshape(4, channels, channels).transpose(1, 0, 2).reshape(channels, 4 * channels)
    grad_c = grad_c.reshape(4 * bins // channels, channels, channels).transpose(1, 0, 2).reshape(channels, 4 * bins)
    return (grad_w, grad_v, grad_b, grad_c)


def solution(mesh):
    rows, cols = mesh.devices.shape
    inner = Mesh(mesh.devices.reshape(rows, cols // 2, 2), ("row", "pair", "core"))
    spread = ("row", "pair", "core")
    return jax.shard_map(
        local,
        mesh=inner,
        in_specs=(P(spread, None, None), P(spread, None), P(spread), P(), P(), P(), P()),
        out_specs=(P(), P(), P(), P()),
        check_vma=False,
    )
```

```python
import functools

import jax
import jax.numpy as jnp
from jax import lax
from jax.experimental import pallas as pl
from jax.experimental.pallas import tpu as pltpu
from jax.sharding import Mesh, PartitionSpec as P

WIN_SENSOR = 8
EPS = 1e-05
F32 = jnp.float32
BF16 = jnp.bfloat16
LANES = 128
STEP_WINDOWS = 4
SCALE_ROWS = 8
VMEM_LIMIT = 56 * 1024 * 1024


def dot(left, right):
    return jnp.dot(left, right, preferred_element_type=F32)


def dot_nt(left, right):
    return lax.dot_general(left, right, (((1,), (1,)), ((), ())), preferred_element_type=F32)


def dot_tn(left, right):
    return lax.dot_general(left, right, (((0,), (0,)), ((), ())), preferred_element_type=F32)


def split3(values):
    first = values.astype(BF16)
    rest = values - first.astype(F32)
    second = rest.astype(BF16)
    third = (rest - second.astype(F32)).astype(BF16)
    return first, second, third


def sigmoid(values):
    return 1.0 / (1.0 + jnp.exp(-values))


def shift_down(values, period):
    rows = lax.broadcasted_iota(jnp.int32, values.shape, 0) % period
    return jnp.where(rows == 0, 0.0, pltpu.roll(values, 1, 0))


def shift_up(values, period):
    total = values.shape[0]
    rows = lax.broadcasted_iota(jnp.int32, values.shape, 0) % period
    return jnp.where(rows == period - 1, 0.0, pltpu.roll(values, total - 1, 0))


def group_rank(perm_ref, window, window_dev, col_count):
    trainer = perm_ref[window] // window_dev
    per_row = 2
    return (trainer // col_count) * per_row + trainer % per_row


def sums_kernel(ids_ref, spec_ref, out_ref, acc, *, chunks, count):
    step = pl.program_id(0)
    windows, frames, bins = spec_ref.shape
    rows = 16

    for w in range(windows):
        def body(i, carry):
            total, square = carry
            start = pl.multiple_of(i * rows, rows)
            value = jnp.log(1.0 + spec_ref[w, pl.ds(start, rows), :].astype(F32))
            value_sq = value * value
            return (total + value[0:8] + value[8:16], square + value_sq[0:8] + value_sq[8:16])

        zero = jnp.zeros((8, bins), F32)
        total, square = lax.fori_loop(0, frames // rows, body, (zero, zero), unroll=4)
        total = jnp.sum(total, axis=0, keepdims=True)
        square = jnp.sum(square, axis=0, keepdims=True)
        pieces = [total[:, k * LANES:(k + 1) * LANES] for k in range(chunks)]
        pieces += [square[:, k * LANES:(k + 1) * LANES] for k in range(chunks)]
        start = pl.multiple_of((step * windows + w) * 2 * chunks, 2 * chunks)
        acc[pl.ds(start, 2 * chunks), :] = jnp.concatenate(pieces, axis=0)

    @pl.when(step == pl.num_programs(0) - 1)
    def _():
        acc[LANES:2 * LANES, :] = jnp.zeros((LANES, LANES), F32)
        for w in range(count):
            acc[LANES + w:LANES + w + 1, :] = jnp.full((1, LANES), ids_ref[w], jnp.int32).astype(F32)
        out_ref[pl.ds(0, LANES, stride=2), :] = acc[0:LANES, :].T
        out_ref[pl.ds(1, LANES, stride=2), :] = acc[LANES:2 * LANES, :].T


def sums_call(spectra, sensor_ids):
    windows, frames, bins = spectra.shape
    chunks = bins // LANES
    grid_spec = pltpu.PrefetchScalarGridSpec(
        num_scalar_prefetch=1,
        grid=(windows // STEP_WINDOWS,),
        in_specs=[pl.BlockSpec((STEP_WINDOWS, frames, bins), lambda i, s: (i, 0, 0))],
        out_specs=pl.BlockSpec((2 * LANES, LANES), lambda i, s: (0, 0)),
        scratch_shapes=[pltpu.VMEM((2 * LANES, LANES), F32)],
    )
    return pl.pallas_call(
        functools.partial(sums_kernel, chunks=chunks, count=windows),
        grid_spec=grid_spec,
        out_shape=jax.ShapeDtypeStruct((2 * LANES, LANES), F32),
        compiler_params=pltpu.CompilerParams(vmem_limit_bytes=VMEM_LIMIT),
        name="window_sums",
    )(sensor_ids.reshape(windows), spectra)


def sort_kernel(spec_ref, out_ref, lane, *, chunks):
    windows, frames, bins = spec_ref.shape
    quarter = frames // 4
    rows = 32
    for w in range(windows):
        def body(i, carry):
            at = pl.multiple_of(i * rows, rows)
            value = jnp.log(1.0 + spec_ref[w, pl.ds(at, rows), :].astype(F32))
            for k in range(chunks):
                lane[w % 2, k, pl.ds(at, rows), :] = value[:, k * LANES:(k + 1) * LANES]
            return carry

        lax.fori_loop(0, frames // rows, body, 0, unroll=2)
        for i in range(4):
            for k in range(chunks):
                out_ref[i, w * quarter:(w + 1) * quarter, k * LANES:(k + 1) * LANES] = lane[w % 2, k, pl.ds(i, quarter, stride=4), :]


def sort_call(spectra):
    windows, frames, bins = spectra.shape
    chunks = bins // LANES
    quarter = frames // 4
    rows = STEP_WINDOWS * quarter
    size = windows * frames * bins
    return pl.pallas_call(
        functools.partial(sort_kernel, chunks=chunks),
        grid=(windows // STEP_WINDOWS,),
        in_specs=[pl.BlockSpec((STEP_WINDOWS, frames, bins), lambda i: (i, 0, 0))],
        out_specs=pl.BlockSpec((4, rows, bins), lambda i: (0, i, 0)),
        out_shape=jax.ShapeDtypeStruct((4, windows * quarter, bins), F32),
        scratch_shapes=[pltpu.VMEM((2, chunks, frames, LANES), F32)],
        compiler_params=pltpu.CompilerParams(vmem_limit_bytes=VMEM_LIMIT),
        cost_estimate=pl.CostEstimate(flops=8 * size, bytes_accessed=6 * size, transcendentals=size),
        name="sort_frames",
    )(spectra)


def stats_kernel(in_ref, out_ref, *, windows, chunks, sensors, per_sensor):
    width = 2 * chunks
    data = in_ref[pl.ds(0, LANES, stride=2), :].T
    labels = in_ref[pl.ds(1, LANES, stride=2), :].T
    sensor_rows = lax.broadcasted_iota(jnp.int32, (sensors, LANES), 0).astype(F32)
    tables = [(sensor_rows == labels[w:w + 1, :]).astype(F32).astype(BF16) for w in range(windows)]
    table = jnp.concatenate(tables, axis=1)
    values = jnp.concatenate([data[w * width:(w + 1) * width, :] for w in range(windows)], axis=1)
    parts = dot_nt(jnp.concatenate(split3(values), axis=0), table)
    sums = parts[0:width] + parts[width:2 * width] + parts[2 * width:3 * width]
    center = sums[0:chunks] / per_sensor
    factor = lax.rsqrt(sums[chunks:width] / per_sensor - center * center + EPS)
    both = jnp.concatenate([center, factor], axis=0)
    back = dot(jnp.concatenate(split3(both), axis=0), table)
    back = back[0:width] + back[width:2 * width] + back[2 * width:3 * width]
    rows = jnp.concatenate([back[:, w * LANES:(w + 1) * LANES] for w in range(windows)], axis=0)
    out_ref[...] = rows.T


def stats_call(received, windows, chunks, sensors, per_sensor):
    return pl.pallas_call(
        functools.partial(stats_kernel, windows=windows, chunks=chunks, sensors=sensors, per_sensor=float(per_sensor)),
        out_shape=jax.ShapeDtypeStruct((LANES, LANES), F32),
        compiler_params=pltpu.CompilerParams(vmem_limit_bytes=VMEM_LIMIT),
        name="sensor_stats",
    )(received)


def enc1_kernel(perm_ref, log_ref, coef_ref, w_ref, normed_ref, pre_ref, stat_ref, coef, stat, *, chunks, quarter, cols, copies):
    step = pl.program_id(0)
    bins = log_ref.shape[2]
    windows = log_ref.shape[1] // quarter
    channels = w_ref.shape[1]
    all_windows = windows * pl.num_programs(0)
    width = 2 * chunks

    @pl.when(step == 0)
    def _():
        coef[...] = coef_ref[...].T

    for w in range(windows):
        start = pl.multiple_of((step * windows + w) * width, width)
        both = coef[pl.ds(start, width), :]
        low, high = w * quarter, (w + 1) * quarter
        for k in range(chunks):
            left, right = k * LANES, (k + 1) * LANES
            center = both[k:k + 1, :]
            factor = both[chunks + k:chunks + k + 1, :]
            for i in range(4):
                normed_ref[i, low:high, left:right] = ((log_ref[i, low:high, left:right] - center) * factor).astype(BF16)

    w0, w1, w2, w3 = (w_ref[k * bins:(k + 1) * bins, :] for k in range(4))
    f0, f1, f2, f3 = (normed_ref[i] for i in range(4))
    even = shift_down(dot(f3, w0), quarter) + dot(f0, w1) + dot(f1, w2) + dot(f2, w3)
    odd = dot(f1, w0) + dot(f2, w1) + dot(f3, w2) + shift_up(dot(f0, w3), quarter)
    pre_ref[0] = even
    pre_ref[1] = odd
    for w in range(windows):
        part_e = even[w * quarter:(w + 1) * quarter]
        part_o = odd[w * quarter:(w + 1) * quarter]
        mean = (jnp.sum(part_e, axis=0, keepdims=True) + jnp.sum(part_o, axis=0, keepdims=True)) / (2 * quarter)
        diff_e = part_e - mean
        diff_o = part_o - mean
        spread = (jnp.sum(diff_e * diff_e, axis=0, keepdims=True) + jnp.sum(diff_o * diff_o, axis=0, keepdims=True)) / (2 * quarter)
        place = group_rank(perm_ref, step * windows + w, all_windows, cols)
        stat[pl.ds(place, 1), 0:channels] = mean
        stat[pl.ds(place, 1), channels:2 * channels] = spread

    @pl.when(step == pl.num_programs(0) - 1)
    def _():
        for d in range(copies):
            stat_ref[d] = stat[...]


def enc1_call(permutation, logs, coef, w_enc1, quarter, cols):
    bins = logs.shape[2]
    windows = logs.shape[1] // quarter
    chunks = bins // LANES
    channels = w_enc1.shape[1]
    rows = STEP_WINDOWS * quarter
    grid_spec = pltpu.PrefetchScalarGridSpec(
        num_scalar_prefetch=1,
        grid=(windows // STEP_WINDOWS,),
        in_specs=[
            pl.BlockSpec((4, rows, bins), lambda i, p: (0, i, 0)),
            pl.BlockSpec((LANES, LANES), lambda i, p: (0, 0)),
            pl.BlockSpec(w_enc1.shape, lambda i, p: (0, 0)),
        ],
        out_specs=[
            pl.BlockSpec((4, rows, bins), lambda i, p: (0, i, 0)),
            pl.BlockSpec((2, rows, channels), lambda i, p: (0, i, 0)),
            pl.BlockSpec((cols, windows, 2 * channels), lambda i, p: (0, 0, 0)),
        ],
        scratch_shapes=[
            pltpu.VMEM((LANES, LANES), F32),
            pltpu.VMEM((windows, 2 * channels), F32),
        ],
    )
    return pl.pallas_call(
        functools.partial(enc1_kernel, chunks=chunks, quarter=quarter, cols=cols, copies=cols),
        grid_spec=grid_spec,
        out_shape=[
            jax.ShapeDtypeStruct((4, windows * quarter, bins), BF16),
            jax.ShapeDtypeStruct((2, windows * quarter, channels), F32),
            jax.ShapeDtypeStruct((cols, windows, 2 * channels), F32),
        ],
        compiler_params=pltpu.CompilerParams(vmem_limit_bytes=VMEM_LIMIT),
        name="normalize_enc1",
    )(permutation, logs, coef, w_enc1)


def turn_kernel(in_ref, out_ref):
    out_ref[0] = in_ref[0].T


def turn_call(normed, steps):
    classes, total, bins = normed.shape
    rows = total // steps
    size = classes * total * bins
    return pl.pallas_call(
        turn_kernel,
        grid=(classes, steps),
        in_specs=[pl.BlockSpec((1, rows, bins), lambda i, j: (i, j, 0))],
        out_specs=pl.BlockSpec((1, bins, rows), lambda i, j: (i, 0, j)),
        out_shape=jax.ShapeDtypeStruct((classes, bins, total), normed.dtype),
        compiler_params=pltpu.CompilerParams(vmem_limit_bytes=VMEM_LIMIT),
        cost_estimate=pl.CostEstimate(flops=4 * size, bytes_accessed=4 * size, transcendentals=0),
        name="turn_normed",
    )(normed)


def window_rows(perm_ref, table, step, windows, quarter, all_windows, cols, first, last):
    parts = []
    for w in range(windows):
        place = group_rank(perm_ref, step * windows + w, all_windows, cols)
        parts.append(jnp.broadcast_to(table[pl.ds(place, 1), first:last], (quarter, last - first)))
    return jnp.concatenate(parts, axis=0)


def write_halves(core_ref, grads, own_ref, send_ref):
    half = own_ref.shape[0]
    own_ref[...] = grads[pl.ds(pl.multiple_of(core_ref[0] * half, half), half), :]
    send_ref[...] = grads[pl.ds(pl.multiple_of((1 - core_ref[0]) * half, half), half), :]


def middle_kernel(perm_ref, core_ref, normed_ref, pre_ref, stat_ref, v_ref, b_ref, c_ref,
                  own_ref, send_ref, back_ref, moment_ref, sums_ref,
                  grads, moment, sums, *, quarter, cols, total_windows):
    step = pl.program_id(0)
    channels = v_ref.shape[1]
    bins = normed_ref.shape[2]
    rows = normed_ref.shape[1]
    windows = rows // quarter
    all_windows = windows * pl.num_programs(0)
    ch = channels

    @pl.when(step == 0)
    def _():
        means = stat_ref[:, :, 0:ch]
        mean = jnp.mean(means, axis=0)
        diff = means - mean[None]
        variance = jnp.mean(stat_ref[:, :, ch:2 * ch] + diff * diff, axis=0)
        moment[:, 0:ch] = mean
        moment[:, ch:2 * ch] = lax.rsqrt(variance + EPS)
        moment_ref[...] = moment[...]
        grads[...] = jnp.zeros_like(grads)

    mean = window_rows(perm_ref, moment, step, windows, quarter, all_windows, cols, 0, ch)
    inverse = window_rows(perm_ref, moment, step, windows, quarter, all_windows, cols, ch, 2 * ch)
    hat_e = (pre_ref[0] - mean) * inverse
    hat_o = (pre_ref[1] - mean) * inverse
    a_e = (hat_e * sigmoid(hat_e)).astype(BF16)
    a_o = (hat_o * sigmoid(hat_o)).astype(BF16)
    v0, v1, v2, v3 = (v_ref[k * ch:(k + 1) * ch, :] for k in range(4))
    pre2 = shift_down(dot(a_o, v0), quarter) + dot(a_e, v1) + dot(a_o, v2) + shift_up(dot(a_e, v3), quarter)
    gate2 = sigmoid(pre2)
    h32 = (pre2 * gate2).astype(BF16).astype(F32)
    h = h32.astype(BF16)
    b0, b1, b2, b3 = (b_ref[:, k * ch:(k + 1) * ch] for k in range(4))
    d1_e = dot(h, b1) + shift_down(dot(h, b3), quarter)
    d1_o = dot(h, b2) + shift_up(dot(h, b0), quarter)
    gate_e = sigmoid(d1_e)
    gate_o = sigmoid(d1_o)
    de32 = (d1_e * gate_e)
    do32 = (d1_o * gate_o)
    de = de32.astype(BF16)
    do = do32.astype(BF16)
    de_up = shift_up(de32, quarter).astype(BF16)
    do_down = shift_down(do32, quarter).astype(BF16)
    c0, c1, c2, c3 = (c_ref[:, k * bins:(k + 1) * bins] for k in range(4))

    def delta(rebuilt, i):
        return ((rebuilt - normed_ref[i].astype(F32)) / total_windows).astype(BF16)

    g0 = delta(dot(de, c1) + dot(do_down, c3), 0)
    g1 = delta(dot(de, c2) + dot(do, c0), 1)
    g2 = delta(dot(do, c1) + dot(de, c3), 2)
    g3 = delta(dot(do, c2) + dot(de_up, c0), 3)
    halves = bins // ch
    base_b = 4 * bins
    base_v = base_b + 4 * ch

    def add_c(k, value):
        for j in range(halves):
            at = (k * halves + j) * ch
            grads[at:at + ch, :] += value[:, j * ch:(j + 1) * ch]

    add_c(0, dot_tn(de_up, g3) + dot_tn(do, g1))
    add_c(1, dot_tn(de, g0) + dot_tn(do, g2))
    add_c(2, dot_tn(de, g1) + dot_tn(do, g3))
    add_c(3, dot_tn(de, g2) + dot_tn(do_down, g0))
    back_e = shift_down(dot_nt(g3, c0), quarter) + dot_nt(g0, c1) + dot_nt(g1, c2) + dot_nt(g2, c3)
    back_o = dot_nt(g1, c0) + dot_nt(g2, c1) + dot_nt(g3, c2) + shift_up(dot_nt(g0, c3), quarter)
    dd_e = (back_e * (gate_e * (1.0 + d1_e * (1.0 - gate_e)))).astype(BF16)
    dd_o = (back_o * (gate_o * (1.0 + d1_o * (1.0 - gate_o)))).astype(BF16)
    h_up = shift_up(h32, quarter).astype(BF16)
    h_down = shift_down(h32, quarter).astype(BF16)
    grads[base_b:base_b + ch, :] += dot_tn(h_up, dd_o)
    grads[base_b + ch:base_b + 2 * ch, :] += dot_tn(h, dd_e)
    grads[base_b + 2 * ch:base_b + 3 * ch, :] += dot_tn(h, dd_o)
    grads[base_b + 3 * ch:base_b + 4 * ch, :] += dot_tn(h_down, dd_e)
    back2 = shift_down(dot_nt(dd_o, b0), quarter) + dot_nt(dd_e, b1) + dot_nt(dd_o, b2) + shift_up(dot_nt(dd_e, b3), quarter)
    d2_32 = (back2 * (gate2 * (1.0 + pre2 * (1.0 - gate2)))).astype(BF16).astype(F32)
    d2 = d2_32.astype(BF16)
    d2_up = shift_up(d2_32, quarter).astype(BF16)
    d2_down = shift_down(d2_32, quarter).astype(BF16)
    grads[base_v:base_v + ch, :] += dot_tn(a_o, d2_up)
    grads[base_v + ch:base_v + 2 * ch, :] += dot_tn(a_e, d2)
    grads[base_v + 2 * ch:base_v + 3 * ch, :] += dot_tn(a_o, d2)
    grads[base_v + 3 * ch:base_v + 4 * ch, :] += dot_tn(a_e, d2_down)
    fold_e = dot_nt(d2, v1) + shift_down(dot_nt(d2, v3), quarter)
    fold_o = dot_nt(d2, v2) + shift_up(dot_nt(d2, v0), quarter)
    gate_he = sigmoid(hat_e)
    gate_ho = sigmoid(hat_o)
    fold_e = fold_e * (gate_he * (1.0 + hat_e * (1.0 - gate_he)))
    fold_o = fold_o * (gate_ho * (1.0 + hat_o * (1.0 - gate_ho)))
    back_ref[0] = fold_e
    back_ref[1] = fold_o
    cross_e = fold_e * hat_e
    cross_o = fold_o * hat_o
    for w in range(windows):
        low, high = w * quarter, (w + 1) * quarter
        first = jnp.sum(fold_e[low:high] + fold_o[low:high], axis=0, keepdims=True)
        second = jnp.sum(cross_e[low:high] + cross_o[low:high], axis=0, keepdims=True)
        place = group_rank(perm_ref, step * windows + w, all_windows, cols)
        sums[pl.ds(place, 1), 0:ch] = first
        sums[pl.ds(place, 1), ch:2 * ch] = second

    @pl.when(step == pl.num_programs(0) - 1)
    def _():
        for d in range(cols):
            sums_ref[d] = sums[...]
        write_halves(core_ref, grads, own_ref, send_ref)


def middle_call(permutation, core, normed, pre, stat, w_enc2, w_dec1, w_dec2, quarter, cols, total_windows):
    bins = normed.shape[2]
    channels = w_enc2.shape[1]
    windows = normed.shape[1] // quarter
    rows = STEP_WINDOWS * quarter
    total = 4 * bins + 8 * channels
    whole2 = lambda i, p, c: (0, 0)
    whole3 = lambda i, p, c: (0, 0, 0)
    grid_spec = pltpu.PrefetchScalarGridSpec(
        num_scalar_prefetch=2,
        grid=(windows // STEP_WINDOWS,),
        in_specs=[
            pl.BlockSpec((4, rows, bins), lambda i, p, c: (0, i, 0)),
            pl.BlockSpec((2, rows, channels), lambda i, p, c: (0, i, 0)),
            pl.BlockSpec(stat.shape, whole3),
            pl.BlockSpec(w_enc2.shape, whole2),
            pl.BlockSpec(w_dec1.shape, whole2),
            pl.BlockSpec(w_dec2.shape, whole2),
        ],
        out_specs=[
            pl.BlockSpec((total // 2, channels), whole2),
            pl.BlockSpec((total // 2, channels), whole2),
            pl.BlockSpec((2, rows, channels), lambda i, p, c: (0, i, 0)),
            pl.BlockSpec((windows, 2 * channels), whole2),
            pl.BlockSpec(stat.shape, whole3),
        ],
        scratch_shapes=[
            pltpu.VMEM((total, channels), F32),
            pltpu.VMEM((windows, 2 * channels), F32),
            pltpu.VMEM((windows, 2 * channels), F32),
        ],
    )
    return pl.pallas_call(
        functools.partial(middle_kernel, quarter=quarter, cols=cols, total_windows=float(total_windows)),
        grid_spec=grid_spec,
        out_shape=[
            jax.ShapeDtypeStruct((total // 2, channels), F32),
            jax.ShapeDtypeStruct((total // 2, channels), F32),
            jax.ShapeDtypeStruct(pre.shape, F32),
            jax.ShapeDtypeStruct((windows, 2 * channels), F32),
            jax.ShapeDtypeStruct(stat.shape, F32),
        ],
        compiler_params=pltpu.CompilerParams(vmem_limit_bytes=VMEM_LIMIT),
        name="middle",
    )(permutation, core, normed, pre, stat, w_enc2, w_dec1, w_dec2)


def grad_kernel(perm_ref, core_ref, turned_ref, pre_ref, back_ref, moment_ref, sums_ref, own_ref, send_ref, grads, scale, *, quarter, cols):
    step = pl.program_id(0)
    bins = turned_ref.shape[1]
    rows = turned_ref.shape[2]
    ch = pre_ref.shape[2]
    windows = rows // quarter
    all_windows = windows * pl.num_programs(0)

    @pl.when(step == 0)
    def _():
        scale[...] = jnp.sum(sums_ref[...], axis=0) / (2.0 * quarter * cols)
        grads[...] = jnp.zeros_like(grads)

    pick = functools.partial(window_rows, perm_ref, step=step, windows=windows, quarter=quarter, all_windows=all_windows, cols=cols)
    mean = pick(table=moment_ref, first=0, last=ch)
    inverse = pick(table=moment_ref, first=ch, last=2 * ch)
    first = pick(table=scale, first=0, last=ch)
    second = pick(table=scale, first=ch, last=2 * ch)
    hat_e = (pre_ref[0] - mean) * inverse
    hat_o = (pre_ref[1] - mean) * inverse
    de32 = (back_ref[0] - first - hat_e * second) * inverse
    do32 = (back_ref[1] - first - hat_o * second) * inverse
    de = de32.astype(BF16)
    do = do32.astype(BF16)
    de_up = shift_up(de32, quarter).astype(BF16)
    do_down = shift_down(do32, quarter).astype(BF16)
    f0, f1, f2, f3 = (turned_ref[i] for i in range(4))
    grads[0:bins, :] += dot(f3, de_up) + dot(f1, do)
    grads[bins:2 * bins, :] += dot(f0, de) + dot(f2, do)
    grads[2 * bins:3 * bins, :] += dot(f1, de) + dot(f3, do)
    grads[3 * bins:4 * bins, :] += dot(f2, de) + dot(f0, do_down)

    @pl.when(step == pl.num_programs(0) - 1)
    def _():
        write_halves(core_ref, grads, own_ref, send_ref)


def grad_call(permutation, core, turned, pre, back, moment, sums, quarter, cols):
    bins = turned.shape[1]
    channels = pre.shape[2]
    windows = turned.shape[2] // quarter
    rows = STEP_WINDOWS * quarter
    grid_spec = pltpu.PrefetchScalarGridSpec(
        num_scalar_prefetch=2,
        grid=(windows // STEP_WINDOWS,),
        in_specs=[
            pl.BlockSpec((4, bins, rows), lambda i, p, c: (0, 0, i)),
            pl.BlockSpec((2, rows, channels), lambda i, p, c: (0, i, 0)),
            pl.BlockSpec((2, rows, channels), lambda i, p, c: (0, i, 0)),
            pl.BlockSpec(moment.shape, lambda i, p, c: (0, 0)),
            pl.BlockSpec(sums.shape, lambda i, p, c: (0, 0, 0)),
        ],
        out_specs=[pl.BlockSpec((2 * bins, channels), lambda i, p, c: (0, 0))] * 2,
        scratch_shapes=[pltpu.VMEM((4 * bins, channels), F32), pltpu.VMEM((windows, 2 * channels), F32)],
    )
    return pl.pallas_call(
        functools.partial(grad_kernel, quarter=quarter, cols=cols),
        grid_spec=grid_spec,
        out_shape=[jax.ShapeDtypeStruct((2 * bins, channels), F32)] * 2,
        compiler_params=pltpu.CompilerParams(vmem_limit_bytes=VMEM_LIMIT),
        name="grad_enc1",
    )(permutation, core, turned, pre, back, moment, sums)


def swap_cores(values):
    return lax.ppermute(values, "core", [(0, 1), (1, 0)])


def exchange(values, axes):
    return lax.all_to_all(values, axes, split_axis=0, concat_axis=0, tiled=True)


def chip_sums(parts, axes, chips):
    total = [(own + swap_cores(send)).astype(BF16).reshape(chips, -1, own.shape[1]) for own, send in parts]
    total = jnp.concatenate(total, axis=1)
    return exchange(total.reshape(-1, total.shape[2]), axes).reshape(total.shape)


def owner_kernel(in_ref, out_ref):
    chips, rows, width = in_ref.shape

    def body(i, total):
        return total + in_ref[i].astype(F32)

    total = lax.fori_loop(0, chips, body, jnp.zeros((rows, width), F32), unroll=4)
    largest = jnp.max(jnp.max(jnp.abs(total), axis=0, keepdims=True), axis=1, keepdims=True)
    exponent = jnp.clip(jnp.ceil(jnp.log2(largest)), -110.0, 126.0)
    out_ref[0:rows, :] = total * jnp.exp2(14.0 - exponent)
    out_ref[rows:, :] = jnp.broadcast_to(exponent, (SCALE_ROWS, width))


def owner_call(pieces):
    chips, rows, width = pieces.shape
    return pl.pallas_call(
        owner_kernel,
        out_shape=jax.ShapeDtypeStruct((rows + SCALE_ROWS, width), F32),
        compiler_params=pltpu.CompilerParams(vmem_limit_bytes=VMEM_LIMIT),
        name="owner_sum",
    )(pieces)


def gather_rows(piece, axes, chips):
    rows, width = piece.shape
    copies = jnp.broadcast_to(piece.astype(jnp.float16)[None], (chips, rows, width))
    return exchange(copies.reshape(-1, width), axes).reshape(chips, rows, width)


def place_kernel(core_ref, mine_ref, other_ref, grad_w_ref, grad_v_ref, grad_b_ref, grad_c_ref, *, cut):
    step = pl.program_id(0)
    half = pl.num_programs(0) // 2
    total = mine_ref.shape[1]
    rows = total - SCALE_ROWS
    first = core_ref[0] == 0
    for i in range(mine_ref.shape[0]):
        mine, other = mine_ref[i], other_ref[i]
        low = jnp.where(first, mine, other)
        high = jnp.where(first, other, mine)
        low = low[0:rows] * jnp.exp2(low[rows:rows + 1] - 14.0)
        high = high[0:rows] * jnp.exp2(high[rows:rows + 1] - 14.0)
        early, late = i * cut, i * (rows - cut)
        grad_c_ref[early:early + cut, :] = low[0:cut]
        grad_w_ref[0, late:late + rows - cut, :] = low[cut:rows]
        grad_w_ref[1, late:late + rows - cut, :] = high[cut:rows]

        @pl.when(step < half)
        def _():
            grad_b_ref[early:early + cut, :] = high[0:cut]

        @pl.when(step >= half)
        def _():
            grad_v_ref[early:early + cut, :] = high[0:cut]


def place_call(core, mine, other, cut, channels, bins):
    chips, total, width = mine.shape
    late = total - SCALE_ROWS - cut
    group = channels // cut
    steps = chips // group
    grid_spec = pltpu.PrefetchScalarGridSpec(
        num_scalar_prefetch=1,
        grid=(steps,),
        in_specs=[pl.BlockSpec((group, total, width), lambda i, c: (i, 0, 0))] * 2,
        out_specs=[
            pl.BlockSpec((2, group * late, width), lambda i, c: (0, i, 0)),
            pl.BlockSpec((channels, width), lambda i, c: (jnp.maximum(i - steps // 2, 0), 0)),
            pl.BlockSpec((channels, width), lambda i, c: (0, jnp.minimum(i, steps // 2 - 1))),
            pl.BlockSpec((channels, width), lambda i, c: (0, i)),
        ],
    )
    return pl.pallas_call(
        functools.partial(place_kernel, cut=cut),
        grid_spec=grid_spec,
        out_shape=[
            jax.ShapeDtypeStruct((2, chips * late, width), F32),
            jax.ShapeDtypeStruct((4 * channels, channels), F32),
            jax.ShapeDtypeStruct((channels, 4 * channels), F32),
            jax.ShapeDtypeStruct((channels, 4 * bins), F32),
        ],
        compiler_params=pltpu.CompilerParams(vmem_limit_bytes=VMEM_LIMIT),
        name="place_gradients",
    )(core, mine, other)


def local(spectra, sensor_ids, permutation, w_enc1, w_enc2, w_dec1, w_dec2):
    windows, frames, bins = spectra.shape
    channels = w_enc1.shape[1]
    col_axes = ("pair", "core")
    chip_axes = ("row", "pair")
    every = ("row", "pair", "core")
    cols = lax.axis_size("pair") * lax.axis_size("core")
    chips = lax.axis_size("row") * lax.axis_size("pair")
    total_windows = windows * lax.axis_size("row") * cols
    sensors = total_windows // WIN_SENSOR
    chunks = bins // LANES
    quarter = frames // 4
    core_index = lax.axis_index("core")
    core = core_index.astype(jnp.int32).reshape(1)

    sums = exchange(sums_call(spectra, sensor_ids), every)
    coef = exchange(stats_call(sums, windows, chunks, sensors, WIN_SENSOR * frames), every)
    logs = sort_call(spectra)
    normed, pre, stat = enc1_call(permutation, logs, coef, w_enc1, quarter, cols)
    turned = turn_call(normed, windows // STEP_WINDOWS)
    stat = exchange(stat.reshape(cols * windows, 2 * channels), col_axes).reshape(cols, windows, 2 * channels)
    own, send, back, moment, moments = middle_call(
        permutation, core, normed, pre, stat, w_enc2, w_dec1, w_dec2, quarter, cols, total_windows)
    moments = exchange(moments.reshape(cols * windows, 2 * channels), col_axes).reshape(cols, windows, 2 * channels)
    late = grad_call(permutation, core, turned, pre, back, moment, moments, quarter, cols)
    piece = owner_call(chip_sums([(own, send), late], chip_axes, chips))
    mine = gather_rows(piece, chip_axes, chips)
    other = swap_cores(mine)
    grad_w, grad_v, grad_b, grad_c = place_call(
        core, mine.astype(F32), other.astype(F32), own.shape[0] // chips, channels, bins)
    return (grad_w.reshape(4 * bins, channels), grad_v, grad_b, grad_c)


def solution(mesh):
    rows, cols = mesh.devices.shape
    inner = Mesh(mesh.devices.reshape(rows, cols // 2, 2), ("row", "pair", "core"))
    spread = ("row", "pair", "core")
    return jax.shard_map(
        local,
        mesh=inner,
        in_specs=(P(spread, None, None), P(spread, None), P(spread), P(), P(), P(), P()),
        out_specs=(P(), P(), P(), P()),
        check_vma=False,
    )
```

```python
import functools

import jax
import jax.numpy as jnp
from jax import lax
from jax.experimental import pallas as pl
from jax.experimental.pallas import tpu as pltpu
from jax.sharding import Mesh, PartitionSpec as P

WIN_SENSOR = 8
EPS = 1e-05
F32 = jnp.float32
BF16 = jnp.bfloat16
LANES = 128
STEP_WINDOWS = 8
SORT_WINDOWS = 4
SCALE_ROWS = 8
MIB = 1024 * 1024


ON_CHIP = pl.BlockSpec(memory_space=pltpu.VMEM)


def on_chip(values):
    return pltpu.with_memory_space_constraint(values, pltpu.VMEM)


def step_rows(ref, rows):
    return ref.at[:, pl.ds(pl.multiple_of(pl.program_id(0) * rows, rows), rows), :]


def dot(left, right):
    return jnp.dot(left, right, preferred_element_type=F32)


def dot_nt(left, right):
    return lax.dot_general(left, right, (((1,), (1,)), ((), ())), preferred_element_type=F32)


def dot_tn(left, right):
    return lax.dot_general(left, right, (((0,), (0,)), ((), ())), preferred_element_type=F32)


def split3(values):
    first = values.astype(BF16)
    rest = values - first.astype(F32)
    second = rest.astype(BF16)
    third = (rest - second.astype(F32)).astype(BF16)
    return first, second, third


def sigmoid(values):
    return 1.0 / (1.0 + jnp.exp(-values))


def shift_down(values, period):
    rows = lax.broadcasted_iota(jnp.int32, values.shape, 0) % period
    return jnp.where(rows == 0, 0.0, pltpu.roll(values, 1, 0))


def shift_up(values, period):
    total = values.shape[0]
    rows = lax.broadcasted_iota(jnp.int32, values.shape, 0) % period
    return jnp.where(rows == period - 1, 0.0, pltpu.roll(values, total - 1, 0))


def group_rank(perm_ref, window, window_dev, col_count):
    trainer = perm_ref[window] // window_dev
    per_row = 2
    return (trainer // col_count) * per_row + trainer % per_row


def sums_kernel(ids_ref, spec_ref, log_ref, out_ref, acc, lane, *, chunks, count):
    step = pl.program_id(0)
    windows, frames, bins = spec_ref.shape
    quarter = frames // 4
    rows = 16
    log_ref = step_rows(log_ref, windows * quarter)

    for w in range(windows):
        def body(i, carry):
            total, square = carry
            start = pl.multiple_of(i * rows, rows)
            value = jnp.log(1.0 + spec_ref[w, pl.ds(start, rows), :].astype(F32))
            for k in range(chunks):
                lane[w % 2, k, pl.ds(start, rows), :] = value[:, k * LANES:(k + 1) * LANES]
            value_sq = value * value
            return (total + value[0:8] + value[8:16], square + value_sq[0:8] + value_sq[8:16])

        zero = jnp.zeros((8, bins), F32)
        total, square = lax.fori_loop(0, frames // rows, body, (zero, zero), unroll=4)
        total = jnp.sum(total, axis=0, keepdims=True)
        square = jnp.sum(square, axis=0, keepdims=True)
        pieces = [total[:, k * LANES:(k + 1) * LANES] for k in range(chunks)]
        pieces += [square[:, k * LANES:(k + 1) * LANES] for k in range(chunks)]
        start = pl.multiple_of((step * windows + w) * 2 * chunks, 2 * chunks)
        acc[pl.ds(start, 2 * chunks), :] = jnp.concatenate(pieces, axis=0)
        for i in range(4):
            for k in range(chunks):
                log_ref[i, w * quarter:(w + 1) * quarter, k * LANES:(k + 1) * LANES] = lane[w % 2, k, pl.ds(i, quarter, stride=4), :]

    @pl.when(step == pl.num_programs(0) - 1)
    def _():
        acc[LANES:2 * LANES, :] = jnp.zeros((LANES, LANES), F32)
        for w in range(count):
            acc[LANES + w:LANES + w + 1, :] = jnp.full((1, LANES), ids_ref[w], jnp.int32).astype(F32)
        out_ref[pl.ds(0, LANES, stride=2), :] = acc[0:LANES, :].T
        out_ref[pl.ds(1, LANES, stride=2), :] = acc[LANES:2 * LANES, :].T


def sums_call(spectra, sensor_ids):
    windows, frames, bins = spectra.shape
    chunks = bins // LANES
    grid_spec = pltpu.PrefetchScalarGridSpec(
        num_scalar_prefetch=1,
        grid=(windows // SORT_WINDOWS,),
        in_specs=[pl.BlockSpec((SORT_WINDOWS, frames, bins), lambda i, s: (i, 0, 0))],
        out_specs=[ON_CHIP, pl.BlockSpec((2 * LANES, LANES), lambda i, s: (0, 0))],
        scratch_shapes=[pltpu.VMEM((2 * LANES, LANES), F32), pltpu.VMEM((2, chunks, frames, LANES), F32)],
    )
    return pl.pallas_call(
        functools.partial(sums_kernel, chunks=chunks, count=windows),
        grid_spec=grid_spec,
        out_shape=[
            pltpu.VMEM((4, windows * frames // 4, bins), F32),
            jax.ShapeDtypeStruct((2 * LANES, LANES), F32),
        ],
        compiler_params=pltpu.CompilerParams(vmem_limit_bytes=10 * MIB),
        name="sort_and_sum",
    )(sensor_ids.reshape(windows), pltpu.with_memory_space_constraint(spectra, pltpu.HBM))


def stats_kernel(in_ref, out_ref, *, windows, chunks, sensors, per_sensor):
    width = 2 * chunks
    data = in_ref[pl.ds(0, LANES, stride=2), :].T
    labels = in_ref[pl.ds(1, LANES, stride=2), :].T
    sensor_rows = lax.broadcasted_iota(jnp.int32, (sensors, LANES), 0).astype(F32)
    tables = [(sensor_rows == labels[w:w + 1, :]).astype(F32).astype(BF16) for w in range(windows)]
    table = jnp.concatenate(tables, axis=1)
    values = jnp.concatenate([data[w * width:(w + 1) * width, :] for w in range(windows)], axis=1)
    parts = dot_nt(jnp.concatenate(split3(values), axis=0), table)
    sums = parts[0:width] + parts[width:2 * width] + parts[2 * width:3 * width]
    center = sums[0:chunks] / per_sensor
    factor = lax.rsqrt(sums[chunks:width] / per_sensor - center * center + EPS)
    both = jnp.concatenate([center, factor], axis=0)
    back = dot(jnp.concatenate(split3(both), axis=0), table)
    back = back[0:width] + back[width:2 * width] + back[2 * width:3 * width]
    rows = jnp.concatenate([back[:, w * LANES:(w + 1) * LANES] for w in range(windows)], axis=0)
    out_ref[...] = rows.T


def stats_call(received, windows, chunks, sensors, per_sensor):
    return pl.pallas_call(
        functools.partial(stats_kernel, windows=windows, chunks=chunks, sensors=sensors, per_sensor=float(per_sensor)),
        out_shape=jax.ShapeDtypeStruct((LANES, LANES), F32),
        compiler_params=pltpu.CompilerParams(vmem_limit_bytes=12 * MIB),
        name="sensor_stats",
    )(received)


def enc1_kernel(perm_ref, log_ref, coef_ref, w_ref, normed_ref, pre_ref, stat_ref, coef, stat, *, chunks, quarter, cols, copies):
    step = pl.program_id(0)
    bins = log_ref.shape[2]
    windows = STEP_WINDOWS
    log_ref, normed_ref, pre_ref = (step_rows(ref, windows * quarter) for ref in (log_ref, normed_ref, pre_ref))
    channels = w_ref.shape[1]
    all_windows = windows * pl.num_programs(0)
    width = 2 * chunks

    @pl.when(step == 0)
    def _():
        coef[...] = coef_ref[...].T

    for w in range(windows):
        start = pl.multiple_of((step * windows + w) * width, width)
        both = coef[pl.ds(start, width), :]
        low, high = w * quarter, (w + 1) * quarter
        for k in range(chunks):
            left, right = k * LANES, (k + 1) * LANES
            center = both[k:k + 1, :]
            factor = both[chunks + k:chunks + k + 1, :]
            for i in range(4):
                normed_ref[i, low:high, left:right] = ((log_ref[i, low:high, left:right] - center) * factor).astype(BF16)

    w0, w1, w2, w3 = (w_ref[k * bins:(k + 1) * bins, :] for k in range(4))
    f0, f1, f2, f3 = (normed_ref[i] for i in range(4))
    even = shift_down(dot(f3, w0), quarter) + dot(f0, w1) + dot(f1, w2) + dot(f2, w3)
    odd = dot(f1, w0) + dot(f2, w1) + dot(f3, w2) + shift_up(dot(f0, w3), quarter)
    pre_ref[0] = even
    pre_ref[1] = odd
    for w in range(windows):
        part_e = even[w * quarter:(w + 1) * quarter]
        part_o = odd[w * quarter:(w + 1) * quarter]
        mean = (jnp.sum(part_e, axis=0, keepdims=True) + jnp.sum(part_o, axis=0, keepdims=True)) / (2 * quarter)
        diff_e = part_e - mean
        diff_o = part_o - mean
        spread = (jnp.sum(diff_e * diff_e, axis=0, keepdims=True) + jnp.sum(diff_o * diff_o, axis=0, keepdims=True)) / (2 * quarter)
        place = group_rank(perm_ref, step * windows + w, all_windows, cols)
        stat[pl.ds(place, 1), 0:channels] = mean
        stat[pl.ds(place, 1), channels:2 * channels] = spread

    @pl.when(step == pl.num_programs(0) - 1)
    def _():
        for d in range(copies):
            stat_ref[d] = stat[...]


def enc1_call(permutation, logs, coef, w_enc1, quarter, cols):
    bins = logs.shape[2]
    windows = logs.shape[1] // quarter
    chunks = bins // LANES
    channels = w_enc1.shape[1]
    grid_spec = pltpu.PrefetchScalarGridSpec(
        num_scalar_prefetch=1,
        grid=(windows // STEP_WINDOWS,),
        in_specs=[
            ON_CHIP,
            pl.BlockSpec((LANES, LANES), lambda i, p: (0, 0)),
            pl.BlockSpec(w_enc1.shape, lambda i, p: (0, 0)),
        ],
        out_specs=[
            ON_CHIP,
            ON_CHIP,
            pl.BlockSpec((cols, windows, 2 * channels), lambda i, p: (0, 0, 0)),
        ],
        scratch_shapes=[
            pltpu.VMEM((LANES, LANES), F32),
            pltpu.VMEM((windows, 2 * channels), F32),
        ],
    )
    return pl.pallas_call(
        functools.partial(enc1_kernel, chunks=chunks, quarter=quarter, cols=cols, copies=cols),
        grid_spec=grid_spec,
        out_shape=[
            pltpu.VMEM((4, windows * quarter, bins), BF16),
            pltpu.VMEM((2, windows * quarter, channels), F32),
            jax.ShapeDtypeStruct((cols, windows, 2 * channels), F32),
        ],
        compiler_params=pltpu.CompilerParams(vmem_limit_bytes=16 * MIB),
        name="normalize_enc1",
    )(permutation, on_chip(logs), coef, w_enc1)


def window_rows(perm_ref, table, step, windows, quarter, all_windows, cols, first, last):
    parts = []
    for w in range(windows):
        place = group_rank(perm_ref, step * windows + w, all_windows, cols)
        parts.append(jnp.broadcast_to(table[pl.ds(place, 1), first:last], (quarter, last - first)))
    return jnp.concatenate(parts, axis=0)


def write_halves(core_ref, grads, own_ref, send_ref):
    half = own_ref.shape[0]
    own_ref[...] = grads[pl.ds(pl.multiple_of(core_ref[0] * half, half), half), :]
    send_ref[...] = grads[pl.ds(pl.multiple_of((1 - core_ref[0]) * half, half), half), :]


def middle_kernel(perm_ref, core_ref, normed_ref, pre_ref, stat_ref, v_ref, b_ref, c_ref,
                  own_ref, send_ref, back_ref, moment_ref, sums_ref,
                  grads, moment, sums, *, quarter, cols, total_windows):
    step = pl.program_id(0)
    channels = v_ref.shape[1]
    bins = normed_ref.shape[2]
    windows = STEP_WINDOWS
    normed_ref, pre_ref, back_ref = (step_rows(ref, windows * quarter) for ref in (normed_ref, pre_ref, back_ref))
    all_windows = windows * pl.num_programs(0)
    ch = channels

    @pl.when(step == 0)
    def _():
        means = stat_ref[:, :, 0:ch]
        mean = jnp.mean(means, axis=0)
        diff = means - mean[None]
        variance = jnp.mean(stat_ref[:, :, ch:2 * ch] + diff * diff, axis=0)
        moment[:, 0:ch] = mean
        moment[:, ch:2 * ch] = lax.rsqrt(variance + EPS)
        moment_ref[...] = moment[...]
        grads[...] = jnp.zeros_like(grads)

    mean = window_rows(perm_ref, moment, step, windows, quarter, all_windows, cols, 0, ch)
    inverse = window_rows(perm_ref, moment, step, windows, quarter, all_windows, cols, ch, 2 * ch)
    hat_e = (pre_ref[0] - mean) * inverse
    hat_o = (pre_ref[1] - mean) * inverse
    a_e = (hat_e * sigmoid(hat_e)).astype(BF16)
    a_o = (hat_o * sigmoid(hat_o)).astype(BF16)
    v0, v1, v2, v3 = (v_ref[k * ch:(k + 1) * ch, :] for k in range(4))
    pre2 = shift_down(dot(a_o, v0), quarter) + dot(a_e, v1) + dot(a_o, v2) + shift_up(dot(a_e, v3), quarter)
    gate2 = sigmoid(pre2)
    h32 = (pre2 * gate2).astype(BF16).astype(F32)
    h = h32.astype(BF16)
    b0, b1, b2, b3 = (b_ref[:, k * ch:(k + 1) * ch] for k in range(4))
    d1_e = dot(h, b1) + shift_down(dot(h, b3), quarter)
    d1_o = dot(h, b2) + shift_up(dot(h, b0), quarter)
    gate_e = sigmoid(d1_e)
    gate_o = sigmoid(d1_o)
    de32 = (d1_e * gate_e)
    do32 = (d1_o * gate_o)
    de = de32.astype(BF16)
    do = do32.astype(BF16)
    de_up = shift_up(de32, quarter).astype(BF16)
    do_down = shift_down(do32, quarter).astype(BF16)
    c0, c1, c2, c3 = (c_ref[:, k * bins:(k + 1) * bins] for k in range(4))

    def delta(rebuilt, i):
        return ((rebuilt - normed_ref[i].astype(F32)) / total_windows).astype(BF16)

    g0 = delta(dot(de, c1) + dot(do_down, c3), 0)
    g1 = delta(dot(de, c2) + dot(do, c0), 1)
    g2 = delta(dot(do, c1) + dot(de, c3), 2)
    g3 = delta(dot(do, c2) + dot(de_up, c0), 3)
    halves = bins // ch
    base_b = 4 * bins
    base_v = base_b + 4 * ch

    def add_c(k, value):
        for j in range(halves):
            at = (k * halves + j) * ch
            grads[at:at + ch, :] += value[:, j * ch:(j + 1) * ch]

    add_c(0, dot_tn(de_up, g3) + dot_tn(do, g1))
    add_c(1, dot_tn(de, g0) + dot_tn(do, g2))
    add_c(2, dot_tn(de, g1) + dot_tn(do, g3))
    add_c(3, dot_tn(de, g2) + dot_tn(do_down, g0))
    back_e = shift_down(dot_nt(g3, c0), quarter) + dot_nt(g0, c1) + dot_nt(g1, c2) + dot_nt(g2, c3)
    back_o = dot_nt(g1, c0) + dot_nt(g2, c1) + dot_nt(g3, c2) + shift_up(dot_nt(g0, c3), quarter)
    dd_e = (back_e * (gate_e * (1.0 + d1_e * (1.0 - gate_e)))).astype(BF16)
    dd_o = (back_o * (gate_o * (1.0 + d1_o * (1.0 - gate_o)))).astype(BF16)
    h_up = shift_up(h32, quarter).astype(BF16)
    h_down = shift_down(h32, quarter).astype(BF16)
    grads[base_b:base_b + ch, :] += dot_tn(h_up, dd_o)
    grads[base_b + ch:base_b + 2 * ch, :] += dot_tn(h, dd_e)
    grads[base_b + 2 * ch:base_b + 3 * ch, :] += dot_tn(h, dd_o)
    grads[base_b + 3 * ch:base_b + 4 * ch, :] += dot_tn(h_down, dd_e)
    back2 = shift_down(dot_nt(dd_o, b0), quarter) + dot_nt(dd_e, b1) + dot_nt(dd_o, b2) + shift_up(dot_nt(dd_e, b3), quarter)
    d2_32 = (back2 * (gate2 * (1.0 + pre2 * (1.0 - gate2)))).astype(BF16).astype(F32)
    d2 = d2_32.astype(BF16)
    d2_up = shift_up(d2_32, quarter).astype(BF16)
    d2_down = shift_down(d2_32, quarter).astype(BF16)
    grads[base_v:base_v + ch, :] += dot_tn(a_o, d2_up)
    grads[base_v + ch:base_v + 2 * ch, :] += dot_tn(a_e, d2)
    grads[base_v + 2 * ch:base_v + 3 * ch, :] += dot_tn(a_o, d2)
    grads[base_v + 3 * ch:base_v + 4 * ch, :] += dot_tn(a_e, d2_down)
    fold_e = dot_nt(d2, v1) + shift_down(dot_nt(d2, v3), quarter)
    fold_o = dot_nt(d2, v2) + shift_up(dot_nt(d2, v0), quarter)
    gate_he = sigmoid(hat_e)
    gate_ho = sigmoid(hat_o)
    fold_e = fold_e * (gate_he * (1.0 + hat_e * (1.0 - gate_he)))
    fold_o = fold_o * (gate_ho * (1.0 + hat_o * (1.0 - gate_ho)))
    back_ref[0] = fold_e
    back_ref[1] = fold_o
    cross_e = fold_e * hat_e
    cross_o = fold_o * hat_o
    for w in range(windows):
        low, high = w * quarter, (w + 1) * quarter
        first = jnp.sum(fold_e[low:high] + fold_o[low:high], axis=0, keepdims=True)
        second = jnp.sum(cross_e[low:high] + cross_o[low:high], axis=0, keepdims=True)
        place = group_rank(perm_ref, step * windows + w, all_windows, cols)
        sums[pl.ds(place, 1), 0:ch] = first
        sums[pl.ds(place, 1), ch:2 * ch] = second

    @pl.when(step == pl.num_programs(0) - 1)
    def _():
        for d in range(cols):
            sums_ref[d] = sums[...]
        write_halves(core_ref, grads, own_ref, send_ref)


def middle_call(permutation, core, normed, pre, stat, w_enc2, w_dec1, w_dec2, quarter, cols, total_windows):
    bins = normed.shape[2]
    channels = w_enc2.shape[1]
    windows = normed.shape[1] // quarter
    total = 4 * bins + 8 * channels
    whole2 = lambda i, p, c: (0, 0)
    whole3 = lambda i, p, c: (0, 0, 0)
    grid_spec = pltpu.PrefetchScalarGridSpec(
        num_scalar_prefetch=2,
        grid=(windows // STEP_WINDOWS,),
        in_specs=[
            ON_CHIP,
            ON_CHIP,
            pl.BlockSpec(stat.shape, whole3),
            pl.BlockSpec(w_enc2.shape, whole2),
            pl.BlockSpec(w_dec1.shape, whole2),
            pl.BlockSpec(w_dec2.shape, whole2),
        ],
        out_specs=[
            pl.BlockSpec((total // 2, channels), whole2),
            pl.BlockSpec((total // 2, channels), whole2),
            ON_CHIP,
            pl.BlockSpec((windows, 2 * channels), whole2),
            pl.BlockSpec(stat.shape, whole3),
        ],
        scratch_shapes=[
            pltpu.VMEM((total, channels), F32),
            pltpu.VMEM((windows, 2 * channels), F32),
            pltpu.VMEM((windows, 2 * channels), F32),
        ],
    )
    return pl.pallas_call(
        functools.partial(middle_kernel, quarter=quarter, cols=cols, total_windows=float(total_windows)),
        grid_spec=grid_spec,
        out_shape=[
            jax.ShapeDtypeStruct((total // 2, channels), F32),
            jax.ShapeDtypeStruct((total // 2, channels), F32),
            pltpu.VMEM(pre.shape, F32),
            jax.ShapeDtypeStruct((windows, 2 * channels), F32),
            jax.ShapeDtypeStruct(stat.shape, F32),
        ],
        compiler_params=pltpu.CompilerParams(vmem_limit_bytes=36 * MIB),
        name="middle",
    )(permutation, core, on_chip(normed), on_chip(pre), stat, w_enc2, w_dec1, w_dec2)


def grad_kernel(perm_ref, core_ref, normed_ref, pre_ref, back_ref, moment_ref, sums_ref, own_ref, send_ref, grads, scale, *, quarter, cols):
    step = pl.program_id(0)
    bins = normed_ref.shape[2]
    ch = pre_ref.shape[2]
    windows = STEP_WINDOWS
    rows = windows * quarter
    normed_ref = step_rows(normed_ref, rows)
    pre_ref, back_ref = step_rows(pre_ref, rows), step_rows(back_ref, rows)
    all_windows = windows * pl.num_programs(0)

    @pl.when(step == 0)
    def _():
        scale[...] = jnp.sum(sums_ref[...], axis=0) / (2.0 * quarter * cols)
        grads[...] = jnp.zeros_like(grads)

    pick = functools.partial(window_rows, perm_ref, step=step, windows=windows, quarter=quarter, all_windows=all_windows, cols=cols)
    mean = pick(table=moment_ref, first=0, last=ch)
    inverse = pick(table=moment_ref, first=ch, last=2 * ch)
    first = pick(table=scale, first=0, last=ch)
    second = pick(table=scale, first=ch, last=2 * ch)
    hat_e = (pre_ref[0] - mean) * inverse
    hat_o = (pre_ref[1] - mean) * inverse
    de32 = (back_ref[0] - first - hat_e * second) * inverse
    do32 = (back_ref[1] - first - hat_o * second) * inverse
    de = de32.astype(BF16)
    do = do32.astype(BF16)
    de_up = shift_up(de32, quarter).astype(BF16)
    do_down = shift_down(do32, quarter).astype(BF16)
    f0, f1, f2, f3 = (normed_ref[i] for i in range(4))
    grads[0:bins, :] += dot_tn(f3, de_up) + dot_tn(f1, do)
    grads[bins:2 * bins, :] += dot_tn(f0, de) + dot_tn(f2, do)
    grads[2 * bins:3 * bins, :] += dot_tn(f1, de) + dot_tn(f3, do)
    grads[3 * bins:4 * bins, :] += dot_tn(f2, de) + dot_tn(f0, do_down)

    @pl.when(step == pl.num_programs(0) - 1)
    def _():
        write_halves(core_ref, grads, own_ref, send_ref)


def grad_call(permutation, core, normed, pre, back, moment, sums, quarter, cols):
    bins = normed.shape[2]
    channels = pre.shape[2]
    windows = normed.shape[1] // quarter
    grid_spec = pltpu.PrefetchScalarGridSpec(
        num_scalar_prefetch=2,
        grid=(windows // STEP_WINDOWS,),
        in_specs=[
            ON_CHIP,
            ON_CHIP,
            ON_CHIP,
            pl.BlockSpec(moment.shape, lambda i, p, c: (0, 0)),
            pl.BlockSpec(sums.shape, lambda i, p, c: (0, 0, 0)),
        ],
        out_specs=[pl.BlockSpec((2 * bins, channels), lambda i, p, c: (0, 0))] * 2,
        scratch_shapes=[pltpu.VMEM((4 * bins, channels), F32), pltpu.VMEM((windows, 2 * channels), F32)],
    )
    return pl.pallas_call(
        functools.partial(grad_kernel, quarter=quarter, cols=cols),
        grid_spec=grid_spec,
        out_shape=[jax.ShapeDtypeStruct((2 * bins, channels), F32)] * 2,
        compiler_params=pltpu.CompilerParams(vmem_limit_bytes=16 * MIB),
        name="grad_enc1",
    )(permutation, core, on_chip(normed), on_chip(pre), on_chip(back), moment, sums)


def swap_cores(values):
    return lax.ppermute(values, "core", [(0, 1), (1, 0)])


def exchange(values, axes):
    return lax.all_to_all(values, axes, split_axis=0, concat_axis=0, tiled=True)


def chip_sums(parts, axes, chips):
    total = [(own + swap_cores(send)).astype(BF16).reshape(chips, -1, own.shape[1]) for own, send in parts]
    total = jnp.concatenate(total, axis=1)
    return exchange(total.reshape(-1, total.shape[2]), axes).reshape(total.shape)


def owner_kernel(in_ref, out_ref):
    chips, rows, width = in_ref.shape

    def body(i, total):
        return total + in_ref[i].astype(F32)

    total = lax.fori_loop(0, chips, body, jnp.zeros((rows, width), F32), unroll=4)
    largest = jnp.max(jnp.max(jnp.abs(total), axis=0, keepdims=True), axis=1, keepdims=True)
    exponent = jnp.clip(jnp.ceil(jnp.log2(largest)), -110.0, 126.0)
    out_ref[0:rows, :] = total * jnp.exp2(14.0 - exponent)
    out_ref[rows:, :] = jnp.broadcast_to(exponent, (SCALE_ROWS, width))


def owner_call(pieces):
    chips, rows, width = pieces.shape
    return pl.pallas_call(
        owner_kernel,
        out_shape=jax.ShapeDtypeStruct((rows + SCALE_ROWS, width), F32),
        compiler_params=pltpu.CompilerParams(vmem_limit_bytes=6 * MIB),
        name="owner_sum",
    )(pieces)


def gather_rows(piece, axes, chips):
    rows, width = piece.shape
    copies = jnp.broadcast_to(piece.astype(jnp.float16)[None], (chips, rows, width))
    return exchange(copies.reshape(-1, width), axes).reshape(chips, rows, width)


def place_kernel(core_ref, mine_ref, other_ref, grad_w_ref, grad_v_ref, grad_b_ref, grad_c_ref, *, cut):
    step = pl.program_id(0)
    half = pl.num_programs(0) // 2
    total = mine_ref.shape[1]
    rows = total - SCALE_ROWS
    first = core_ref[0] == 0
    for i in range(mine_ref.shape[0]):
        mine, other = mine_ref[i], other_ref[i]
        low = jnp.where(first, mine, other)
        high = jnp.where(first, other, mine)
        low = low[0:rows] * jnp.exp2(low[rows:rows + 1] - 14.0)
        high = high[0:rows] * jnp.exp2(high[rows:rows + 1] - 14.0)
        early, late = i * cut, i * (rows - cut)
        grad_c_ref[early:early + cut, :] = low[0:cut]
        grad_w_ref[0, late:late + rows - cut, :] = low[cut:rows]
        grad_w_ref[1, late:late + rows - cut, :] = high[cut:rows]

        @pl.when(step < half)
        def _():
            grad_b_ref[early:early + cut, :] = high[0:cut]

        @pl.when(step >= half)
        def _():
            grad_v_ref[early:early + cut, :] = high[0:cut]


def place_call(core, mine, other, cut, channels, bins):
    chips, total, width = mine.shape
    late = total - SCALE_ROWS - cut
    group = channels // cut
    steps = chips // group
    grid_spec = pltpu.PrefetchScalarGridSpec(
        num_scalar_prefetch=1,
        grid=(steps,),
        in_specs=[pl.BlockSpec((group, total, width), lambda i, c: (i, 0, 0))] * 2,
        out_specs=[
            pl.BlockSpec((2, group * late, width), lambda i, c: (0, i, 0)),
            pl.BlockSpec((channels, width), lambda i, c: (jnp.maximum(i - steps // 2, 0), 0)),
            pl.BlockSpec((channels, width), lambda i, c: (0, jnp.minimum(i, steps // 2 - 1))),
            pl.BlockSpec((channels, width), lambda i, c: (0, i)),
        ],
    )
    return pl.pallas_call(
        functools.partial(place_kernel, cut=cut),
        grid_spec=grid_spec,
        out_shape=[
            jax.ShapeDtypeStruct((2, chips * late, width), F32),
            jax.ShapeDtypeStruct((4 * channels, channels), F32),
            jax.ShapeDtypeStruct((channels, 4 * channels), F32),
            jax.ShapeDtypeStruct((channels, 4 * bins), F32),
        ],
        compiler_params=pltpu.CompilerParams(vmem_limit_bytes=12 * MIB),
        name="place_gradients",
    )(core, mine, other)


def local(spectra, sensor_ids, permutation, w_enc1, w_enc2, w_dec1, w_dec2):
    windows, frames, bins = spectra.shape
    channels = w_enc1.shape[1]
    col_axes = ("pair", "core")
    chip_axes = ("row", "pair")
    every = ("row", "pair", "core")
    cols = lax.axis_size("pair") * lax.axis_size("core")
    chips = lax.axis_size("row") * lax.axis_size("pair")
    total_windows = windows * lax.axis_size("row") * cols
    sensors = total_windows // WIN_SENSOR
    chunks = bins // LANES
    quarter = frames // 4
    core_index = lax.axis_index("core")
    core = core_index.astype(jnp.int32).reshape(1)

    logs, sums = sums_call(spectra, sensor_ids)
    sums, core = lax.optimization_barrier((sums, core))
    sums = exchange(sums, every)
    coef = exchange(stats_call(sums, windows, chunks, sensors, WIN_SENSOR * frames), every)
    normed, pre, stat = enc1_call(permutation, logs, coef, w_enc1, quarter, cols)
    stat = exchange(stat.reshape(cols * windows, 2 * channels), col_axes).reshape(cols, windows, 2 * channels)
    own, send, back, moment, moments = middle_call(
        permutation, core, normed, pre, stat, w_enc2, w_dec1, w_dec2, quarter, cols, total_windows)
    moments = exchange(moments.reshape(cols * windows, 2 * channels), col_axes).reshape(cols, windows, 2 * channels)
    late = grad_call(permutation, core, normed, pre, back, moment, moments, quarter, cols)
    piece = owner_call(chip_sums([(own, send), late], chip_axes, chips))
    mine = gather_rows(piece, chip_axes, chips)
    other = swap_cores(mine)
    grad_w, grad_v, grad_b, grad_c = place_call(
        core, mine.astype(F32), other.astype(F32), own.shape[0] // chips, channels, bins)
    return (grad_w.reshape(4 * bins, channels), grad_v, grad_b, grad_c)


def solution(mesh):
    rows, cols = mesh.devices.shape
    inner = Mesh(mesh.devices.reshape(rows, cols // 2, 2), ("row", "pair", "core"))
    spread = ("row", "pair", "core")
    return jax.shard_map(
        local,
        mesh=inner,
        in_specs=(P(spread, None, None), P(spread, None), P(spread), P(), P(), P(), P()),
        out_specs=(P(), P(), P(), P()),
        check_vma=False,
    )
```

```python
import functools

import jax
import jax.numpy as jnp
from jax import lax
from jax.experimental import pallas as pl
from jax.experimental.pallas import tpu as pltpu
from jax.sharding import Mesh, PartitionSpec as P

WIN_SENSOR = 8
EPS = 1e-05
F32 = jnp.float32
BF16 = jnp.bfloat16
LANES = 128
STEP_WINDOWS = 8
SORT_WINDOWS = 4
SCALE_ROWS = 8
MIB = 1024 * 1024


ON_CHIP = pl.BlockSpec(memory_space=pltpu.VMEM)


def on_chip(values):
    return pltpu.with_memory_space_constraint(values, pltpu.VMEM)


def in_hbm(values):
    return pltpu.with_memory_space_constraint(values, pltpu.HBM)


def step_rows(ref, rows):
    return ref.at[:, pl.ds(pl.multiple_of(pl.program_id(0) * rows, rows), rows), :]


def dot(left, right):
    return jnp.dot(left, right, preferred_element_type=F32)


def dot_nt(left, right):
    return lax.dot_general(left, right, (((1,), (1,)), ((), ())), preferred_element_type=F32)


def dot_tn(left, right):
    return lax.dot_general(left, right, (((0,), (0,)), ((), ())), preferred_element_type=F32)


def split3(values):
    first = values.astype(BF16)
    rest = values - first.astype(F32)
    second = rest.astype(BF16)
    third = (rest - second.astype(F32)).astype(BF16)
    return first, second, third


def sigmoid(values):
    return 1.0 / (1.0 + jnp.exp(-values))


def shift_down(values, period):
    rows = lax.broadcasted_iota(jnp.int32, values.shape, 0) % period
    return jnp.where(rows == 0, 0.0, pltpu.roll(values, 1, 0))


def shift_up(values, period):
    total = values.shape[0]
    rows = lax.broadcasted_iota(jnp.int32, values.shape, 0) % period
    return jnp.where(rows == period - 1, 0.0, pltpu.roll(values, total - 1, 0))


def group_rank(perm_ref, window, window_dev, col_count):
    trainer = perm_ref[window] // window_dev
    per_row = 2
    return (trainer // col_count) * per_row + trainer % per_row


def sums_kernel(ids_ref, spec_ref, log_ref, out_ref, acc, lane, *, chunks, count):
    step = pl.program_id(0)
    windows, frames, bins = spec_ref.shape
    quarter = frames // 4
    rows = 16
    log_ref = step_rows(log_ref, windows * quarter)

    for w in range(windows):
        def body(i, carry):
            total, square = carry
            start = pl.multiple_of(i * rows, rows)
            value = jnp.log(1.0 + spec_ref[w, pl.ds(start, rows), :].astype(F32))
            for k in range(chunks):
                lane[w % 2, k, pl.ds(start, rows), :] = value[:, k * LANES:(k + 1) * LANES]
            value_sq = value * value
            return (total + value[0:8] + value[8:16], square + value_sq[0:8] + value_sq[8:16])

        zero = jnp.zeros((8, bins), F32)
        total, square = lax.fori_loop(0, frames // rows, body, (zero, zero), unroll=4)
        total = jnp.sum(total, axis=0, keepdims=True)
        square = jnp.sum(square, axis=0, keepdims=True)
        pieces = [total[:, k * LANES:(k + 1) * LANES] for k in range(chunks)]
        pieces += [square[:, k * LANES:(k + 1) * LANES] for k in range(chunks)]
        start = pl.multiple_of((step * windows + w) * 2 * chunks, 2 * chunks)
        acc[pl.ds(start, 2 * chunks), :] = jnp.concatenate(pieces, axis=0)
        for i in range(4):
            for k in range(chunks):
                log_ref[i, w * quarter:(w + 1) * quarter, k * LANES:(k + 1) * LANES] = lane[w % 2, k, pl.ds(i, quarter, stride=4), :]

    @pl.when(step == pl.num_programs(0) - 1)
    def _():
        acc[LANES:2 * LANES, :] = jnp.zeros((LANES, LANES), F32)
        for w in range(count):
            acc[LANES + w:LANES + w + 1, :] = jnp.full((1, LANES), ids_ref[w], jnp.int32).astype(F32)
        out_ref[pl.ds(0, LANES, stride=2), :] = acc[0:LANES, :].T
        out_ref[pl.ds(1, LANES, stride=2), :] = acc[LANES:2 * LANES, :].T


def sums_call(spectra, sensor_ids):
    windows, frames, bins = spectra.shape
    chunks = bins // LANES
    grid_spec = pltpu.PrefetchScalarGridSpec(
        num_scalar_prefetch=1,
        grid=(windows // SORT_WINDOWS,),
        in_specs=[pl.BlockSpec((SORT_WINDOWS, frames, bins), lambda i, s: (i, 0, 0))],
        out_specs=[ON_CHIP, pl.BlockSpec((2 * LANES, LANES), lambda i, s: (0, 0))],
        scratch_shapes=[pltpu.VMEM((2 * LANES, LANES), F32), pltpu.VMEM((2, chunks, frames, LANES), F32)],
    )
    return pl.pallas_call(
        functools.partial(sums_kernel, chunks=chunks, count=windows),
        grid_spec=grid_spec,
        out_shape=[
            pltpu.VMEM((4, windows * frames // 4, bins), F32),
            jax.ShapeDtypeStruct((2 * LANES, LANES), F32),
        ],
        compiler_params=pltpu.CompilerParams(vmem_limit_bytes=10 * MIB),
        name="sort_and_sum",
    )(in_hbm(sensor_ids.reshape(windows)), in_hbm(spectra))


def stats_kernel(in_ref, out_ref, *, windows, chunks, sensors, per_sensor):
    width = 2 * chunks
    data = in_ref[pl.ds(0, LANES, stride=2), :].T
    labels = in_ref[pl.ds(1, LANES, stride=2), :].T
    sensor_rows = lax.broadcasted_iota(jnp.int32, (sensors, LANES), 0).astype(F32)
    tables = [(sensor_rows == labels[w:w + 1, :]).astype(F32).astype(BF16) for w in range(windows)]
    table = jnp.concatenate(tables, axis=1)
    values = jnp.concatenate([data[w * width:(w + 1) * width, :] for w in range(windows)], axis=1)
    parts = dot_nt(jnp.concatenate(split3(values), axis=0), table)
    sums = parts[0:width] + parts[width:2 * width] + parts[2 * width:3 * width]
    center = sums[0:chunks] / per_sensor
    factor = lax.rsqrt(sums[chunks:width] / per_sensor - center * center + EPS)
    both = jnp.concatenate([center, factor], axis=0)
    back = dot(jnp.concatenate(split3(both), axis=0), table)
    back = back[0:width] + back[width:2 * width] + back[2 * width:3 * width]
    rows = jnp.concatenate([back[:, w * LANES:(w + 1) * LANES] for w in range(windows)], axis=0)
    out_ref[...] = rows.T


def stats_call(received, windows, chunks, sensors, per_sensor):
    return pl.pallas_call(
        functools.partial(stats_kernel, windows=windows, chunks=chunks, sensors=sensors, per_sensor=float(per_sensor)),
        out_shape=jax.ShapeDtypeStruct((LANES, LANES), F32),
        compiler_params=pltpu.CompilerParams(vmem_limit_bytes=12 * MIB),
        name="sensor_stats",
    )(received)


def enc1_kernel(perm_ref, log_ref, coef_ref, w_ref, normed_ref, pre_ref, stat_ref, coef, stat, *, chunks, quarter, cols, copies):
    step = pl.program_id(0)
    bins = log_ref.shape[2]
    windows = STEP_WINDOWS
    log_ref, normed_ref, pre_ref = (step_rows(ref, windows * quarter) for ref in (log_ref, normed_ref, pre_ref))
    channels = w_ref.shape[1]
    all_windows = windows * pl.num_programs(0)
    width = 2 * chunks

    @pl.when(step == 0)
    def _():
        coef[...] = coef_ref[...].T

    for w in range(windows):
        start = pl.multiple_of((step * windows + w) * width, width)
        both = coef[pl.ds(start, width), :]
        low, high = w * quarter, (w + 1) * quarter
        for k in range(chunks):
            left, right = k * LANES, (k + 1) * LANES
            center = both[k:k + 1, :]
            factor = both[chunks + k:chunks + k + 1, :]
            for i in range(4):
                normed_ref[i, low:high, left:right] = ((log_ref[i, low:high, left:right] - center) * factor).astype(BF16)

    w0, w1, w2, w3 = (w_ref[k * bins:(k + 1) * bins, :] for k in range(4))
    f0, f1, f2, f3 = (normed_ref[i] for i in range(4))
    even = shift_down(dot(f3, w0), quarter) + dot(f0, w1) + dot(f1, w2) + dot(f2, w3)
    odd = dot(f1, w0) + dot(f2, w1) + dot(f3, w2) + shift_up(dot(f0, w3), quarter)
    pre_ref[0] = even
    pre_ref[1] = odd
    for w in range(windows):
        part_e = even[w * quarter:(w + 1) * quarter]
        part_o = odd[w * quarter:(w + 1) * quarter]
        mean = (jnp.sum(part_e, axis=0, keepdims=True) + jnp.sum(part_o, axis=0, keepdims=True)) / (2 * quarter)
        diff_e = part_e - mean
        diff_o = part_o - mean
        spread = (jnp.sum(diff_e * diff_e, axis=0, keepdims=True) + jnp.sum(diff_o * diff_o, axis=0, keepdims=True)) / (2 * quarter)
        place = group_rank(perm_ref, step * windows + w, all_windows, cols)
        stat[pl.ds(place, 1), 0:channels] = mean
        stat[pl.ds(place, 1), channels:2 * channels] = spread

    @pl.when(step == pl.num_programs(0) - 1)
    def _():
        for d in range(copies):
            stat_ref[d] = stat[...]


def enc1_call(permutation, logs, coef, w_enc1, quarter, cols):
    bins = logs.shape[2]
    windows = logs.shape[1] // quarter
    chunks = bins // LANES
    channels = w_enc1.shape[1]
    grid_spec = pltpu.PrefetchScalarGridSpec(
        num_scalar_prefetch=1,
        grid=(windows // STEP_WINDOWS,),
        in_specs=[
            ON_CHIP,
            pl.BlockSpec((LANES, LANES), lambda i, p: (0, 0)),
            ON_CHIP,
        ],
        out_specs=[
            ON_CHIP,
            ON_CHIP,
            pl.BlockSpec((cols, windows, 2 * channels), lambda i, p: (0, 0, 0)),
        ],
        scratch_shapes=[
            pltpu.VMEM((LANES, LANES), F32),
            pltpu.VMEM((windows, 2 * channels), F32),
        ],
    )
    return pl.pallas_call(
        functools.partial(enc1_kernel, chunks=chunks, quarter=quarter, cols=cols, copies=cols),
        grid_spec=grid_spec,
        out_shape=[
            pltpu.VMEM((4, windows * quarter, bins), BF16),
            pltpu.VMEM((2, windows * quarter, channels), F32),
            jax.ShapeDtypeStruct((cols, windows, 2 * channels), F32),
        ],
        compiler_params=pltpu.CompilerParams(vmem_limit_bytes=16 * MIB),
        name="normalize_enc1",
    )(permutation, on_chip(logs), coef, on_chip(w_enc1))


def window_rows(perm_ref, table, step, windows, quarter, all_windows, cols, first, last):
    parts = []
    for w in range(windows):
        place = group_rank(perm_ref, step * windows + w, all_windows, cols)
        parts.append(jnp.broadcast_to(table[pl.ds(place, 1), first:last], (quarter, last - first)))
    return jnp.concatenate(parts, axis=0)


def write_halves(core_ref, grads, own_ref, send_ref, bounds):
    for first, last in zip(bounds[:-1], bounds[1:]):
        half = (last - first) // 2
        at = first // 2
        own = pl.multiple_of(first + core_ref[0] * half, half)
        send = pl.multiple_of(first + (1 - core_ref[0]) * half, half)
        own_ref[at:at + half, :] = grads[pl.ds(own, half), :]
        send_ref[at:at + half, :] = grads[pl.ds(send, half), :]


def middle_kernel(perm_ref, core_ref, normed_ref, pre_ref, stat_ref, v_ref, b_ref, c_ref,
                  own_ref, send_ref, back_ref, moment_ref, sums_ref,
                  grads, moment, sums, *, quarter, cols, total_windows):
    step = pl.program_id(0)
    channels = v_ref.shape[1]
    bins = normed_ref.shape[2]
    windows = STEP_WINDOWS
    normed_ref, pre_ref, back_ref = (step_rows(ref, windows * quarter) for ref in (normed_ref, pre_ref, back_ref))
    all_windows = windows * pl.num_programs(0)
    ch = channels

    @pl.when(step == 0)
    def _():
        means = stat_ref[:, :, 0:ch]
        mean = jnp.mean(means, axis=0)
        diff = means - mean[None]
        variance = jnp.mean(stat_ref[:, :, ch:2 * ch] + diff * diff, axis=0)
        moment[:, 0:ch] = mean
        moment[:, ch:2 * ch] = lax.rsqrt(variance + EPS)
        moment_ref[...] = moment[...]
        grads[...] = jnp.zeros_like(grads)

    mean = window_rows(perm_ref, moment, step, windows, quarter, all_windows, cols, 0, ch)
    inverse = window_rows(perm_ref, moment, step, windows, quarter, all_windows, cols, ch, 2 * ch)
    hat_e = (pre_ref[0] - mean) * inverse
    hat_o = (pre_ref[1] - mean) * inverse
    a_e = (hat_e * sigmoid(hat_e)).astype(BF16)
    a_o = (hat_o * sigmoid(hat_o)).astype(BF16)
    v0, v1, v2, v3 = (v_ref[k * ch:(k + 1) * ch, :] for k in range(4))
    pre2 = shift_down(dot(a_o, v0), quarter) + dot(a_e, v1) + dot(a_o, v2) + shift_up(dot(a_e, v3), quarter)
    gate2 = sigmoid(pre2)
    h32 = (pre2 * gate2).astype(BF16).astype(F32)
    h = h32.astype(BF16)
    b0, b1, b2, b3 = (b_ref[:, k * ch:(k + 1) * ch] for k in range(4))
    d1_e = dot(h, b1) + shift_down(dot(h, b3), quarter)
    d1_o = dot(h, b2) + shift_up(dot(h, b0), quarter)
    gate_e = sigmoid(d1_e)
    gate_o = sigmoid(d1_o)
    de32 = (d1_e * gate_e)
    do32 = (d1_o * gate_o)
    de = de32.astype(BF16)
    do = do32.astype(BF16)
    de_up = shift_up(de32, quarter).astype(BF16)
    do_down = shift_down(do32, quarter).astype(BF16)
    c0, c1, c2, c3 = (c_ref[:, k * bins:(k + 1) * bins] for k in range(4))

    def delta(rebuilt, i):
        return ((rebuilt - normed_ref[i].astype(F32)) / total_windows).astype(BF16)

    g0 = delta(dot(de, c1) + dot(do_down, c3), 0)
    g1 = delta(dot(de, c2) + dot(do, c0), 1)
    g2 = delta(dot(do, c1) + dot(de, c3), 2)
    g3 = delta(dot(do, c2) + dot(de_up, c0), 3)
    halves = bins // ch
    base_b = 4 * bins
    base_v = base_b + 4 * ch

    def add_c(k, value):
        for j in range(halves):
            at = (k * halves + j) * ch
            grads[at:at + ch, :] += value[:, j * ch:(j + 1) * ch]

    add_c(0, dot_tn(de_up, g3) + dot_tn(do, g1))
    add_c(1, dot_tn(de, g0) + dot_tn(do, g2))
    add_c(2, dot_tn(de, g1) + dot_tn(do, g3))
    add_c(3, dot_tn(de, g2) + dot_tn(do_down, g0))
    back_e = shift_down(dot_nt(g3, c0), quarter) + dot_nt(g0, c1) + dot_nt(g1, c2) + dot_nt(g2, c3)
    back_o = dot_nt(g1, c0) + dot_nt(g2, c1) + dot_nt(g3, c2) + shift_up(dot_nt(g0, c3), quarter)
    dd_e = (back_e * (gate_e * (1.0 + d1_e * (1.0 - gate_e)))).astype(BF16)
    dd_o = (back_o * (gate_o * (1.0 + d1_o * (1.0 - gate_o)))).astype(BF16)
    h_up = shift_up(h32, quarter).astype(BF16)
    h_down = shift_down(h32, quarter).astype(BF16)
    grads[base_b:base_b + ch, :] += dot_tn(h_up, dd_o)
    grads[base_b + ch:base_b + 2 * ch, :] += dot_tn(h, dd_e)
    grads[base_b + 2 * ch:base_b + 3 * ch, :] += dot_tn(h, dd_o)
    grads[base_b + 3 * ch:base_b + 4 * ch, :] += dot_tn(h_down, dd_e)
    back2 = shift_down(dot_nt(dd_o, b0), quarter) + dot_nt(dd_e, b1) + dot_nt(dd_o, b2) + shift_up(dot_nt(dd_e, b3), quarter)
    d2_32 = (back2 * (gate2 * (1.0 + pre2 * (1.0 - gate2)))).astype(BF16).astype(F32)
    d2 = d2_32.astype(BF16)
    d2_up = shift_up(d2_32, quarter).astype(BF16)
    d2_down = shift_down(d2_32, quarter).astype(BF16)
    grads[base_v:base_v + ch, :] += dot_tn(a_o, d2_up)
    grads[base_v + ch:base_v + 2 * ch, :] += dot_tn(a_e, d2)
    grads[base_v + 2 * ch:base_v + 3 * ch, :] += dot_tn(a_o, d2)
    grads[base_v + 3 * ch:base_v + 4 * ch, :] += dot_tn(a_e, d2_down)
    fold_e = dot_nt(d2, v1) + shift_down(dot_nt(d2, v3), quarter)
    fold_o = dot_nt(d2, v2) + shift_up(dot_nt(d2, v0), quarter)
    gate_he = sigmoid(hat_e)
    gate_ho = sigmoid(hat_o)
    fold_e = fold_e * (gate_he * (1.0 + hat_e * (1.0 - gate_he)))
    fold_o = fold_o * (gate_ho * (1.0 + hat_o * (1.0 - gate_ho)))
    back_ref[0] = fold_e
    back_ref[1] = fold_o
    cross_e = fold_e * hat_e
    cross_o = fold_o * hat_o
    for w in range(windows):
        low, high = w * quarter, (w + 1) * quarter
        first = jnp.sum(fold_e[low:high] + fold_o[low:high], axis=0, keepdims=True)
        second = jnp.sum(cross_e[low:high] + cross_o[low:high], axis=0, keepdims=True)
        place = group_rank(perm_ref, step * windows + w, all_windows, cols)
        sums[pl.ds(place, 1), 0:ch] = first
        sums[pl.ds(place, 1), ch:2 * ch] = second

    @pl.when(step == pl.num_programs(0) - 1)
    def _():
        for d in range(cols):
            sums_ref[d] = sums[...]
        write_halves(core_ref, grads, own_ref, send_ref, (0, base_b, base_v, base_v + 4 * ch))


def middle_call(permutation, core, normed, pre, stat, w_enc2, w_dec1, w_dec2, quarter, cols, total_windows):
    bins = normed.shape[2]
    channels = w_enc2.shape[1]
    windows = normed.shape[1] // quarter
    total = 4 * bins + 8 * channels
    whole2 = lambda i, p, c: (0, 0)
    whole3 = lambda i, p, c: (0, 0, 0)
    grid_spec = pltpu.PrefetchScalarGridSpec(
        num_scalar_prefetch=2,
        grid=(windows // STEP_WINDOWS,),
        in_specs=[
            ON_CHIP,
            ON_CHIP,
            ON_CHIP,
            ON_CHIP,
            ON_CHIP,
            ON_CHIP,
        ],
        out_specs=[
            ON_CHIP,
            ON_CHIP,
            ON_CHIP,
            pl.BlockSpec((windows, 2 * channels), whole2),
            pl.BlockSpec(stat.shape, whole3),
        ],
        scratch_shapes=[
            pltpu.VMEM((total, channels), F32),
            pltpu.VMEM((windows, 2 * channels), F32),
            pltpu.VMEM((windows, 2 * channels), F32),
        ],
    )
    return pl.pallas_call(
        functools.partial(middle_kernel, quarter=quarter, cols=cols, total_windows=float(total_windows)),
        grid_spec=grid_spec,
        out_shape=[
            pltpu.VMEM((total // 2, channels), F32),
            pltpu.VMEM((total // 2, channels), F32),
            pltpu.VMEM(pre.shape, F32),
            jax.ShapeDtypeStruct((windows, 2 * channels), F32),
            jax.ShapeDtypeStruct(stat.shape, F32),
        ],
        compiler_params=pltpu.CompilerParams(vmem_limit_bytes=30 * MIB),
        name="middle",
    )(permutation, core, on_chip(normed), on_chip(pre), on_chip(stat), on_chip(w_enc2), on_chip(w_dec1), on_chip(w_dec2))


def grad_kernel(perm_ref, core_ref, normed_ref, pre_ref, back_ref, moment_ref, sums_ref, own_ref, send_ref, grads, scale, *, quarter, cols):
    step = pl.program_id(0)
    bins = normed_ref.shape[2]
    ch = pre_ref.shape[2]
    windows = STEP_WINDOWS
    rows = windows * quarter
    normed_ref = step_rows(normed_ref, rows)
    pre_ref, back_ref = step_rows(pre_ref, rows), step_rows(back_ref, rows)
    all_windows = windows * pl.num_programs(0)

    @pl.when(step == 0)
    def _():
        scale[...] = jnp.sum(sums_ref[...], axis=0) / (2.0 * quarter * cols)
        grads[...] = jnp.zeros_like(grads)

    pick = functools.partial(window_rows, perm_ref, step=step, windows=windows, quarter=quarter, all_windows=all_windows, cols=cols)
    mean = pick(table=moment_ref, first=0, last=ch)
    inverse = pick(table=moment_ref, first=ch, last=2 * ch)
    first = pick(table=scale, first=0, last=ch)
    second = pick(table=scale, first=ch, last=2 * ch)
    hat_e = (pre_ref[0] - mean) * inverse
    hat_o = (pre_ref[1] - mean) * inverse
    de32 = (back_ref[0] - first - hat_e * second) * inverse
    do32 = (back_ref[1] - first - hat_o * second) * inverse
    de = de32.astype(BF16)
    do = do32.astype(BF16)
    de_up = shift_up(de32, quarter).astype(BF16)
    do_down = shift_down(do32, quarter).astype(BF16)
    f0, f1, f2, f3 = (normed_ref[i] for i in range(4))
    grads[0:bins, :] += dot_tn(f3, de_up) + dot_tn(f1, do)
    grads[bins:2 * bins, :] += dot_tn(f0, de) + dot_tn(f2, do)
    grads[2 * bins:3 * bins, :] += dot_tn(f1, de) + dot_tn(f3, do)
    grads[3 * bins:4 * bins, :] += dot_tn(f2, de) + dot_tn(f0, do_down)

    @pl.when(step == pl.num_programs(0) - 1)
    def _():
        write_halves(core_ref, grads, own_ref, send_ref, (0, 4 * bins))


def grad_call(permutation, core, normed, pre, back, moment, sums, quarter, cols):
    bins = normed.shape[2]
    channels = pre.shape[2]
    windows = normed.shape[1] // quarter
    grid_spec = pltpu.PrefetchScalarGridSpec(
        num_scalar_prefetch=2,
        grid=(windows // STEP_WINDOWS,),
        in_specs=[
            ON_CHIP,
            ON_CHIP,
            ON_CHIP,
            pl.BlockSpec(moment.shape, lambda i, p, c: (0, 0)),
            ON_CHIP,
        ],
        out_specs=[ON_CHIP] * 2,
        scratch_shapes=[pltpu.VMEM((4 * bins, channels), F32), pltpu.VMEM((windows, 2 * channels), F32)],
    )
    return pl.pallas_call(
        functools.partial(grad_kernel, quarter=quarter, cols=cols),
        grid_spec=grid_spec,
        out_shape=[pltpu.VMEM((2 * bins, channels), F32)] * 2,
        compiler_params=pltpu.CompilerParams(vmem_limit_bytes=16 * MIB),
        name="grad_enc1",
    )(permutation, core, on_chip(normed), on_chip(pre), on_chip(back), moment, on_chip(sums))


def swap_cores(values):
    return lax.ppermute(values, "core", [(0, 1), (1, 0)])


def exchange(values, axes):
    return lax.all_to_all(values, axes, split_axis=0, concat_axis=0, tiled=True)


def chip_sums(parts, axes, chips):
    total = [(own + swap_cores(send)).astype(BF16).reshape(chips, -1, own.shape[1]) for own, send in parts]
    total = jnp.concatenate(total, axis=1)
    return exchange(total.reshape(-1, total.shape[2]), axes).reshape(total.shape)


def owner_kernel(in_ref, out_ref):
    chips, rows, width = in_ref.shape

    def body(i, total):
        return total + in_ref[i].astype(F32)

    total = lax.fori_loop(0, chips, body, jnp.zeros((rows, width), F32), unroll=4)
    largest = jnp.max(jnp.max(jnp.abs(total), axis=0, keepdims=True), axis=1, keepdims=True)
    exponent = jnp.clip(jnp.ceil(jnp.log2(largest)), -110.0, 126.0)
    total = total * jnp.exp2(14.0 - exponent)
    for k in range(width // LANES):
        out_ref[k * rows:(k + 1) * rows, :] = total[:, k * LANES:(k + 1) * LANES]
    out_ref[width // LANES * rows:, :] = jnp.broadcast_to(exponent, (SCALE_ROWS, LANES))


def owner_call(pieces):
    chips, rows, width = pieces.shape
    return pl.pallas_call(
        owner_kernel,
        out_shape=jax.ShapeDtypeStruct((width // LANES * rows + SCALE_ROWS, LANES), F32),
        compiler_params=pltpu.CompilerParams(vmem_limit_bytes=6 * MIB),
        name="owner_sum",
    )(pieces)


def gather_rows(piece, axes, chips):
    rows, width = piece.shape
    copies = jnp.broadcast_to(piece.astype(jnp.float16)[None], (chips, rows, width))
    return exchange(copies.reshape(-1, width), axes).reshape(chips, rows, width)


def place_kernel(half_ref, blocks_ref, *refs, rows, cut):
    grad_w_ref, grad_v_ref, grad_b_ref, grad_c_ref = refs[-4:]
    step = pl.program_id(0)
    steps = pl.num_programs(0)
    late = rows - cut
    for i in range(blocks_ref.shape[0]):
        scale = jnp.exp2(blocks_ref[i, 2 * rows:2 * rows + 1, :] - 14.0)
        for k in range(2):
            lanes = slice(k * LANES, (k + 1) * LANES)
            block = blocks_ref[i, k * rows:(k + 1) * rows, :] * scale
            grad_w_ref[i * late:(i + 1) * late, lanes] = block[cut:rows]
            top = block[0:cut]
            at = slice(i * cut, (i + 1) * cut)

            @pl.when(step < steps // 2)
            def _():
                grad_c_ref[at, lanes] = top

            @pl.when((step >= steps // 2) & (step < 3 * steps // 4))
            def _():
                grad_b_ref[at, lanes] = top

            @pl.when(step >= 3 * steps // 4)
            def _():
                grad_v_ref[at, lanes] = top


def place_call(half, blocks, rows, cut, channels, bins, earlier=()):
    chips, total, _ = blocks.shape
    late = rows - cut
    group = channels // cut
    steps = chips // group
    quarter = steps // 4
    within = lambda i, low, count: jnp.clip(i - low, 0, count - 1)
    grid_spec = pltpu.PrefetchScalarGridSpec(
        num_scalar_prefetch=1,
        grid=(steps,),
        in_specs=[pl.BlockSpec((group, total, LANES), lambda i, h: (i, 0, 0))]
        + [pl.BlockSpec(memory_space=pl.ANY)] * len(earlier),
        out_specs=[
            pl.BlockSpec((group * late, channels), lambda i, h: (h[0] * steps + i, 0)),
            pl.BlockSpec((channels, channels), lambda i, h: (h[0] * quarter + within(i, 3 * quarter, quarter), 0)),
            pl.BlockSpec((channels, channels), lambda i, h: (0, h[0] * quarter + within(i, 2 * quarter, quarter))),
            pl.BlockSpec((channels, channels), lambda i, h: (0, h[0] * 2 * quarter + within(i, 0, 2 * quarter))),
        ],
    )
    return pl.pallas_call(
        functools.partial(place_kernel, rows=rows, cut=cut),
        grid_spec=grid_spec,
        out_shape=[
            jax.ShapeDtypeStruct((4 * bins, channels), F32),
            jax.ShapeDtypeStruct((4 * channels, channels), F32),
            jax.ShapeDtypeStruct((channels, 4 * channels), F32),
            jax.ShapeDtypeStruct((channels, 4 * bins), F32),
        ],
        input_output_aliases={2 + k: k for k in range(len(earlier))},
        compiler_params=pltpu.CompilerParams(vmem_limit_bytes=12 * MIB),
        cost_estimate=pl.CostEstimate(flops=chips * total * LANES, bytes_accessed=8 * chips * total * LANES, transcendentals=0),
        name="place_gradients",
    )(half, blocks, *earlier)


def local(spectra, sensor_ids, permutation, w_enc1, w_enc2, w_dec1, w_dec2):
    windows, frames, bins = spectra.shape
    channels = w_enc1.shape[1]
    col_axes = ("pair", "core")
    chip_axes = ("row", "pair")
    every = ("row", "pair", "core")
    cols = lax.axis_size("pair") * lax.axis_size("core")
    chips = lax.axis_size("row") * lax.axis_size("pair")
    total_windows = windows * lax.axis_size("row") * cols
    sensors = total_windows // WIN_SENSOR
    chunks = bins // LANES
    quarter = frames // 4
    core_index = lax.axis_index("core")
    core = core_index.astype(jnp.int32).reshape(1)

    logs, sums = sums_call(spectra, sensor_ids)
    sums, core = lax.optimization_barrier((sums, core))
    sums = exchange(sums, every)
    coef = exchange(stats_call(sums, windows, chunks, sensors, WIN_SENSOR * frames), every)
    normed, pre, stat = enc1_call(permutation, logs, coef, w_enc1, quarter, cols)
    stat = exchange(stat.reshape(cols * windows, 2 * channels), col_axes).reshape(cols, windows, 2 * channels)
    own, send, back, moment, moments = middle_call(
        permutation, core, normed, pre, stat, w_enc2, w_dec1, w_dec2, quarter, cols, total_windows)
    moments = exchange(moments.reshape(cols * windows, 2 * channels), col_axes).reshape(cols, windows, 2 * channels)
    late = grad_call(permutation, core, normed, pre, back, moment, moments, quarter, cols)
    piece = owner_call(chip_sums([(own, send), late], chip_axes, chips))
    mine = gather_rows(piece, chip_axes, chips)
    other = swap_cores(mine)
    rows, cut = own.shape[0] // chips + late[0].shape[0] // chips, own.shape[0] // chips
    placed = place_call(core, mine.astype(F32), rows, cut, channels, bins)
    return tuple(place_call(1 - core, other.astype(F32), rows, cut, channels, bins, placed))


def solution(mesh):
    rows, cols = mesh.devices.shape
    inner = Mesh(mesh.devices.reshape(rows, cols // 2, 2), ("row", "pair", "core"))
    spread = ("row", "pair", "core")
    return jax.shard_map(
        local,
        mesh=inner,
        in_specs=(P(spread, None, None), P(spread, None), P(spread), P(), P(), P(), P()),
        out_specs=(P(), P(), P(), P()),
        check_vma=False,
    )
```

```python
import functools

import jax
import jax.numpy as jnp
from jax import lax
from jax.experimental import pallas as pl
from jax.experimental.pallas import tpu as pltpu
from jax.sharding import Mesh, PartitionSpec as P

WIN_SENSOR = 8
EPS = 1e-05
F32 = jnp.float32
BF16 = jnp.bfloat16
LANES = 128
STEP_WINDOWS = 16
SORT_WINDOWS = 4
SCALE_ROWS = 8
MIB = 1024 * 1024


ON_CHIP = pl.BlockSpec(memory_space=pltpu.VMEM)


def on_chip(values):
    return pltpu.with_memory_space_constraint(values, pltpu.VMEM)


def in_hbm(values):
    return pltpu.with_memory_space_constraint(values, pltpu.HBM)


def step_rows(ref, rows):
    return ref.at[:, pl.ds(pl.multiple_of(pl.program_id(0) * rows, rows), rows), :]


def dot(left, right):
    return jnp.dot(left, right, preferred_element_type=F32)


def dot_nt(left, right):
    return lax.dot_general(left, right, (((1,), (1,)), ((), ())), preferred_element_type=F32)


def dot_tn(left, right):
    return lax.dot_general(left, right, (((0,), (0,)), ((), ())), preferred_element_type=F32)


def split3(values):
    first = values.astype(BF16)
    rest = values - first.astype(F32)
    second = rest.astype(BF16)
    third = (rest - second.astype(F32)).astype(BF16)
    return first, second, third


def sigmoid(values):
    return 1.0 / (1.0 + jnp.exp(-values))


def shift_down(values, period):
    rows = lax.broadcasted_iota(jnp.int32, values.shape, 0) % period
    return jnp.where(rows == 0, 0.0, pltpu.roll(values, 1, 0))


def shift_up(values, period):
    total = values.shape[0]
    rows = lax.broadcasted_iota(jnp.int32, values.shape, 0) % period
    return jnp.where(rows == period - 1, 0.0, pltpu.roll(values, total - 1, 0))


def group_rank(perm_ref, window, window_dev, col_count):
    trainer = perm_ref[window] // window_dev
    per_row = 2
    return (trainer // col_count) * per_row + trainer % per_row


def sums_kernel(ids_ref, spec_ref, log_ref, out_ref, acc, lane, *, chunks, count):
    step = pl.program_id(0)
    windows, frames, bins = spec_ref.shape
    quarter = frames // 4
    rows = 16
    log_ref = step_rows(log_ref, windows * quarter)

    for w in range(windows):
        def body(i, carry):
            total, square = carry
            start = pl.multiple_of(i * rows, rows)
            value = jnp.log(1.0 + spec_ref[w, pl.ds(start, rows), :].astype(F32))
            for k in range(chunks):
                lane[w % 2, k, pl.ds(start, rows), :] = value[:, k * LANES:(k + 1) * LANES]
            value_sq = value * value
            return (total + value[0:8] + value[8:16], square + value_sq[0:8] + value_sq[8:16])

        zero = jnp.zeros((8, bins), F32)
        total, square = lax.fori_loop(0, frames // rows, body, (zero, zero), unroll=4)
        total = jnp.sum(total, axis=0, keepdims=True)
        square = jnp.sum(square, axis=0, keepdims=True)
        pieces = [total[:, k * LANES:(k + 1) * LANES] for k in range(chunks)]
        pieces += [square[:, k * LANES:(k + 1) * LANES] for k in range(chunks)]
        start = pl.multiple_of((step * windows + w) * 2 * chunks, 2 * chunks)
        acc[pl.ds(start, 2 * chunks), :] = jnp.concatenate(pieces, axis=0)
        for i in range(4):
            for k in range(chunks):
                log_ref[i, w * quarter:(w + 1) * quarter, k * LANES:(k + 1) * LANES] = lane[w % 2, k, pl.ds(i, quarter, stride=4), :]

    @pl.when(step == pl.num_programs(0) - 1)
    def _():
        acc[LANES:2 * LANES, :] = jnp.zeros((LANES, LANES), F32)
        for w in range(count):
            acc[LANES + w:LANES + w + 1, :] = jnp.full((1, LANES), ids_ref[w], jnp.int32).astype(F32)
        out_ref[pl.ds(0, LANES, stride=2), :] = acc[0:LANES, :].T
        out_ref[pl.ds(1, LANES, stride=2), :] = acc[LANES:2 * LANES, :].T


def sums_call(spectra, sensor_ids):
    windows, frames, bins = spectra.shape
    chunks = bins // LANES
    grid_spec = pltpu.PrefetchScalarGridSpec(
        num_scalar_prefetch=1,
        grid=(windows // SORT_WINDOWS,),
        in_specs=[pl.BlockSpec((SORT_WINDOWS, frames, bins), lambda i, s: (i, 0, 0))],
        out_specs=[ON_CHIP, pl.BlockSpec((2 * LANES, LANES), lambda i, s: (0, 0))],
        scratch_shapes=[pltpu.VMEM((2 * LANES, LANES), F32), pltpu.VMEM((2, chunks, frames, LANES), F32)],
    )
    return pl.pallas_call(
        functools.partial(sums_kernel, chunks=chunks, count=windows),
        grid_spec=grid_spec,
        out_shape=[
            pltpu.VMEM((4, windows * frames // 4, bins), F32),
            jax.ShapeDtypeStruct((2 * LANES, LANES), F32),
        ],
        compiler_params=pltpu.CompilerParams(vmem_limit_bytes=10 * MIB),
        name="sort_and_sum",
    )(in_hbm(sensor_ids.reshape(windows)), in_hbm(spectra))


def stats_kernel(in_ref, out_ref, *, windows, chunks, sensors, per_sensor):
    width = 2 * chunks
    data = in_ref[pl.ds(0, LANES, stride=2), :].T
    labels = in_ref[pl.ds(1, LANES, stride=2), :].T
    sensor_rows = lax.broadcasted_iota(jnp.int32, (sensors, LANES), 0).astype(F32)
    tables = [(sensor_rows == labels[w:w + 1, :]).astype(F32).astype(BF16) for w in range(windows)]
    table = jnp.concatenate(tables, axis=1)
    values = jnp.concatenate([data[w * width:(w + 1) * width, :] for w in range(windows)], axis=1)
    parts = dot_nt(jnp.concatenate(split3(values), axis=0), table)
    sums = parts[0:width] + parts[width:2 * width] + parts[2 * width:3 * width]
    center = sums[0:chunks] / per_sensor
    factor = lax.rsqrt(sums[chunks:width] / per_sensor - center * center + EPS)
    both = jnp.concatenate([center, factor], axis=0)
    back = dot(jnp.concatenate(split3(both), axis=0), table)
    back = back[0:width] + back[width:2 * width] + back[2 * width:3 * width]
    rows = jnp.concatenate([back[:, w * LANES:(w + 1) * LANES] for w in range(windows)], axis=0)
    out_ref[...] = rows.T


def stats_call(received, windows, chunks, sensors, per_sensor):
    return pl.pallas_call(
        functools.partial(stats_kernel, windows=windows, chunks=chunks, sensors=sensors, per_sensor=float(per_sensor)),
        out_shape=jax.ShapeDtypeStruct((LANES, LANES), F32),
        compiler_params=pltpu.CompilerParams(vmem_limit_bytes=12 * MIB),
        name="sensor_stats",
    )(received)


def enc1_kernel(perm_ref, log_ref, coef_ref, w_ref, normed_ref, pre_ref, stat_ref, coef, stat, *, chunks, quarter, cols, copies):
    step = pl.program_id(0)
    bins = log_ref.shape[2]
    windows = STEP_WINDOWS
    log_ref, normed_ref, pre_ref = (step_rows(ref, windows * quarter) for ref in (log_ref, normed_ref, pre_ref))
    channels = w_ref.shape[1]
    all_windows = windows * pl.num_programs(0)
    width = 2 * chunks

    @pl.when(step == 0)
    def _():
        coef[...] = coef_ref[...].T

    for w in range(windows):
        start = pl.multiple_of((step * windows + w) * width, width)
        both = coef[pl.ds(start, width), :]
        low, high = w * quarter, (w + 1) * quarter
        for k in range(chunks):
            left, right = k * LANES, (k + 1) * LANES
            center = both[k:k + 1, :]
            factor = both[chunks + k:chunks + k + 1, :]
            for i in range(4):
                normed_ref[i, low:high, left:right] = ((log_ref[i, low:high, left:right] - center) * factor).astype(BF16)

    w0, w1, w2, w3 = (w_ref[k * bins:(k + 1) * bins, :] for k in range(4))
    f0, f1, f2, f3 = (normed_ref[i] for i in range(4))
    even = shift_down(dot(f3, w0), quarter) + dot(f0, w1) + dot(f1, w2) + dot(f2, w3)
    odd = dot(f1, w0) + dot(f2, w1) + dot(f3, w2) + shift_up(dot(f0, w3), quarter)
    pre_ref[0] = even
    pre_ref[1] = odd
    for w in range(windows):
        part_e = even[w * quarter:(w + 1) * quarter]
        part_o = odd[w * quarter:(w + 1) * quarter]
        mean = (jnp.sum(part_e, axis=0, keepdims=True) + jnp.sum(part_o, axis=0, keepdims=True)) / (2 * quarter)
        diff_e = part_e - mean
        diff_o = part_o - mean
        spread = (jnp.sum(diff_e * diff_e, axis=0, keepdims=True) + jnp.sum(diff_o * diff_o, axis=0, keepdims=True)) / (2 * quarter)
        place = group_rank(perm_ref, step * windows + w, all_windows, cols)
        stat[pl.ds(place, 1), 0:channels] = mean
        stat[pl.ds(place, 1), channels:2 * channels] = spread

    @pl.when(step == pl.num_programs(0) - 1)
    def _():
        for d in range(copies):
            stat_ref[d] = stat[...]


def enc1_call(permutation, logs, coef, w_enc1, quarter, cols):
    bins = logs.shape[2]
    windows = logs.shape[1] // quarter
    chunks = bins // LANES
    channels = w_enc1.shape[1]
    grid_spec = pltpu.PrefetchScalarGridSpec(
        num_scalar_prefetch=1,
        grid=(windows // STEP_WINDOWS,),
        in_specs=[
            ON_CHIP,
            pl.BlockSpec((LANES, LANES), lambda i, p: (0, 0)),
            ON_CHIP,
        ],
        out_specs=[
            ON_CHIP,
            ON_CHIP,
            pl.BlockSpec((cols, windows, 2 * channels), lambda i, p: (0, 0, 0)),
        ],
        scratch_shapes=[
            pltpu.VMEM((LANES, LANES), F32),
            pltpu.VMEM((windows, 2 * channels), F32),
        ],
    )
    return pl.pallas_call(
        functools.partial(enc1_kernel, chunks=chunks, quarter=quarter, cols=cols, copies=cols),
        grid_spec=grid_spec,
        out_shape=[
            pltpu.VMEM((4, windows * quarter, bins), BF16),
            pltpu.VMEM((2, windows * quarter, channels), F32),
            jax.ShapeDtypeStruct((cols, windows, 2 * channels), F32),
        ],
        compiler_params=pltpu.CompilerParams(vmem_limit_bytes=16 * MIB),
        name="normalize_enc1",
    )(permutation, on_chip(logs), coef, on_chip(w_enc1))


def window_rows(perm_ref, table, step, windows, quarter, all_windows, cols, first, last):
    parts = []
    for w in range(windows):
        place = group_rank(perm_ref, step * windows + w, all_windows, cols)
        parts.append(jnp.broadcast_to(table[pl.ds(place, 1), first:last], (quarter, last - first)))
    return jnp.concatenate(parts, axis=0)


def write_halves(core_ref, grads, own_ref, send_ref, bounds):
    for first, last in zip(bounds[:-1], bounds[1:]):
        half = (last - first) // 2
        at = first // 2
        own = pl.multiple_of(first + core_ref[0] * half, half)
        send = pl.multiple_of(first + (1 - core_ref[0]) * half, half)
        own_ref[at:at + half, :] = grads[pl.ds(own, half), :]
        send_ref[at:at + half, :] = grads[pl.ds(send, half), :]


def middle_kernel(perm_ref, core_ref, normed_ref, pre_ref, stat_ref, v_ref, b_ref, c_ref,
                  own_ref, send_ref, back_ref, moment_ref, sums_ref,
                  grads, moment, sums, *, quarter, cols, total_windows):
    step = pl.program_id(0)
    channels = v_ref.shape[1]
    bins = normed_ref.shape[2]
    windows = STEP_WINDOWS
    normed_ref, pre_ref, back_ref = (step_rows(ref, windows * quarter) for ref in (normed_ref, pre_ref, back_ref))
    all_windows = windows * pl.num_programs(0)
    ch = channels

    @pl.when(step == 0)
    def _():
        means = stat_ref[:, :, 0:ch]
        mean = jnp.mean(means, axis=0)
        diff = means - mean[None]
        variance = jnp.mean(stat_ref[:, :, ch:2 * ch] + diff * diff, axis=0)
        moment[:, 0:ch] = mean
        moment[:, ch:2 * ch] = lax.rsqrt(variance + EPS)
        moment_ref[...] = moment[...]
        grads[...] = jnp.zeros_like(grads)

    mean = window_rows(perm_ref, moment, step, windows, quarter, all_windows, cols, 0, ch)
    inverse = window_rows(perm_ref, moment, step, windows, quarter, all_windows, cols, ch, 2 * ch)
    hat_e = (pre_ref[0] - mean) * inverse
    hat_o = (pre_ref[1] - mean) * inverse
    a_e = (hat_e * sigmoid(hat_e)).astype(BF16)
    a_o = (hat_o * sigmoid(hat_o)).astype(BF16)
    v0, v1, v2, v3 = (v_ref[k * ch:(k + 1) * ch, :] for k in range(4))
    pre2 = shift_down(dot(a_o, v0), quarter) + dot(a_e, v1) + dot(a_o, v2) + shift_up(dot(a_e, v3), quarter)
    gate2 = sigmoid(pre2)
    h32 = (pre2 * gate2).astype(BF16).astype(F32)
    h = h32.astype(BF16)
    b0, b1, b2, b3 = (b_ref[:, k * ch:(k + 1) * ch] for k in range(4))
    d1_e = dot(h, b1) + shift_down(dot(h, b3), quarter)
    d1_o = dot(h, b2) + shift_up(dot(h, b0), quarter)
    gate_e = sigmoid(d1_e)
    gate_o = sigmoid(d1_o)
    de32 = (d1_e * gate_e)
    do32 = (d1_o * gate_o)
    de = de32.astype(BF16)
    do = do32.astype(BF16)
    de_up = shift_up(de32, quarter).astype(BF16)
    do_down = shift_down(do32, quarter).astype(BF16)
    c0, c1, c2, c3 = (c_ref[:, k * bins:(k + 1) * bins] for k in range(4))

    def delta(rebuilt, i):
        return ((rebuilt - normed_ref[i].astype(F32)) / total_windows).astype(BF16)

    g0 = delta(dot(de, c1) + dot(do_down, c3), 0)
    g1 = delta(dot(de, c2) + dot(do, c0), 1)
    g2 = delta(dot(do, c1) + dot(de, c3), 2)
    g3 = delta(dot(do, c2) + dot(de_up, c0), 3)
    halves = bins // ch
    base_b = 4 * bins
    base_v = base_b + 4 * ch

    def add_c(k, value):
        for j in range(halves):
            at = (k * halves + j) * ch
            grads[at:at + ch, :] += value[:, j * ch:(j + 1) * ch]

    add_c(0, dot_tn(de_up, g3) + dot_tn(do, g1))
    add_c(1, dot_tn(de, g0) + dot_tn(do, g2))
    add_c(2, dot_tn(de, g1) + dot_tn(do, g3))
    add_c(3, dot_tn(de, g2) + dot_tn(do_down, g0))
    back_e = shift_down(dot_nt(g3, c0), quarter) + dot_nt(g0, c1) + dot_nt(g1, c2) + dot_nt(g2, c3)
    back_o = dot_nt(g1, c0) + dot_nt(g2, c1) + dot_nt(g3, c2) + shift_up(dot_nt(g0, c3), quarter)
    dd_e = (back_e * (gate_e * (1.0 + d1_e * (1.0 - gate_e)))).astype(BF16)
    dd_o = (back_o * (gate_o * (1.0 + d1_o * (1.0 - gate_o)))).astype(BF16)
    h_up = shift_up(h32, quarter).astype(BF16)
    h_down = shift_down(h32, quarter).astype(BF16)
    grads[base_b:base_b + ch, :] += dot_tn(h_up, dd_o)
    grads[base_b + ch:base_b + 2 * ch, :] += dot_tn(h, dd_e)
    grads[base_b + 2 * ch:base_b + 3 * ch, :] += dot_tn(h, dd_o)
    grads[base_b + 3 * ch:base_b + 4 * ch, :] += dot_tn(h_down, dd_e)
    back2 = shift_down(dot_nt(dd_o, b0), quarter) + dot_nt(dd_e, b1) + dot_nt(dd_o, b2) + shift_up(dot_nt(dd_e, b3), quarter)
    d2_32 = (back2 * (gate2 * (1.0 + pre2 * (1.0 - gate2)))).astype(BF16).astype(F32)
    d2 = d2_32.astype(BF16)
    d2_up = shift_up(d2_32, quarter).astype(BF16)
    d2_down = shift_down(d2_32, quarter).astype(BF16)
    grads[base_v:base_v + ch, :] += dot_tn(a_o, d2_up)
    grads[base_v + ch:base_v + 2 * ch, :] += dot_tn(a_e, d2)
    grads[base_v + 2 * ch:base_v + 3 * ch, :] += dot_tn(a_o, d2)
    grads[base_v + 3 * ch:base_v + 4 * ch, :] += dot_tn(a_e, d2_down)
    fold_e = dot_nt(d2, v1) + shift_down(dot_nt(d2, v3), quarter)
    fold_o = dot_nt(d2, v2) + shift_up(dot_nt(d2, v0), quarter)
    gate_he = sigmoid(hat_e)
    gate_ho = sigmoid(hat_o)
    fold_e = fold_e * (gate_he * (1.0 + hat_e * (1.0 - gate_he)))
    fold_o = fold_o * (gate_ho * (1.0 + hat_o * (1.0 - gate_ho)))
    back_ref[0] = fold_e
    back_ref[1] = fold_o
    cross_e = fold_e * hat_e
    cross_o = fold_o * hat_o
    for w in range(windows):
        low, high = w * quarter, (w + 1) * quarter
        first = jnp.sum(fold_e[low:high] + fold_o[low:high], axis=0, keepdims=True)
        second = jnp.sum(cross_e[low:high] + cross_o[low:high], axis=0, keepdims=True)
        place = group_rank(perm_ref, step * windows + w, all_windows, cols)
        sums[pl.ds(place, 1), 0:ch] = first
        sums[pl.ds(place, 1), ch:2 * ch] = second

    @pl.when(step == pl.num_programs(0) - 1)
    def _():
        for d in range(cols):
            sums_ref[d] = sums[...]
        write_halves(core_ref, grads, own_ref, send_ref, (0, base_b, base_v, base_v + 4 * ch))


def middle_call(permutation, core, normed, pre, stat, w_enc2, w_dec1, w_dec2, quarter, cols, total_windows):
    bins = normed.shape[2]
    channels = w_enc2.shape[1]
    windows = normed.shape[1] // quarter
    total = 4 * bins + 8 * channels
    whole2 = lambda i, p, c: (0, 0)
    whole3 = lambda i, p, c: (0, 0, 0)
    grid_spec = pltpu.PrefetchScalarGridSpec(
        num_scalar_prefetch=2,
        grid=(windows // STEP_WINDOWS,),
        in_specs=[
            ON_CHIP,
            ON_CHIP,
            ON_CHIP,
            ON_CHIP,
            ON_CHIP,
            ON_CHIP,
        ],
        out_specs=[
            ON_CHIP,
            ON_CHIP,
            ON_CHIP,
            pl.BlockSpec((windows, 2 * channels), whole2),
            pl.BlockSpec(stat.shape, whole3),
        ],
        scratch_shapes=[
            pltpu.VMEM((total, channels), F32),
            pltpu.VMEM((windows, 2 * channels), F32),
            pltpu.VMEM((windows, 2 * channels), F32),
        ],
    )
    return pl.pallas_call(
        functools.partial(middle_kernel, quarter=quarter, cols=cols, total_windows=float(total_windows)),
        grid_spec=grid_spec,
        out_shape=[
            pltpu.VMEM((total // 2, channels), F32),
            pltpu.VMEM((total // 2, channels), F32),
            pltpu.VMEM(pre.shape, F32),
            jax.ShapeDtypeStruct((windows, 2 * channels), F32),
            jax.ShapeDtypeStruct(stat.shape, F32),
        ],
        compiler_params=pltpu.CompilerParams(vmem_limit_bytes=30 * MIB),
        name="middle",
    )(permutation, core, on_chip(normed), on_chip(pre), on_chip(stat), on_chip(w_enc2), on_chip(w_dec1), on_chip(w_dec2))


def grad_kernel(perm_ref, core_ref, normed_ref, pre_ref, back_ref, moment_ref, sums_ref, own_ref, send_ref, grads, scale, *, quarter, cols):
    step = pl.program_id(0)
    bins = normed_ref.shape[2]
    ch = pre_ref.shape[2]
    windows = STEP_WINDOWS
    rows = windows * quarter
    normed_ref = step_rows(normed_ref, rows)
    pre_ref, back_ref = step_rows(pre_ref, rows), step_rows(back_ref, rows)
    all_windows = windows * pl.num_programs(0)

    @pl.when(step == 0)
    def _():
        scale[...] = jnp.sum(sums_ref[...], axis=0) / (2.0 * quarter * cols)
        grads[...] = jnp.zeros_like(grads)

    pick = functools.partial(window_rows, perm_ref, step=step, windows=windows, quarter=quarter, all_windows=all_windows, cols=cols)
    mean = pick(table=moment_ref, first=0, last=ch)
    inverse = pick(table=moment_ref, first=ch, last=2 * ch)
    first = pick(table=scale, first=0, last=ch)
    second = pick(table=scale, first=ch, last=2 * ch)
    hat_e = (pre_ref[0] - mean) * inverse
    hat_o = (pre_ref[1] - mean) * inverse
    de32 = (back_ref[0] - first - hat_e * second) * inverse
    do32 = (back_ref[1] - first - hat_o * second) * inverse
    de = de32.astype(BF16)
    do = do32.astype(BF16)
    de_up = shift_up(de32, quarter).astype(BF16)
    do_down = shift_down(do32, quarter).astype(BF16)
    f0, f1, f2, f3 = (normed_ref[i] for i in range(4))
    grads[0:bins, :] += dot_tn(f3, de_up) + dot_tn(f1, do)
    grads[bins:2 * bins, :] += dot_tn(f0, de) + dot_tn(f2, do)
    grads[2 * bins:3 * bins, :] += dot_tn(f1, de) + dot_tn(f3, do)
    grads[3 * bins:4 * bins, :] += dot_tn(f2, de) + dot_tn(f0, do_down)

    @pl.when(step == pl.num_programs(0) - 1)
    def _():
        write_halves(core_ref, grads, own_ref, send_ref, (0, 4 * bins))


def grad_call(permutation, core, normed, pre, back, moment, sums, quarter, cols):
    bins = normed.shape[2]
    channels = pre.shape[2]
    windows = normed.shape[1] // quarter
    grid_spec = pltpu.PrefetchScalarGridSpec(
        num_scalar_prefetch=2,
        grid=(windows // STEP_WINDOWS,),
        in_specs=[
            ON_CHIP,
            ON_CHIP,
            ON_CHIP,
            pl.BlockSpec(moment.shape, lambda i, p, c: (0, 0)),
            ON_CHIP,
        ],
        out_specs=[ON_CHIP] * 2,
        scratch_shapes=[pltpu.VMEM((4 * bins, channels), F32), pltpu.VMEM((windows, 2 * channels), F32)],
    )
    return pl.pallas_call(
        functools.partial(grad_kernel, quarter=quarter, cols=cols),
        grid_spec=grid_spec,
        out_shape=[pltpu.VMEM((2 * bins, channels), F32)] * 2,
        compiler_params=pltpu.CompilerParams(vmem_limit_bytes=16 * MIB),
        name="grad_enc1",
    )(permutation, core, on_chip(normed), on_chip(pre), on_chip(back), moment, on_chip(sums))


def swap_cores(values):
    return lax.ppermute(values, "core", [(0, 1), (1, 0)])


def exchange(values, axes):
    return lax.all_to_all(values, axes, split_axis=0, concat_axis=0, tiled=True)


def chip_sums(parts, axes, chips):
    total = [(own + swap_cores(send)).astype(BF16).reshape(chips, -1, own.shape[1]) for own, send in parts]
    total = jnp.concatenate(total, axis=1)
    return exchange(total.reshape(-1, total.shape[2]), axes).reshape(total.shape)


def owner_kernel(in_ref, out_ref):
    chips, rows, width = in_ref.shape

    def body(i, total):
        return total + in_ref[i].astype(F32)

    total = lax.fori_loop(0, chips, body, jnp.zeros((rows, width), F32), unroll=4)
    largest = jnp.max(jnp.max(jnp.abs(total), axis=0, keepdims=True), axis=1, keepdims=True)
    exponent = jnp.clip(jnp.ceil(jnp.log2(largest)), -110.0, 126.0)
    total = total * jnp.exp2(14.0 - exponent)
    for k in range(width // LANES):
        out_ref[k * rows:(k + 1) * rows, :] = total[:, k * LANES:(k + 1) * LANES]
    out_ref[width // LANES * rows:, :] = jnp.broadcast_to(exponent, (SCALE_ROWS, LANES))


def owner_call(pieces):
    chips, rows, width = pieces.shape
    return pl.pallas_call(
        owner_kernel,
        out_shape=jax.ShapeDtypeStruct((width // LANES * rows + SCALE_ROWS, LANES), F32),
        compiler_params=pltpu.CompilerParams(vmem_limit_bytes=6 * MIB),
        name="owner_sum",
    )(pieces)


def gather_rows(piece, axes, chips):
    rows, width = piece.shape
    copies = jnp.broadcast_to(piece.astype(jnp.float16)[None], (chips, rows, width))
    return exchange(copies.reshape(-1, width), axes).reshape(chips, rows, width)


def place_kernel(half_ref, blocks_ref, *refs, rows, cut):
    grad_w_ref, grad_v_ref, grad_b_ref, grad_c_ref = refs[-4:]
    step = pl.program_id(0)
    channels = grad_w_ref.shape[1]
    late = rows - cut
    group = channels // cut

    def copy(out_ref, i, row, column):
        scale = jnp.exp2(blocks_ref[i, 2 * rows:2 * rows + 1, :] - 14.0)
        for k in range(2):
            block = blocks_ref[i, k * rows:(k + 1) * rows, :] * scale
            grad_w_ref[i * late:(i + 1) * late, k * LANES:(k + 1) * LANES] = block[cut:rows]
            out_ref[row:row + cut, column + k * LANES:column + (k + 1) * LANES] = block[0:cut]

    @pl.when(step < 2)
    def _():
        for i in range(2 * group):
            copy(grad_c_ref, i, i % group * cut, i // group * channels)

    @pl.when(step == 2)
    def _():
        for i in range(2 * group):
            copy(grad_b_ref, i, i % group * cut, i // group * channels)

    @pl.when(step == 3)
    def _():
        for i in range(2 * group):
            copy(grad_v_ref, i, i * cut, 0)


def place_call(half, blocks, rows, cut, channels, bins, earlier=()):
    chips, total, _ = blocks.shape
    group = channels // cut
    late = rows - cut
    grid_spec = pltpu.PrefetchScalarGridSpec(
        num_scalar_prefetch=1,
        grid=(4,),
        in_specs=[pl.BlockSpec((2 * group, total, LANES), lambda i, h: (i, 0, 0))]
        + [pl.BlockSpec(memory_space=pl.ANY)] * len(earlier),
        out_specs=[
            pl.BlockSpec((2 * group * late, channels), lambda i, h: (h[0] * 4 + i, 0)),
            pl.BlockSpec((2 * channels, channels), lambda i, h: (h[0], 0)),
            pl.BlockSpec((channels, 2 * channels), lambda i, h: (0, h[0])),
            pl.BlockSpec((channels, 2 * channels), lambda i, h: (0, h[0] * 2 + jnp.minimum(i, 1))),
        ],
    )
    return pl.pallas_call(
        functools.partial(place_kernel, rows=rows, cut=cut),
        grid_spec=grid_spec,
        out_shape=[
            jax.ShapeDtypeStruct((4 * bins, channels), F32),
            jax.ShapeDtypeStruct((4 * channels, channels), F32),
            jax.ShapeDtypeStruct((channels, 4 * channels), F32),
            jax.ShapeDtypeStruct((channels, 4 * bins), F32),
        ],
        input_output_aliases={2 + k: k for k in range(len(earlier))},
        compiler_params=pltpu.CompilerParams(vmem_limit_bytes=16 * MIB),
        cost_estimate=pl.CostEstimate(flops=chips * total * LANES, bytes_accessed=8 * chips * total * LANES, transcendentals=0),
        name="place_gradients",
    )(half, blocks, *earlier)


def local(spectra, sensor_ids, permutation, w_enc1, w_enc2, w_dec1, w_dec2):
    windows, frames, bins = spectra.shape
    channels = w_enc1.shape[1]
    col_axes = ("pair", "core")
    chip_axes = ("row", "pair")
    every = ("row", "pair", "core")
    cols = lax.axis_size("pair") * lax.axis_size("core")
    chips = lax.axis_size("row") * lax.axis_size("pair")
    total_windows = windows * lax.axis_size("row") * cols
    sensors = total_windows // WIN_SENSOR
    chunks = bins // LANES
    quarter = frames // 4
    core_index = lax.axis_index("core")
    core = core_index.astype(jnp.int32).reshape(1)

    logs, sums = sums_call(spectra, sensor_ids)
    sums, core = lax.optimization_barrier((sums, core))
    sums = exchange(sums, every)
    coef = exchange(stats_call(sums, windows, chunks, sensors, WIN_SENSOR * frames), every)
    normed, pre, stat = enc1_call(permutation, logs, coef, w_enc1, quarter, cols)
    stat = exchange(stat.reshape(cols * windows, 2 * channels), col_axes).reshape(cols, windows, 2 * channels)
    own, send, back, moment, moments = middle_call(
        permutation, core, normed, pre, stat, w_enc2, w_dec1, w_dec2, quarter, cols, total_windows)
    moments = exchange(moments.reshape(cols * windows, 2 * channels), col_axes).reshape(cols, windows, 2 * channels)
    late = grad_call(permutation, core, normed, pre, back, moment, moments, quarter, cols)
    piece = owner_call(chip_sums([(own, send), late], chip_axes, chips))
    mine = gather_rows(piece, chip_axes, chips)
    other = swap_cores(mine)
    rows, cut = own.shape[0] // chips + late[0].shape[0] // chips, own.shape[0] // chips
    placed = place_call(core, mine.astype(F32), rows, cut, channels, bins)
    return tuple(place_call(1 - core, other.astype(F32), rows, cut, channels, bins, placed))


def solution(mesh):
    rows, cols = mesh.devices.shape
    inner = Mesh(mesh.devices.reshape(rows, cols // 2, 2), ("row", "pair", "core"))
    spread = ("row", "pair", "core")
    return jax.shard_map(
        local,
        mesh=inner,
        in_specs=(P(spread, None, None), P(spread, None), P(spread), P(), P(), P(), P()),
        out_specs=(P(), P(), P(), P()),
        check_vma=False,
    )
```

```python
import functools

import jax
import jax.numpy as jnp
from jax import lax
from jax.experimental import pallas as pl
from jax.experimental.pallas import tpu as pltpu
from jax.sharding import Mesh, PartitionSpec as P

WIN_SENSOR = 8
EPS = 1e-05
F32 = jnp.float32
BF16 = jnp.bfloat16
LANES = 128
STEP_WINDOWS = 16
SORT_WINDOWS = 8
SCALE_ROWS = 8
MIB = 1024 * 1024


ON_CHIP = pl.BlockSpec(memory_space=pltpu.VMEM)


def on_chip(values):
    return pltpu.with_memory_space_constraint(values, pltpu.VMEM)


def in_hbm(values):
    return pltpu.with_memory_space_constraint(values, pltpu.HBM)


def step_rows(ref, rows):
    return ref.at[:, pl.ds(pl.multiple_of(pl.program_id(0) * rows, rows), rows), :]


def dot(left, right):
    return jnp.dot(left, right, preferred_element_type=F32)


def dot_nt(left, right):
    return lax.dot_general(left, right, (((1,), (1,)), ((), ())), preferred_element_type=F32)


def dot_tn(left, right):
    return lax.dot_general(left, right, (((0,), (0,)), ((), ())), preferred_element_type=F32)


def split3(values):
    first = values.astype(BF16)
    rest = values - first.astype(F32)
    second = rest.astype(BF16)
    third = (rest - second.astype(F32)).astype(BF16)
    return first, second, third


def sigmoid(values):
    return 1.0 / (1.0 + jnp.exp(-values))


def shift_down(values, period):
    rows = lax.broadcasted_iota(jnp.int32, values.shape, 0) % period
    return jnp.where(rows == 0, 0.0, pltpu.roll(values, 1, 0))


def shift_up(values, period):
    total = values.shape[0]
    rows = lax.broadcasted_iota(jnp.int32, values.shape, 0) % period
    return jnp.where(rows == period - 1, 0.0, pltpu.roll(values, total - 1, 0))


def group_rank(perm_ref, window, window_dev, col_count):
    trainer = perm_ref[window] // window_dev
    per_row = 2
    return (trainer // col_count) * per_row + trainer % per_row


def sums_kernel(ids_ref, spec_ref, log_ref, out_ref, acc, *, chunks, count):
    step = pl.program_id(0)
    windows, frames, bins = spec_ref.shape
    rows = 16

    for w in range(windows):
        def body(i, carry):
            total, square = carry
            start = pl.multiple_of(i * rows, rows)
            value = jnp.log(1.0 + spec_ref[w, pl.ds(start, rows), :].astype(F32))
            for k in range(chunks):
                log_ref[step * windows + w, k, pl.ds(start, rows), :] = value[:, k * LANES:(k + 1) * LANES]
            value_sq = value * value
            return (total + value[0:8] + value[8:16], square + value_sq[0:8] + value_sq[8:16])

        zero = jnp.zeros((8, bins), F32)
        total, square = lax.fori_loop(0, frames // rows, body, (zero, zero), unroll=4)
        total = jnp.sum(total, axis=0, keepdims=True)
        square = jnp.sum(square, axis=0, keepdims=True)
        pieces = [total[:, k * LANES:(k + 1) * LANES] for k in range(chunks)]
        pieces += [square[:, k * LANES:(k + 1) * LANES] for k in range(chunks)]
        start = pl.multiple_of((step * windows + w) * 2 * chunks, 2 * chunks)
        acc[pl.ds(start, 2 * chunks), :] = jnp.concatenate(pieces, axis=0)

    @pl.when(step == pl.num_programs(0) - 1)
    def _():
        acc[LANES:2 * LANES, :] = jnp.zeros((LANES, LANES), F32)
        for w in range(count):
            acc[LANES + w:LANES + w + 1, :] = jnp.full((1, LANES), ids_ref[w], jnp.int32).astype(F32)
        out_ref[pl.ds(0, LANES, stride=2), :] = acc[0:LANES, :].T
        out_ref[pl.ds(1, LANES, stride=2), :] = acc[LANES:2 * LANES, :].T


def sums_call(spectra, sensor_ids):
    windows, frames, bins = spectra.shape
    chunks = bins // LANES
    grid_spec = pltpu.PrefetchScalarGridSpec(
        num_scalar_prefetch=1,
        grid=(windows // SORT_WINDOWS,),
        in_specs=[pl.BlockSpec((SORT_WINDOWS, frames, bins), lambda i, s: (i, 0, 0))],
        out_specs=[ON_CHIP, pl.BlockSpec((2 * LANES, LANES), lambda i, s: (0, 0))],
        scratch_shapes=[pltpu.VMEM((2 * LANES, LANES), F32)],
    )
    return pl.pallas_call(
        functools.partial(sums_kernel, chunks=chunks, count=windows),
        grid_spec=grid_spec,
        out_shape=[
            pltpu.VMEM((windows, chunks, frames, LANES), F32),
            jax.ShapeDtypeStruct((2 * LANES, LANES), F32),
        ],
        compiler_params=pltpu.CompilerParams(vmem_limit_bytes=10 * MIB),
        name="log_and_sum",
    )(in_hbm(sensor_ids.reshape(windows)), in_hbm(spectra))


def stats_kernel(in_ref, out_ref, *, windows, chunks, sensors, per_sensor):
    width = 2 * chunks
    data = in_ref[pl.ds(0, LANES, stride=2), :].T
    labels = in_ref[pl.ds(1, LANES, stride=2), :].T
    sensor_rows = lax.broadcasted_iota(jnp.int32, (sensors, LANES), 0).astype(F32)
    tables = [(sensor_rows == labels[w:w + 1, :]).astype(F32).astype(BF16) for w in range(windows)]
    table = jnp.concatenate(tables, axis=1)
    values = jnp.concatenate([data[w * width:(w + 1) * width, :] for w in range(windows)], axis=1)
    parts = dot_nt(jnp.concatenate(split3(values), axis=0), table)
    sums = parts[0:width] + parts[width:2 * width] + parts[2 * width:3 * width]
    center = sums[0:chunks] / per_sensor
    factor = lax.rsqrt(sums[chunks:width] / per_sensor - center * center + EPS)
    both = jnp.concatenate([center, factor], axis=0)
    back = dot(jnp.concatenate(split3(both), axis=0), table)
    back = back[0:width] + back[width:2 * width] + back[2 * width:3 * width]
    rows = jnp.concatenate([back[:, w * LANES:(w + 1) * LANES] for w in range(windows)], axis=0)
    out_ref[...] = rows.T


def stats_call(received, windows, chunks, sensors, per_sensor):
    return pl.pallas_call(
        functools.partial(stats_kernel, windows=windows, chunks=chunks, sensors=sensors, per_sensor=float(per_sensor)),
        out_shape=jax.ShapeDtypeStruct((LANES, LANES), F32),
        compiler_params=pltpu.CompilerParams(vmem_limit_bytes=12 * MIB),
        name="sensor_stats",
    )(received)


def enc1_kernel(perm_ref, log_ref, coef_ref, w_ref, normed_ref, pre_ref, stat_ref, coef, *, cols):
    step = pl.program_id(0)
    all_windows, chunks, frames, _ = log_ref.shape
    quarter = frames // 4
    bins = chunks * LANES
    windows = STEP_WINDOWS
    normed_ref, pre_ref = (step_rows(ref, windows * quarter) for ref in (normed_ref, pre_ref))
    channels = w_ref.shape[1]
    width = 2 * chunks

    @pl.when(step == 0)
    def _():
        coef[...] = coef_ref[...].T

    for w in range(windows):
        start = pl.multiple_of((step * windows + w) * width, width)
        both = coef[pl.ds(start, width), :]
        low, high = w * quarter, (w + 1) * quarter
        for k in range(chunks):
            center = both[k:k + 1, :]
            factor = both[chunks + k:chunks + k + 1, :]
            for i in range(4):
                value = log_ref[step * windows + w, k, pl.ds(i, quarter, stride=4), :]
                normed_ref[i, low:high, k * LANES:(k + 1) * LANES] = ((value - center) * factor).astype(BF16)

    w0, w1, w2, w3 = (w_ref[k * bins:(k + 1) * bins, :] for k in range(4))
    f0, f1, f2, f3 = (normed_ref[i] for i in range(4))
    even = shift_down(dot(f3, w0), quarter) + dot(f0, w1) + dot(f1, w2) + dot(f2, w3)
    odd = dot(f1, w0) + dot(f2, w1) + dot(f3, w2) + shift_up(dot(f0, w3), quarter)
    pre_ref[0] = even
    pre_ref[1] = odd
    for w in range(windows):
        part_e = even[w * quarter:(w + 1) * quarter]
        part_o = odd[w * quarter:(w + 1) * quarter]
        mean = (jnp.sum(part_e, axis=0, keepdims=True) + jnp.sum(part_o, axis=0, keepdims=True)) / (2 * quarter)
        diff_e = part_e - mean
        diff_o = part_o - mean
        spread = (jnp.sum(diff_e * diff_e, axis=0, keepdims=True) + jnp.sum(diff_o * diff_o, axis=0, keepdims=True)) / (2 * quarter)
        place = group_rank(perm_ref, step * windows + w, all_windows, cols)
        stat_ref[pl.ds(place, 1), 0:channels] = mean
        stat_ref[pl.ds(place, 1), channels:2 * channels] = spread


def enc1_call(permutation, logs, coef, w_enc1, cols):
    windows, chunks, frames, _ = logs.shape
    channels = w_enc1.shape[1]
    rows = windows * frames // 4
    grid_spec = pltpu.PrefetchScalarGridSpec(
        num_scalar_prefetch=1,
        grid=(windows // STEP_WINDOWS,),
        in_specs=[ON_CHIP, pl.BlockSpec((LANES, LANES), lambda i, p: (0, 0)), ON_CHIP],
        out_specs=[ON_CHIP] * 3,
        scratch_shapes=[pltpu.VMEM((LANES, LANES), F32)],
    )
    return pl.pallas_call(
        functools.partial(enc1_kernel, cols=cols),
        grid_spec=grid_spec,
        out_shape=[
            pltpu.VMEM((4, rows, chunks * LANES), BF16),
            pltpu.VMEM((2, rows, channels), F32),
            pltpu.VMEM((windows, 2 * channels), F32),
        ],
        compiler_params=pltpu.CompilerParams(vmem_limit_bytes=16 * MIB),
        name="normalize_enc1",
    )(permutation, on_chip(logs), coef, on_chip(w_enc1))


def window_rows(perm_ref, table, step, windows, quarter, all_windows, cols, first, last):
    parts = []
    for w in range(windows):
        place = group_rank(perm_ref, step * windows + w, all_windows, cols)
        parts.append(jnp.broadcast_to(table[pl.ds(place, 1), first:last], (quarter, last - first)))
    return jnp.concatenate(parts, axis=0)


def write_halves(core_ref, grads, own_ref, send_ref, bounds):
    for first, last in zip(bounds[:-1], bounds[1:]):
        half = (last - first) // 2
        at = first // 2
        own = pl.multiple_of(first + core_ref[0] * half, half)
        send = pl.multiple_of(first + (1 - core_ref[0]) * half, half)
        own_ref[at:at + half, :] = grads[pl.ds(own, half), :]
        send_ref[at:at + half, :] = grads[pl.ds(send, half), :]


def middle_kernel(perm_ref, core_ref, normed_ref, pre_ref, stat_ref, v_ref, b_ref, c_ref,
                  own_ref, send_ref, back_ref, moment_ref, sums_ref,
                  grads, moment, *, quarter, cols, total_windows):
    step = pl.program_id(0)
    channels = v_ref.shape[1]
    bins = normed_ref.shape[2]
    windows = STEP_WINDOWS
    normed_ref, pre_ref, back_ref = (step_rows(ref, windows * quarter) for ref in (normed_ref, pre_ref, back_ref))
    all_windows = windows * pl.num_programs(0)
    ch = channels

    @pl.when(step == 0)
    def _():
        means = stat_ref[:, :, 0:ch]
        mean = jnp.mean(means, axis=0)
        diff = means - mean[None]
        variance = jnp.mean(stat_ref[:, :, ch:2 * ch] + diff * diff, axis=0)
        moment[:, 0:ch] = mean
        moment[:, ch:2 * ch] = lax.rsqrt(variance + EPS)
        moment_ref[...] = moment[...]
        grads[...] = jnp.zeros_like(grads)

    mean = window_rows(perm_ref, moment, step, windows, quarter, all_windows, cols, 0, ch)
    inverse = window_rows(perm_ref, moment, step, windows, quarter, all_windows, cols, ch, 2 * ch)
    hat_e = (pre_ref[0] - mean) * inverse
    hat_o = (pre_ref[1] - mean) * inverse
    a_e = (hat_e * sigmoid(hat_e)).astype(BF16)
    a_o = (hat_o * sigmoid(hat_o)).astype(BF16)
    v0, v1, v2, v3 = (v_ref[k * ch:(k + 1) * ch, :] for k in range(4))
    pre2 = shift_down(dot(a_o, v0), quarter) + dot(a_e, v1) + dot(a_o, v2) + shift_up(dot(a_e, v3), quarter)
    gate2 = sigmoid(pre2)
    h32 = (pre2 * gate2).astype(BF16).astype(F32)
    h = h32.astype(BF16)
    b0, b1, b2, b3 = (b_ref[:, k * ch:(k + 1) * ch] for k in range(4))
    d1_e = dot(h, b1) + shift_down(dot(h, b3), quarter)
    d1_o = dot(h, b2) + shift_up(dot(h, b0), quarter)
    gate_e = sigmoid(d1_e)
    gate_o = sigmoid(d1_o)
    de32 = (d1_e * gate_e)
    do32 = (d1_o * gate_o)
    de = de32.astype(BF16)
    do = do32.astype(BF16)
    de_up = shift_up(de32, quarter).astype(BF16)
    do_down = shift_down(do32, quarter).astype(BF16)
    c0, c1, c2, c3 = (c_ref[:, k * bins:(k + 1) * bins] for k in range(4))

    def delta(rebuilt, i):
        return ((rebuilt - normed_ref[i].astype(F32)) / total_windows).astype(BF16)

    g0 = delta(dot(de, c1) + dot(do_down, c3), 0)
    g1 = delta(dot(de, c2) + dot(do, c0), 1)
    g2 = delta(dot(do, c1) + dot(de, c3), 2)
    g3 = delta(dot(do, c2) + dot(de_up, c0), 3)
    halves = bins // ch
    base_b = 4 * bins
    base_v = base_b + 4 * ch

    def add_c(k, value):
        for j in range(halves):
            at = (k * halves + j) * ch
            grads[at:at + ch, :] += value[:, j * ch:(j + 1) * ch]

    add_c(0, dot_tn(de_up, g3) + dot_tn(do, g1))
    add_c(1, dot_tn(de, g0) + dot_tn(do, g2))
    add_c(2, dot_tn(de, g1) + dot_tn(do, g3))
    add_c(3, dot_tn(de, g2) + dot_tn(do_down, g0))
    back_e = shift_down(dot_nt(g3, c0), quarter) + dot_nt(g0, c1) + dot_nt(g1, c2) + dot_nt(g2, c3)
    back_o = dot_nt(g1, c0) + dot_nt(g2, c1) + dot_nt(g3, c2) + shift_up(dot_nt(g0, c3), quarter)
    dd_e = (back_e * (gate_e * (1.0 + d1_e * (1.0 - gate_e)))).astype(BF16)
    dd_o = (back_o * (gate_o * (1.0 + d1_o * (1.0 - gate_o)))).astype(BF16)
    h_up = shift_up(h32, quarter).astype(BF16)
    h_down = shift_down(h32, quarter).astype(BF16)
    grads[base_b:base_b + ch, :] += dot_tn(h_up, dd_o)
    grads[base_b + ch:base_b + 2 * ch, :] += dot_tn(h, dd_e)
    grads[base_b + 2 * ch:base_b + 3 * ch, :] += dot_tn(h, dd_o)
    grads[base_b + 3 * ch:base_b + 4 * ch, :] += dot_tn(h_down, dd_e)
    back2 = shift_down(dot_nt(dd_o, b0), quarter) + dot_nt(dd_e, b1) + dot_nt(dd_o, b2) + shift_up(dot_nt(dd_e, b3), quarter)
    d2_32 = (back2 * (gate2 * (1.0 + pre2 * (1.0 - gate2)))).astype(BF16).astype(F32)
    d2 = d2_32.astype(BF16)
    d2_up = shift_up(d2_32, quarter).astype(BF16)
    d2_down = shift_down(d2_32, quarter).astype(BF16)
    grads[base_v:base_v + ch, :] += dot_tn(a_o, d2_up)
    grads[base_v + ch:base_v + 2 * ch, :] += dot_tn(a_e, d2)
    grads[base_v + 2 * ch:base_v + 3 * ch, :] += dot_tn(a_o, d2)
    grads[base_v + 3 * ch:base_v + 4 * ch, :] += dot_tn(a_e, d2_down)
    fold_e = dot_nt(d2, v1) + shift_down(dot_nt(d2, v3), quarter)
    fold_o = dot_nt(d2, v2) + shift_up(dot_nt(d2, v0), quarter)
    gate_he = sigmoid(hat_e)
    gate_ho = sigmoid(hat_o)
    fold_e = fold_e * (gate_he * (1.0 + hat_e * (1.0 - gate_he)))
    fold_o = fold_o * (gate_ho * (1.0 + hat_o * (1.0 - gate_ho)))
    back_ref[0] = fold_e
    back_ref[1] = fold_o
    cross_e = fold_e * hat_e
    cross_o = fold_o * hat_o
    for w in range(windows):
        low, high = w * quarter, (w + 1) * quarter
        first = jnp.sum(fold_e[low:high] + fold_o[low:high], axis=0, keepdims=True)
        second = jnp.sum(cross_e[low:high] + cross_o[low:high], axis=0, keepdims=True)
        place = group_rank(perm_ref, step * windows + w, all_windows, cols)
        sums_ref[pl.ds(place, 1), 0:ch] = first
        sums_ref[pl.ds(place, 1), ch:2 * ch] = second

    @pl.when(step == pl.num_programs(0) - 1)
    def _():
        write_halves(core_ref, grads, own_ref, send_ref, (0, base_b, base_v, base_v + 4 * ch))


def middle_call(permutation, core, normed, pre, stat, w_enc2, w_dec1, w_dec2, quarter, cols, total_windows):
    bins = normed.shape[2]
    channels = w_enc2.shape[1]
    windows = normed.shape[1] // quarter
    total = 4 * bins + 8 * channels
    whole2 = lambda i, p, c: (0, 0)
    grid_spec = pltpu.PrefetchScalarGridSpec(
        num_scalar_prefetch=2,
        grid=(windows // STEP_WINDOWS,),
        in_specs=[
            ON_CHIP,
            ON_CHIP,
            ON_CHIP,
            ON_CHIP,
            ON_CHIP,
            ON_CHIP,
        ],
        out_specs=[
            ON_CHIP,
            ON_CHIP,
            ON_CHIP,
            pl.BlockSpec((windows, 2 * channels), whole2),
            ON_CHIP,
        ],
        scratch_shapes=[
            pltpu.VMEM((total, channels), F32),
            pltpu.VMEM((windows, 2 * channels), F32),
        ],
    )
    return pl.pallas_call(
        functools.partial(middle_kernel, quarter=quarter, cols=cols, total_windows=float(total_windows)),
        grid_spec=grid_spec,
        out_shape=[
            pltpu.VMEM((total // 2, channels), F32),
            pltpu.VMEM((total // 2, channels), F32),
            pltpu.VMEM(pre.shape, F32),
            jax.ShapeDtypeStruct((windows, 2 * channels), F32),
            pltpu.VMEM((windows, 2 * channels), F32),
        ],
        compiler_params=pltpu.CompilerParams(vmem_limit_bytes=30 * MIB),
        name="middle",
    )(permutation, core, on_chip(normed), on_chip(pre), on_chip(stat), on_chip(w_enc2), on_chip(w_dec1), on_chip(w_dec2))


def grad_kernel(perm_ref, core_ref, normed_ref, pre_ref, back_ref, moment_ref, sums_ref, own_ref, send_ref, grads, scale, *, quarter, cols):
    step = pl.program_id(0)
    bins = normed_ref.shape[2]
    ch = pre_ref.shape[2]
    windows = STEP_WINDOWS
    rows = windows * quarter
    normed_ref = step_rows(normed_ref, rows)
    pre_ref, back_ref = step_rows(pre_ref, rows), step_rows(back_ref, rows)
    all_windows = windows * pl.num_programs(0)

    @pl.when(step == 0)
    def _():
        scale[...] = jnp.sum(sums_ref[...], axis=0) / (2.0 * quarter * cols)
        grads[...] = jnp.zeros_like(grads)

    pick = functools.partial(window_rows, perm_ref, step=step, windows=windows, quarter=quarter, all_windows=all_windows, cols=cols)
    mean = pick(table=moment_ref, first=0, last=ch)
    inverse = pick(table=moment_ref, first=ch, last=2 * ch)
    first = pick(table=scale, first=0, last=ch)
    second = pick(table=scale, first=ch, last=2 * ch)
    hat_e = (pre_ref[0] - mean) * inverse
    hat_o = (pre_ref[1] - mean) * inverse
    de32 = (back_ref[0] - first - hat_e * second) * inverse
    do32 = (back_ref[1] - first - hat_o * second) * inverse
    de = de32.astype(BF16)
    do = do32.astype(BF16)
    de_up = shift_up(de32, quarter).astype(BF16)
    do_down = shift_down(do32, quarter).astype(BF16)
    f0, f1, f2, f3 = (normed_ref[i] for i in range(4))
    grads[0:bins, :] += dot_tn(f3, de_up) + dot_tn(f1, do)
    grads[bins:2 * bins, :] += dot_tn(f0, de) + dot_tn(f2, do)
    grads[2 * bins:3 * bins, :] += dot_tn(f1, de) + dot_tn(f3, do)
    grads[3 * bins:4 * bins, :] += dot_tn(f2, de) + dot_tn(f0, do_down)

    @pl.when(step == pl.num_programs(0) - 1)
    def _():
        write_halves(core_ref, grads, own_ref, send_ref, (0, 4 * bins))


def grad_call(permutation, core, normed, pre, back, moment, sums, quarter, cols):
    bins = normed.shape[2]
    channels = pre.shape[2]
    windows = normed.shape[1] // quarter
    grid_spec = pltpu.PrefetchScalarGridSpec(
        num_scalar_prefetch=2,
        grid=(windows // STEP_WINDOWS,),
        in_specs=[
            ON_CHIP,
            ON_CHIP,
            ON_CHIP,
            pl.BlockSpec(moment.shape, lambda i, p, c: (0, 0)),
            ON_CHIP,
        ],
        out_specs=[ON_CHIP] * 2,
        scratch_shapes=[pltpu.VMEM((4 * bins, channels), F32), pltpu.VMEM((windows, 2 * channels), F32)],
    )
    return pl.pallas_call(
        functools.partial(grad_kernel, quarter=quarter, cols=cols),
        grid_spec=grid_spec,
        out_shape=[pltpu.VMEM((2 * bins, channels), F32)] * 2,
        compiler_params=pltpu.CompilerParams(vmem_limit_bytes=16 * MIB),
        name="grad_enc1",
    )(permutation, core, on_chip(normed), on_chip(pre), on_chip(back), moment, on_chip(sums))


def swap_cores(values):
    return lax.ppermute(values, "core", [(0, 1), (1, 0)])


def exchange(values, axes):
    return lax.all_to_all(values, axes, split_axis=0, concat_axis=0, tiled=True)


def join_kernel(mine_ref, other_ref, out_ref, *, moments):
    mine, other = mine_ref[...], other_ref[...]
    total = mine + other
    width = total.shape[1] // 2
    if moments:
        apart = 0.5 * (mine[:, 0:width] - other[:, 0:width])
        total = jnp.concatenate([0.5 * total[:, 0:width], 0.5 * total[:, width:] + apart * apart], axis=1)
    for d in range(out_ref.shape[0]):
        out_ref[d] = total


def join_cores(mine, chips, moments):
    rows, width = mine.shape
    return pl.pallas_call(
        functools.partial(join_kernel, moments=moments),
        in_specs=[ON_CHIP] * 2,
        out_specs=ON_CHIP,
        out_shape=pltpu.VMEM((chips, rows, width), F32),
        compiler_params=pltpu.CompilerParams(vmem_limit_bytes=2 * MIB),
        name="join_cores",
    )(on_chip(mine), on_chip(swap_cores(mine)))


def exchange_copies(copies):
    return exchange(copies.reshape(-1, copies.shape[2]), "pair").reshape(copies.shape)


def chip_sums(parts, axes, chips):
    total = [(own + swap_cores(send)).astype(BF16).reshape(chips, -1, own.shape[1]) for own, send in parts]
    total = jnp.concatenate(total, axis=1)
    return exchange(total.reshape(-1, total.shape[2]), axes).reshape(total.shape)


def owner_kernel(in_ref, out_ref):
    chips, rows, width = in_ref.shape

    def body(i, total):
        return total + in_ref[i].astype(F32)

    total = lax.fori_loop(0, chips, body, jnp.zeros((rows, width), F32), unroll=4)
    largest = jnp.max(jnp.max(jnp.abs(total), axis=0, keepdims=True), axis=1, keepdims=True)
    exponent = jnp.clip(jnp.ceil(jnp.log2(largest)), -110.0, 126.0)
    total = total * jnp.exp2(14.0 - exponent)
    for k in range(width // LANES):
        out_ref[k * rows:(k + 1) * rows, :] = total[:, k * LANES:(k + 1) * LANES]
    out_ref[width // LANES * rows:, :] = jnp.broadcast_to(exponent, (SCALE_ROWS, LANES))


def owner_call(pieces):
    chips, rows, width = pieces.shape
    return pl.pallas_call(
        owner_kernel,
        out_shape=jax.ShapeDtypeStruct((width // LANES * rows + SCALE_ROWS, LANES), F32),
        compiler_params=pltpu.CompilerParams(vmem_limit_bytes=6 * MIB),
        name="owner_sum",
    )(pieces)


def gather_rows(piece, axes, chips):
    rows, width = piece.shape
    copies = jnp.broadcast_to(piece.astype(jnp.float16)[None], (chips, rows, width))
    return exchange(copies.reshape(-1, width), axes).reshape(chips, rows, width)


def place_kernel(half_ref, blocks_ref, *refs, rows, cut):
    grad_w_ref, grad_v_ref, grad_b_ref, grad_c_ref = refs[-4:]
    step = pl.program_id(0)
    channels = grad_w_ref.shape[1]
    late = rows - cut
    group = channels // cut

    def copy(out_ref, i, row, column):
        scale = jnp.exp2(blocks_ref[i, 2 * rows:2 * rows + 1, :] - 14.0)
        for k in range(2):
            block = blocks_ref[i, k * rows:(k + 1) * rows, :] * scale
            grad_w_ref[i * late:(i + 1) * late, k * LANES:(k + 1) * LANES] = block[cut:rows]
            out_ref[row:row + cut, column + k * LANES:column + (k + 1) * LANES] = block[0:cut]

    @pl.when(step < 2)
    def _():
        for i in range(2 * group):
            copy(grad_c_ref, i, i % group * cut, i // group * channels)

    @pl.when(step == 2)
    def _():
        for i in range(2 * group):
            copy(grad_b_ref, i, i % group * cut, i // group * channels)

    @pl.when(step == 3)
    def _():
        for i in range(2 * group):
            copy(grad_v_ref, i, i * cut, 0)


def place_call(half, blocks, rows, cut, channels, bins, earlier=()):
    chips, total, _ = blocks.shape
    group = channels // cut
    late = rows - cut
    grid_spec = pltpu.PrefetchScalarGridSpec(
        num_scalar_prefetch=1,
        grid=(4,),
        in_specs=[pl.BlockSpec((2 * group, total, LANES), lambda i, h: (i, 0, 0))]
        + [pl.BlockSpec(memory_space=pl.ANY)] * len(earlier),
        out_specs=[
            pl.BlockSpec((2 * group * late, channels), lambda i, h: (h[0] * 4 + i, 0)),
            pl.BlockSpec((2 * channels, channels), lambda i, h: (h[0], 0)),
            pl.BlockSpec((channels, 2 * channels), lambda i, h: (0, h[0])),
            pl.BlockSpec((channels, 2 * channels), lambda i, h: (0, h[0] * 2 + jnp.minimum(i, 1))),
        ],
    )
    return pl.pallas_call(
        functools.partial(place_kernel, rows=rows, cut=cut),
        grid_spec=grid_spec,
        out_shape=[
            jax.ShapeDtypeStruct((4 * bins, channels), F32),
            jax.ShapeDtypeStruct((4 * channels, channels), F32),
            jax.ShapeDtypeStruct((channels, 4 * channels), F32),
            jax.ShapeDtypeStruct((channels, 4 * bins), F32),
        ],
        input_output_aliases={2 + k: k for k in range(len(earlier))},
        compiler_params=pltpu.CompilerParams(vmem_limit_bytes=16 * MIB),
        cost_estimate=pl.CostEstimate(flops=chips * total * LANES, bytes_accessed=8 * chips * total * LANES, transcendentals=0),
        name="place_gradients",
    )(half, blocks, *earlier)


def local(spectra, sensor_ids, permutation, w_enc1, w_enc2, w_dec1, w_dec2):
    windows, frames, bins = spectra.shape
    channels = w_enc1.shape[1]
    chip_axes = ("row", "pair")
    every = ("row", "pair", "core")
    cols = lax.axis_size("pair") * lax.axis_size("core")
    chips = lax.axis_size("row") * lax.axis_size("pair")
    total_windows = windows * lax.axis_size("row") * cols
    sensors = total_windows // WIN_SENSOR
    chunks = bins // LANES
    quarter = frames // 4
    core_index = lax.axis_index("core")
    core = core_index.astype(jnp.int32).reshape(1)

    logs, sums = sums_call(spectra, sensor_ids)
    sums, core = lax.optimization_barrier((sums, core))
    sums = exchange(sums, every)
    coef = exchange(stats_call(sums, windows, chunks, sensors, WIN_SENSOR * frames), every)
    normed, pre, stat = enc1_call(permutation, logs, coef, w_enc1, cols)
    stat = exchange_copies(join_cores(stat, cols // 2, True))
    own, send, back, moment, moments = middle_call(
        permutation, core, normed, pre, stat, w_enc2, w_dec1, w_dec2, quarter, cols, total_windows)
    moments, send = lax.optimization_barrier((join_cores(moments, cols // 2, False), send))
    moments = exchange_copies(moments)
    late = grad_call(permutation, core, normed, pre, back, moment, moments, quarter, cols)
    piece = owner_call(chip_sums([(own, send), late], chip_axes, chips))
    mine = gather_rows(piece, chip_axes, chips)
    other = swap_cores(mine)
    rows, cut = own.shape[0] // chips + late[0].shape[0] // chips, own.shape[0] // chips
    placed = place_call(core, mine.astype(F32), rows, cut, channels, bins)
    return tuple(place_call(1 - core, other.astype(F32), rows, cut, channels, bins, placed))


def solution(mesh):
    rows, cols = mesh.devices.shape
    inner = Mesh(mesh.devices.reshape(rows, cols // 2, 2), ("row", "pair", "core"))
    spread = ("row", "pair", "core")
    return jax.shard_map(
        local,
        mesh=inner,
        in_specs=(P(spread, None, None), P(spread, None), P(spread), P(), P(), P(), P()),
        out_specs=(P(), P(), P(), P()),
        check_vma=False,
    )
```

```python
import functools

import jax
import jax.numpy as jnp
from jax import lax
from jax.experimental import pallas as pl
from jax.experimental.pallas import tpu as pltpu
from jax.sharding import Mesh, PartitionSpec as P

WIN_SENSOR = 8
EPS = 1e-05
F32 = jnp.float32
BF16 = jnp.bfloat16
LANES = 128
STEP_WINDOWS = 16
SORT_WINDOWS = 8
SCALE_ROWS = 8
MIB = 1024 * 1024


ON_CHIP = pl.BlockSpec(memory_space=pltpu.VMEM)


def on_chip(values):
    return pltpu.with_memory_space_constraint(values, pltpu.VMEM)


def in_hbm(values):
    return pltpu.with_memory_space_constraint(values, pltpu.HBM)


def step_rows(ref, rows):
    return ref.at[:, pl.ds(pl.multiple_of(pl.program_id(0) * rows, rows), rows), :]


def dot(left, right):
    return jnp.dot(left, right, preferred_element_type=F32)


def dot_nt(left, right):
    return lax.dot_general(left, right, (((1,), (1,)), ((), ())), preferred_element_type=F32)


def dot_tn(left, right):
    return lax.dot_general(left, right, (((0,), (0,)), ((), ())), preferred_element_type=F32)


def split3(values):
    first = values.astype(BF16)
    rest = values - first.astype(F32)
    second = rest.astype(BF16)
    third = (rest - second.astype(F32)).astype(BF16)
    return first, second, third


def sigmoid(values):
    return 1.0 / (1.0 + jnp.exp(-values))


def shift_down(values, period):
    rows = lax.broadcasted_iota(jnp.int32, values.shape, 0) % period
    return jnp.where(rows == 0, 0.0, pltpu.roll(values, 1, 0))


def shift_up(values, period):
    total = values.shape[0]
    rows = lax.broadcasted_iota(jnp.int32, values.shape, 0) % period
    return jnp.where(rows == period - 1, 0.0, pltpu.roll(values, total - 1, 0))


def group_rank(perm_ref, window, window_dev, col_count):
    trainer = perm_ref[window] // window_dev
    per_row = 2
    return (trainer // col_count) * per_row + trainer % per_row


def sums_kernel(ids_ref, core_ref, spec_ref, log_ref, own_ref, send_ref, acc, turned, *, chunks, count):
    step = pl.program_id(0)
    windows, frames, bins = spec_ref.shape
    rows = 16

    for w in range(windows):
        def body(i, carry):
            total, square = carry
            start = pl.multiple_of(i * rows, rows)
            value = jnp.log(1.0 + spec_ref[w, pl.ds(start, rows), :].astype(F32))
            for k in range(chunks):
                log_ref[step * windows + w, k, pl.ds(start, rows), :] = value[:, k * LANES:(k + 1) * LANES]
            value_sq = value * value
            return (total + value[0:8] + value[8:16], square + value_sq[0:8] + value_sq[8:16])

        zero = jnp.zeros((8, bins), F32)
        total, square = lax.fori_loop(0, frames // rows, body, (zero, zero), unroll=4)
        total = jnp.sum(total, axis=0, keepdims=True)
        square = jnp.sum(square, axis=0, keepdims=True)
        pieces = [total[:, k * LANES:(k + 1) * LANES] for k in range(chunks)]
        pieces += [square[:, k * LANES:(k + 1) * LANES] for k in range(chunks)]
        start = pl.multiple_of((step * windows + w) * 2 * chunks, 2 * chunks)
        acc[pl.ds(start, 2 * chunks), :] = jnp.concatenate(pieces, axis=0)

    @pl.when(step == pl.num_programs(0) - 1)
    def _():
        half = LANES // 2
        turned[...] = acc[...].T
        own_ref[0:half, :] = turned[pl.ds(pl.multiple_of(core_ref[0] * half, half), half), :]
        send_ref[0:half, :] = turned[pl.ds(pl.multiple_of((1 - core_ref[0]) * half, half), half), :]
        lanes = lax.broadcasted_iota(jnp.int32, (8, LANES), 1)
        ids = jnp.zeros((8, LANES), jnp.int32)
        for w in range(count):
            ids = jnp.where(lanes == w, ids_ref[w], ids)
        own_ref[half:, :] = ids.astype(F32)
        send_ref[half:, :] = ids.astype(F32)


def sums_call(spectra, sensor_ids, core):
    windows, frames, bins = spectra.shape
    chunks = bins // LANES
    grid_spec = pltpu.PrefetchScalarGridSpec(
        num_scalar_prefetch=2,
        grid=(windows // SORT_WINDOWS,),
        in_specs=[pl.BlockSpec((SORT_WINDOWS, frames, bins), lambda i, s, c: (i, 0, 0))],
        out_specs=[ON_CHIP] * 3,
        scratch_shapes=[pltpu.VMEM((LANES, LANES), F32)] * 2,
    )
    return pl.pallas_call(
        functools.partial(sums_kernel, chunks=chunks, count=windows),
        grid_spec=grid_spec,
        out_shape=[
            pltpu.VMEM((windows, chunks, frames, LANES), F32),
            pltpu.VMEM((LANES // 2 + 8, LANES), F32),
            pltpu.VMEM((LANES // 2 + 8, LANES), F32),
        ],
        compiler_params=pltpu.CompilerParams(vmem_limit_bytes=10 * MIB),
        name="log_and_sum",
    )(in_hbm(sensor_ids.reshape(windows)), core, in_hbm(spectra))


def pack_kernel(mine_ref, other_ref, out_ref, *, count):
    half = LANES // 2
    out_ref[pl.ds(0, half, stride=4), :] = mine_ref[0:half, :]
    out_ref[pl.ds(1, half, stride=4), :] = other_ref[0:half, :]
    ids = mine_ref[half:half + 8, :] + pltpu.roll(other_ref[half:half + 8, :], count, 1)
    out_ref[pl.ds(2, half, stride=4), :] = jnp.broadcast_to(ids[0:1, :], (half, LANES))
    out_ref[pl.ds(3, half, stride=4), :] = jnp.zeros((half, LANES), F32)


def pack_call(mine, other, count):
    return pl.pallas_call(
        functools.partial(pack_kernel, count=count),
        in_specs=[ON_CHIP] * 2,
        out_specs=ON_CHIP,
        out_shape=pltpu.VMEM((2 * LANES, LANES), F32),
        compiler_params=pltpu.CompilerParams(vmem_limit_bytes=2 * MIB),
        name="pack_sums",
    )(on_chip(mine), on_chip(other))


def stats_kernel(in_ref, out_ref, *, windows, chunks, sensors, per_sensor):
    width = 2 * chunks
    half = LANES // 2
    data = jnp.concatenate([in_ref[pl.ds(n, half, stride=4), :] for n in range(2)], axis=0).T
    ids = in_ref[pl.ds(2, half, stride=4), :].T
    labels = jnp.concatenate([ids[0:windows], ids[windows:2 * windows]], axis=1)
    sensor_rows = lax.broadcasted_iota(jnp.int32, (sensors, LANES), 0).astype(F32)
    tables = [(sensor_rows == labels[w:w + 1, :]).astype(F32).astype(BF16) for w in range(windows)]
    table = jnp.concatenate(tables, axis=1)
    values = jnp.concatenate([data[w * width:(w + 1) * width, :] for w in range(windows)], axis=1)
    parts = dot_nt(jnp.concatenate(split3(values), axis=0), table)
    sums = parts[0:width] + parts[width:2 * width] + parts[2 * width:3 * width]
    center = sums[0:chunks] / per_sensor
    factor = lax.rsqrt(sums[chunks:width] / per_sensor - center * center + EPS)
    both = jnp.concatenate([center, factor], axis=0)
    back = dot(jnp.concatenate(split3(both), axis=0), table)
    back = back[0:width] + back[width:2 * width] + back[2 * width:3 * width]
    rows = jnp.concatenate([back[:, w * LANES:(w + 1) * LANES] for w in range(windows)], axis=0)
    rows = rows.T
    for n in range(2):
        out_ref[pl.ds(n, half, stride=2), :] = rows[n * half:(n + 1) * half]


def stats_call(received, windows, chunks, sensors, per_sensor):
    return pl.pallas_call(
        functools.partial(stats_kernel, windows=windows, chunks=chunks, sensors=sensors, per_sensor=float(per_sensor)),
        out_shape=jax.ShapeDtypeStruct((LANES, LANES), F32),
        compiler_params=pltpu.CompilerParams(vmem_limit_bytes=12 * MIB),
        name="sensor_stats",
    )(received)


def enc1_kernel(perm_ref, core_ref, log_ref, coef_ref, other_ref, w_ref, normed_ref, pre_ref, stat_ref, coef, *, cols):
    step = pl.program_id(0)
    all_windows, chunks, frames, _ = log_ref.shape
    quarter = frames // 4
    bins = chunks * LANES
    windows = STEP_WINDOWS
    normed_ref, pre_ref = (step_rows(ref, windows * quarter) for ref in (normed_ref, pre_ref))
    channels = w_ref.shape[1]
    width = 2 * chunks

    @pl.when(step == 0)
    def _():
        half = LANES // 2
        own = pl.multiple_of(core_ref[0] * half, half)
        coef[pl.ds(own, half), :] = coef_ref[pl.ds(0, half, stride=2), :]
        coef[pl.ds(half - own, half), :] = other_ref[pl.ds(1, half, stride=2), :]
        coef[...] = coef[...].T

    for w in range(windows):
        start = pl.multiple_of((step * windows + w) * width, width)
        both = coef[pl.ds(start, width), :]
        low, high = w * quarter, (w + 1) * quarter
        for k in range(chunks):
            center = both[k:k + 1, :]
            factor = both[chunks + k:chunks + k + 1, :]
            for i in range(4):
                value = log_ref[step * windows + w, k, pl.ds(i, quarter, stride=4), :]
                normed_ref[i, low:high, k * LANES:(k + 1) * LANES] = ((value - center) * factor).astype(BF16)

    w0, w1, w2, w3 = (w_ref[k * bins:(k + 1) * bins, :] for k in range(4))
    f0, f1, f2, f3 = (normed_ref[i] for i in range(4))
    even = shift_down(dot(f3, w0), quarter) + dot(f0, w1) + dot(f1, w2) + dot(f2, w3)
    odd = dot(f1, w0) + dot(f2, w1) + dot(f3, w2) + shift_up(dot(f0, w3), quarter)
    pre_ref[0] = even
    pre_ref[1] = odd
    for w in range(windows):
        part_e = even[w * quarter:(w + 1) * quarter]
        part_o = odd[w * quarter:(w + 1) * quarter]
        mean = (jnp.sum(part_e, axis=0, keepdims=True) + jnp.sum(part_o, axis=0, keepdims=True)) / (2 * quarter)
        diff_e = part_e - mean
        diff_o = part_o - mean
        spread = (jnp.sum(diff_e * diff_e, axis=0, keepdims=True) + jnp.sum(diff_o * diff_o, axis=0, keepdims=True)) / (2 * quarter)
        place = group_rank(perm_ref, step * windows + w, all_windows, cols)
        stat_ref[pl.ds(place, 1), 0:channels] = mean
        stat_ref[pl.ds(place, 1), channels:2 * channels] = spread


def enc1_call(permutation, core, logs, coef, other, w_enc1, cols):
    windows, chunks, frames, _ = logs.shape
    channels = w_enc1.shape[1]
    rows = windows * frames // 4
    grid_spec = pltpu.PrefetchScalarGridSpec(
        num_scalar_prefetch=2,
        grid=(windows // STEP_WINDOWS,),
        in_specs=[ON_CHIP] * 4,
        out_specs=[ON_CHIP] * 3,
        scratch_shapes=[pltpu.VMEM((LANES, LANES), F32)],
    )
    return pl.pallas_call(
        functools.partial(enc1_kernel, cols=cols),
        grid_spec=grid_spec,
        out_shape=[
            pltpu.VMEM((4, rows, chunks * LANES), BF16),
            pltpu.VMEM((2, rows, channels), F32),
            pltpu.VMEM((windows, 2 * channels), F32),
        ],
        compiler_params=pltpu.CompilerParams(vmem_limit_bytes=16 * MIB),
        name="normalize_enc1",
    )(permutation, core, on_chip(logs), on_chip(coef), on_chip(other), on_chip(w_enc1))


def window_rows(perm_ref, table, step, windows, quarter, all_windows, cols, first, last):
    parts = []
    for w in range(windows):
        place = group_rank(perm_ref, step * windows + w, all_windows, cols)
        parts.append(jnp.broadcast_to(table[pl.ds(place, 1), first:last], (quarter, last - first)))
    return jnp.concatenate(parts, axis=0)


def write_halves(core_ref, grads, own_ref, send_ref, bounds):
    for first, last in zip(bounds[:-1], bounds[1:]):
        half = (last - first) // 2
        at = first // 2
        own = pl.multiple_of(first + core_ref[0] * half, half)
        send = pl.multiple_of(first + (1 - core_ref[0]) * half, half)
        own_ref[at:at + half, :] = grads[pl.ds(own, half), :]
        send_ref[at:at + half, :] = grads[pl.ds(send, half), :]


def middle_kernel(perm_ref, core_ref, normed_ref, pre_ref, stat_ref, v_ref, b_ref, c_ref,
                  own_ref, send_ref, back_ref, moment_ref, sums_ref,
                  grads, moment, *, quarter, cols, total_windows):
    step = pl.program_id(0)
    channels = v_ref.shape[1]
    bins = normed_ref.shape[2]
    windows = STEP_WINDOWS
    normed_ref, pre_ref, back_ref = (step_rows(ref, windows * quarter) for ref in (normed_ref, pre_ref, back_ref))
    all_windows = windows * pl.num_programs(0)
    ch = channels

    @pl.when(step == 0)
    def _():
        means = stat_ref[:, :, 0:ch]
        mean = jnp.mean(means, axis=0)
        diff = means - mean[None]
        variance = jnp.mean(stat_ref[:, :, ch:2 * ch] + diff * diff, axis=0)
        moment[:, 0:ch] = mean
        moment[:, ch:2 * ch] = lax.rsqrt(variance + EPS)
        moment_ref[...] = moment[...]
        grads[...] = jnp.zeros_like(grads)

    mean = window_rows(perm_ref, moment, step, windows, quarter, all_windows, cols, 0, ch)
    inverse = window_rows(perm_ref, moment, step, windows, quarter, all_windows, cols, ch, 2 * ch)
    hat_e = (pre_ref[0] - mean) * inverse
    hat_o = (pre_ref[1] - mean) * inverse
    a_e = (hat_e * sigmoid(hat_e)).astype(BF16)
    a_o = (hat_o * sigmoid(hat_o)).astype(BF16)
    v0, v1, v2, v3 = (v_ref[k * ch:(k + 1) * ch, :] for k in range(4))
    pre2 = shift_down(dot(a_o, v0), quarter) + dot(a_e, v1) + dot(a_o, v2) + shift_up(dot(a_e, v3), quarter)
    gate2 = sigmoid(pre2)
    h32 = (pre2 * gate2).astype(BF16).astype(F32)
    h = h32.astype(BF16)
    b0, b1, b2, b3 = (b_ref[:, k * ch:(k + 1) * ch] for k in range(4))
    d1_e = dot(h, b1) + shift_down(dot(h, b3), quarter)
    d1_o = dot(h, b2) + shift_up(dot(h, b0), quarter)
    gate_e = sigmoid(d1_e)
    gate_o = sigmoid(d1_o)
    de32 = (d1_e * gate_e)
    do32 = (d1_o * gate_o)
    de = de32.astype(BF16)
    do = do32.astype(BF16)
    de_up = shift_up(de32, quarter).astype(BF16)
    do_down = shift_down(do32, quarter).astype(BF16)
    c0, c1, c2, c3 = (c_ref[:, k * bins:(k + 1) * bins] for k in range(4))

    def delta(rebuilt, i):
        return ((rebuilt - normed_ref[i].astype(F32)) / total_windows).astype(BF16)

    g0 = delta(dot(de, c1) + dot(do_down, c3), 0)
    g1 = delta(dot(de, c2) + dot(do, c0), 1)
    g2 = delta(dot(do, c1) + dot(de, c3), 2)
    g3 = delta(dot(do, c2) + dot(de_up, c0), 3)
    halves = bins // ch
    base_b = 4 * bins
    base_v = base_b + 4 * ch

    def add_c(k, value):
        for j in range(halves):
            at = (k * halves + j) * ch
            grads[at:at + ch, :] += value[:, j * ch:(j + 1) * ch]

    add_c(0, dot_tn(de_up, g3) + dot_tn(do, g1))
    add_c(1, dot_tn(de, g0) + dot_tn(do, g2))
    add_c(2, dot_tn(de, g1) + dot_tn(do, g3))
    add_c(3, dot_tn(de, g2) + dot_tn(do_down, g0))
    back_e = shift_down(dot_nt(g3, c0), quarter) + dot_nt(g0, c1) + dot_nt(g1, c2) + dot_nt(g2, c3)
    back_o = dot_nt(g1, c0) + dot_nt(g2, c1) + dot_nt(g3, c2) + shift_up(dot_nt(g0, c3), quarter)
    dd_e = (back_e * (gate_e * (1.0 + d1_e * (1.0 - gate_e)))).astype(BF16)
    dd_o = (back_o * (gate_o * (1.0 + d1_o * (1.0 - gate_o)))).astype(BF16)
    h_up = shift_up(h32, quarter).astype(BF16)
    h_down = shift_down(h32, quarter).astype(BF16)
    grads[base_b:base_b + ch, :] += dot_tn(h_up, dd_o)
    grads[base_b + ch:base_b + 2 * ch, :] += dot_tn(h, dd_e)
    grads[base_b + 2 * ch:base_b + 3 * ch, :] += dot_tn(h, dd_o)
    grads[base_b + 3 * ch:base_b + 4 * ch, :] += dot_tn(h_down, dd_e)
    back2 = shift_down(dot_nt(dd_o, b0), quarter) + dot_nt(dd_e, b1) + dot_nt(dd_o, b2) + shift_up(dot_nt(dd_e, b3), quarter)
    d2_32 = (back2 * (gate2 * (1.0 + pre2 * (1.0 - gate2)))).astype(BF16).astype(F32)
    d2 = d2_32.astype(BF16)
    d2_up = shift_up(d2_32, quarter).astype(BF16)
    d2_down = shift_down(d2_32, quarter).astype(BF16)
    grads[base_v:base_v + ch, :] += dot_tn(a_o, d2_up)
    grads[base_v + ch:base_v + 2 * ch, :] += dot_tn(a_e, d2)
    grads[base_v + 2 * ch:base_v + 3 * ch, :] += dot_tn(a_o, d2)
    grads[base_v + 3 * ch:base_v + 4 * ch, :] += dot_tn(a_e, d2_down)
    fold_e = dot_nt(d2, v1) + shift_down(dot_nt(d2, v3), quarter)
    fold_o = dot_nt(d2, v2) + shift_up(dot_nt(d2, v0), quarter)
    gate_he = sigmoid(hat_e)
    gate_ho = sigmoid(hat_o)
    fold_e = fold_e * (gate_he * (1.0 + hat_e * (1.0 - gate_he)))
    fold_o = fold_o * (gate_ho * (1.0 + hat_o * (1.0 - gate_ho)))
    back_ref[0] = fold_e
    back_ref[1] = fold_o
    cross_e = fold_e * hat_e
    cross_o = fold_o * hat_o
    for w in range(windows):
        low, high = w * quarter, (w + 1) * quarter
        first = jnp.sum(fold_e[low:high] + fold_o[low:high], axis=0, keepdims=True)
        second = jnp.sum(cross_e[low:high] + cross_o[low:high], axis=0, keepdims=True)
        place = group_rank(perm_ref, step * windows + w, all_windows, cols)
        sums_ref[pl.ds(place, 1), 0:ch] = first
        sums_ref[pl.ds(place, 1), ch:2 * ch] = second

    @pl.when(step == pl.num_programs(0) - 1)
    def _():
        write_halves(core_ref, grads, own_ref, send_ref, (0, base_b, base_v, base_v + 4 * ch))


def middle_call(permutation, core, normed, pre, stat, w_enc2, w_dec1, w_dec2, quarter, cols, total_windows):
    bins = normed.shape[2]
    channels = w_enc2.shape[1]
    windows = normed.shape[1] // quarter
    total = 4 * bins + 8 * channels
    whole2 = lambda i, p, c: (0, 0)
    grid_spec = pltpu.PrefetchScalarGridSpec(
        num_scalar_prefetch=2,
        grid=(windows // STEP_WINDOWS,),
        in_specs=[
            ON_CHIP,
            ON_CHIP,
            ON_CHIP,
            ON_CHIP,
            ON_CHIP,
            ON_CHIP,
        ],
        out_specs=[
            ON_CHIP,
            ON_CHIP,
            ON_CHIP,
            pl.BlockSpec((windows, 2 * channels), whole2),
            ON_CHIP,
        ],
        scratch_shapes=[
            pltpu.VMEM((total, channels), F32),
            pltpu.VMEM((windows, 2 * channels), F32),
        ],
    )
    return pl.pallas_call(
        functools.partial(middle_kernel, quarter=quarter, cols=cols, total_windows=float(total_windows)),
        grid_spec=grid_spec,
        out_shape=[
            pltpu.VMEM((total // 2, channels), F32),
            pltpu.VMEM((total // 2, channels), F32),
            pltpu.VMEM(pre.shape, F32),
            jax.ShapeDtypeStruct((windows, 2 * channels), F32),
            pltpu.VMEM((windows, 2 * channels), F32),
        ],
        compiler_params=pltpu.CompilerParams(vmem_limit_bytes=30 * MIB),
        name="middle",
    )(permutation, core, on_chip(normed), on_chip(pre), on_chip(stat), on_chip(w_enc2), on_chip(w_dec1), on_chip(w_dec2))


def grad_kernel(perm_ref, core_ref, normed_ref, pre_ref, back_ref, moment_ref, sums_ref, own_ref, send_ref, grads, scale, *, quarter, cols):
    step = pl.program_id(0)
    bins = normed_ref.shape[2]
    ch = pre_ref.shape[2]
    windows = STEP_WINDOWS
    rows = windows * quarter
    normed_ref = step_rows(normed_ref, rows)
    pre_ref, back_ref = step_rows(pre_ref, rows), step_rows(back_ref, rows)
    all_windows = windows * pl.num_programs(0)

    @pl.when(step == 0)
    def _():
        scale[...] = jnp.sum(sums_ref[...], axis=0) / (2.0 * quarter * cols)
        grads[...] = jnp.zeros_like(grads)

    pick = functools.partial(window_rows, perm_ref, step=step, windows=windows, quarter=quarter, all_windows=all_windows, cols=cols)
    mean = pick(table=moment_ref, first=0, last=ch)
    inverse = pick(table=moment_ref, first=ch, last=2 * ch)
    first = pick(table=scale, first=0, last=ch)
    second = pick(table=scale, first=ch, last=2 * ch)
    hat_e = (pre_ref[0] - mean) * inverse
    hat_o = (pre_ref[1] - mean) * inverse
    de32 = (back_ref[0] - first - hat_e * second) * inverse
    do32 = (back_ref[1] - first - hat_o * second) * inverse
    de = de32.astype(BF16)
    do = do32.astype(BF16)
    de_up = shift_up(de32, quarter).astype(BF16)
    do_down = shift_down(do32, quarter).astype(BF16)
    f0, f1, f2, f3 = (normed_ref[i] for i in range(4))
    grads[0:bins, :] += dot_tn(f3, de_up) + dot_tn(f1, do)
    grads[bins:2 * bins, :] += dot_tn(f0, de) + dot_tn(f2, do)
    grads[2 * bins:3 * bins, :] += dot_tn(f1, de) + dot_tn(f3, do)
    grads[3 * bins:4 * bins, :] += dot_tn(f2, de) + dot_tn(f0, do_down)

    @pl.when(step == pl.num_programs(0) - 1)
    def _():
        write_halves(core_ref, grads, own_ref, send_ref, (0, 4 * bins))


def grad_call(permutation, core, normed, pre, back, moment, sums, quarter, cols):
    bins = normed.shape[2]
    channels = pre.shape[2]
    windows = normed.shape[1] // quarter
    grid_spec = pltpu.PrefetchScalarGridSpec(
        num_scalar_prefetch=2,
        grid=(windows // STEP_WINDOWS,),
        in_specs=[
            ON_CHIP,
            ON_CHIP,
            ON_CHIP,
            pl.BlockSpec(moment.shape, lambda i, p, c: (0, 0)),
            ON_CHIP,
        ],
        out_specs=[ON_CHIP] * 2,
        scratch_shapes=[pltpu.VMEM((4 * bins, channels), F32), pltpu.VMEM((windows, 2 * channels), F32)],
    )
    return pl.pallas_call(
        functools.partial(grad_kernel, quarter=quarter, cols=cols),
        grid_spec=grid_spec,
        out_shape=[pltpu.VMEM((2 * bins, channels), F32)] * 2,
        compiler_params=pltpu.CompilerParams(vmem_limit_bytes=16 * MIB),
        name="grad_enc1",
    )(permutation, core, on_chip(normed), on_chip(pre), on_chip(back), moment, on_chip(sums))


def swap_cores(values):
    return lax.ppermute(values, "core", [(0, 1), (1, 0)])


def exchange(values, axes):
    return lax.all_to_all(values, axes, split_axis=0, concat_axis=0, tiled=True)


def join_kernel(mine_ref, other_ref, out_ref, *, moments):
    mine, other = mine_ref[...], other_ref[...]
    total = mine + other
    width = total.shape[1] // 2
    if moments:
        apart = 0.5 * (mine[:, 0:width] - other[:, 0:width])
        total = jnp.concatenate([0.5 * total[:, 0:width], 0.5 * total[:, width:] + apart * apart], axis=1)
    for d in range(out_ref.shape[0]):
        out_ref[d] = total


def join_cores(mine, chips, moments):
    rows, width = mine.shape
    return pl.pallas_call(
        functools.partial(join_kernel, moments=moments),
        in_specs=[ON_CHIP] * 2,
        out_specs=ON_CHIP,
        out_shape=pltpu.VMEM((chips, rows, width), F32),
        compiler_params=pltpu.CompilerParams(vmem_limit_bytes=2 * MIB),
        name="join_cores",
    )(on_chip(mine), on_chip(swap_cores(mine)))


def exchange_copies(copies):
    return exchange(copies.reshape(-1, copies.shape[2]), "pair").reshape(copies.shape)


def chip_sums(parts, axes, chips):
    total = [(own + swap_cores(send)).astype(BF16).reshape(chips, -1, own.shape[1]) for own, send in parts]
    total = jnp.concatenate(total, axis=1)
    return exchange(total.reshape(-1, total.shape[2]), axes).reshape(total.shape)


def owner_kernel(in_ref, out_ref):
    chips, rows, width = in_ref.shape

    def body(i, total):
        return total + in_ref[i].astype(F32)

    total = lax.fori_loop(0, chips, body, jnp.zeros((rows, width), F32), unroll=4)
    largest = jnp.max(jnp.max(jnp.abs(total), axis=0, keepdims=True), axis=1, keepdims=True)
    exponent = jnp.clip(jnp.ceil(jnp.log2(largest)), -110.0, 126.0)
    total = total * jnp.exp2(14.0 - exponent)
    for k in range(width // LANES):
        out_ref[k * rows:(k + 1) * rows, :] = total[:, k * LANES:(k + 1) * LANES]
    out_ref[width // LANES * rows:, :] = jnp.broadcast_to(exponent, (SCALE_ROWS, LANES))


def owner_call(pieces):
    chips, rows, width = pieces.shape
    return pl.pallas_call(
        owner_kernel,
        out_shape=jax.ShapeDtypeStruct((width // LANES * rows + SCALE_ROWS, LANES), F32),
        compiler_params=pltpu.CompilerParams(vmem_limit_bytes=6 * MIB),
        name="owner_sum",
    )(pieces)


def gather_rows(piece, axes, chips):
    rows, width = piece.shape
    copies = jnp.broadcast_to(piece.astype(jnp.float16)[None], (chips, rows, width))
    return exchange(copies.reshape(-1, width), axes).reshape(chips, rows, width)


def place_kernel(half_ref, blocks_ref, *refs, rows, cut):
    grad_w_ref, grad_v_ref, grad_b_ref, grad_c_ref = refs[-4:]
    step = pl.program_id(0)
    channels = grad_w_ref.shape[1]
    late = rows - cut
    group = channels // cut

    def copy(out_ref, i, row, column):
        scale = jnp.exp2(blocks_ref[i, 2 * rows:2 * rows + 1, :] - 14.0)
        for k in range(2):
            block = blocks_ref[i, k * rows:(k + 1) * rows, :] * scale
            grad_w_ref[i * late:(i + 1) * late, k * LANES:(k + 1) * LANES] = block[cut:rows]
            out_ref[row:row + cut, column + k * LANES:column + (k + 1) * LANES] = block[0:cut]

    @pl.when(step < 2)
    def _():
        for i in range(2 * group):
            copy(grad_c_ref, i, i % group * cut, i // group * channels)

    @pl.when(step == 2)
    def _():
        for i in range(2 * group):
            copy(grad_b_ref, i, i % group * cut, i // group * channels)

    @pl.when(step == 3)
    def _():
        for i in range(2 * group):
            copy(grad_v_ref, i, i * cut, 0)


def place_call(half, blocks, rows, cut, channels, bins, earlier=()):
    chips, total, _ = blocks.shape
    group = channels // cut
    late = rows - cut
    grid_spec = pltpu.PrefetchScalarGridSpec(
        num_scalar_prefetch=1,
        grid=(4,),
        in_specs=[pl.BlockSpec((2 * group, total, LANES), lambda i, h: (i, 0, 0))]
        + [pl.BlockSpec(memory_space=pl.ANY)] * len(earlier),
        out_specs=[
            pl.BlockSpec((2 * group * late, channels), lambda i, h: (h[0] * 4 + i, 0)),
            pl.BlockSpec((2 * channels, channels), lambda i, h: (h[0], 0)),
            pl.BlockSpec((channels, 2 * channels), lambda i, h: (0, h[0])),
            pl.BlockSpec((channels, 2 * channels), lambda i, h: (0, h[0] * 2 + jnp.minimum(i, 1))),
        ],
    )
    return pl.pallas_call(
        functools.partial(place_kernel, rows=rows, cut=cut),
        grid_spec=grid_spec,
        out_shape=[
            jax.ShapeDtypeStruct((4 * bins, channels), F32),
            jax.ShapeDtypeStruct((4 * channels, channels), F32),
            jax.ShapeDtypeStruct((channels, 4 * channels), F32),
            jax.ShapeDtypeStruct((channels, 4 * bins), F32),
        ],
        input_output_aliases={2 + k: k for k in range(len(earlier))},
        compiler_params=pltpu.CompilerParams(vmem_limit_bytes=16 * MIB),
        cost_estimate=pl.CostEstimate(flops=chips * total * LANES, bytes_accessed=8 * chips * total * LANES, transcendentals=0),
        name="place_gradients",
    )(half, blocks, *earlier)


def local(spectra, sensor_ids, permutation, w_enc1, w_enc2, w_dec1, w_dec2):
    windows, frames, bins = spectra.shape
    channels = w_enc1.shape[1]
    chip_axes = ("row", "pair")
    cols = lax.axis_size("pair") * lax.axis_size("core")
    chips = lax.axis_size("row") * lax.axis_size("pair")
    total_windows = windows * lax.axis_size("row") * cols
    sensors = total_windows // WIN_SENSOR
    chunks = bins // LANES
    quarter = frames // 4
    core_index = lax.axis_index("core")
    core = core_index.astype(jnp.int32).reshape(1)

    logs, mine, send = sums_call(spectra, sensor_ids, core)
    sums = exchange(pack_call(mine, swap_cores(send), windows), chip_axes)
    coef = exchange(stats_call(sums, windows, chunks, sensors, WIN_SENSOR * frames), chip_axes)
    normed, pre, stat = enc1_call(permutation, core, logs, coef, swap_cores(coef), w_enc1, cols)
    stat = exchange_copies(join_cores(stat, cols // 2, True))
    own, send, back, moment, moments = middle_call(
        permutation, core, normed, pre, stat, w_enc2, w_dec1, w_dec2, quarter, cols, total_windows)
    moments, send = lax.optimization_barrier((join_cores(moments, cols // 2, False), send))
    moments = exchange_copies(moments)
    late = grad_call(permutation, core, normed, pre, back, moment, moments, quarter, cols)
    piece = owner_call(chip_sums([(own, send), late], chip_axes, chips))
    mine = gather_rows(piece, chip_axes, chips)
    other = swap_cores(mine)
    rows, cut = own.shape[0] // chips + late[0].shape[0] // chips, own.shape[0] // chips
    placed = place_call(core, mine.astype(F32), rows, cut, channels, bins)
    return tuple(place_call(1 - core, other.astype(F32), rows, cut, channels, bins, placed))


def solution(mesh):
    rows, cols = mesh.devices.shape
    inner = Mesh(mesh.devices.reshape(rows, cols // 2, 2), ("row", "pair", "core"))
    spread = ("row", "pair", "core")
    return jax.shard_map(
        local,
        mesh=inner,
        in_specs=(P(spread, None, None), P(spread, None), P(spread), P(), P(), P(), P()),
        out_specs=(P(), P(), P(), P()),
        check_vma=False,
    )
```

```python
import functools

import jax
import jax.numpy as jnp
from jax import lax
from jax.experimental import pallas as pl
from jax.experimental.pallas import tpu as pltpu
from jax.sharding import Mesh, PartitionSpec as P

WIN_SENSOR = 8
EPS = 1e-05
F32 = jnp.float32
BF16 = jnp.bfloat16
LANES = 128
STEP_WINDOWS = 16
SORT_WINDOWS = 8
SCALE_ROWS = 8
MIB = 1024 * 1024


ON_CHIP = pl.BlockSpec(memory_space=pltpu.VMEM)


def on_chip(values):
    return pltpu.with_memory_space_constraint(values, pltpu.VMEM)


def in_hbm(values):
    return pltpu.with_memory_space_constraint(values, pltpu.HBM)


def step_rows(ref, rows):
    return ref.at[:, pl.ds(pl.multiple_of(pl.program_id(0) * rows, rows), rows), :]


def dot(left, right):
    return jnp.dot(left, right, preferred_element_type=F32)


def dot_nt(left, right):
    return lax.dot_general(left, right, (((1,), (1,)), ((), ())), preferred_element_type=F32)


def dot_tn(left, right):
    return lax.dot_general(left, right, (((0,), (0,)), ((), ())), preferred_element_type=F32)


def split3(values):
    first = values.astype(BF16)
    rest = values - first.astype(F32)
    second = rest.astype(BF16)
    third = (rest - second.astype(F32)).astype(BF16)
    return first, second, third


def sigmoid(values):
    return 1.0 / (1.0 + jnp.exp(-values))


def shift_down(values, period):
    rows = lax.broadcasted_iota(jnp.int32, values.shape, 0) % period
    return jnp.where(rows == 0, 0.0, pltpu.roll(values, 1, 0))


def shift_up(values, period):
    total = values.shape[0]
    rows = lax.broadcasted_iota(jnp.int32, values.shape, 0) % period
    return jnp.where(rows == period - 1, 0.0, pltpu.roll(values, total - 1, 0))


def group_rank(perm_ref, window, window_dev, col_count):
    trainer = perm_ref[window] // window_dev
    per_row = 2
    return (trainer // col_count) * per_row + trainer % per_row


def sums_kernel(ids_ref, spec_ref, log_ref, out_ref, acc, *, chunks, count):
    step = pl.program_id(0)
    windows, frames, bins = spec_ref.shape
    rows = 16

    for w in range(windows):
        def body(i, carry):
            total, square = carry
            start = pl.multiple_of(i * rows, rows)
            value = jnp.log(1.0 + spec_ref[w, pl.ds(start, rows), :].astype(F32))
            for k in range(chunks):
                log_ref[step * windows + w, k, pl.ds(start, rows), :] = value[:, k * LANES:(k + 1) * LANES]
            value_sq = value * value
            return (total + value[0:8] + value[8:16], square + value_sq[0:8] + value_sq[8:16])

        zero = jnp.zeros((8, bins), F32)
        total, square = lax.fori_loop(0, frames // rows, body, (zero, zero), unroll=4)
        total = jnp.sum(total, axis=0, keepdims=True)
        square = jnp.sum(square, axis=0, keepdims=True)
        pieces = [total[:, k * LANES:(k + 1) * LANES] for k in range(chunks)]
        pieces += [square[:, k * LANES:(k + 1) * LANES] for k in range(chunks)]
        start = pl.multiple_of((step * windows + w) * 2 * chunks, 2 * chunks)
        acc[pl.ds(start, 2 * chunks), :] = jnp.concatenate(pieces, axis=0)

    @pl.when(step == pl.num_programs(0) - 1)
    def _():
        acc[LANES:2 * LANES, :] = jnp.zeros((LANES, LANES), F32)
        for w in range(count):
            acc[LANES + w:LANES + w + 1, :] = jnp.full((1, LANES), ids_ref[w], jnp.int32).astype(F32)
        out_ref[pl.ds(0, LANES, stride=2), :] = acc[0:LANES, :].T
        out_ref[pl.ds(1, LANES, stride=2), :] = acc[LANES:2 * LANES, :].T


def sums_call(spectra, sensor_ids):
    windows, frames, bins = spectra.shape
    chunks = bins // LANES
    grid_spec = pltpu.PrefetchScalarGridSpec(
        num_scalar_prefetch=1,
        grid=(windows // SORT_WINDOWS,),
        in_specs=[pl.BlockSpec((SORT_WINDOWS, frames, bins), lambda i, s: (i, 0, 0))],
        out_specs=[ON_CHIP, pl.BlockSpec((2 * LANES, LANES), lambda i, s: (0, 0))],
        scratch_shapes=[pltpu.VMEM((2 * LANES, LANES), F32)],
    )
    return pl.pallas_call(
        functools.partial(sums_kernel, chunks=chunks, count=windows),
        grid_spec=grid_spec,
        out_shape=[
            pltpu.VMEM((windows, chunks, frames, LANES), F32),
            jax.ShapeDtypeStruct((2 * LANES, LANES), F32),
        ],
        compiler_params=pltpu.CompilerParams(vmem_limit_bytes=10 * MIB),
        name="log_and_sum",
    )(in_hbm(sensor_ids.reshape(windows)), in_hbm(spectra))


def stats_kernel(in_ref, out_ref, *, windows, chunks, sensors, per_sensor):
    width = 2 * chunks
    data = in_ref[pl.ds(0, LANES, stride=2), :].T
    labels = in_ref[pl.ds(1, LANES, stride=2), :].T
    sensor_rows = lax.broadcasted_iota(jnp.int32, (sensors, LANES), 0).astype(F32)
    tables = [(sensor_rows == labels[w:w + 1, :]).astype(F32).astype(BF16) for w in range(windows)]
    table = jnp.concatenate(tables, axis=1)
    values = jnp.concatenate([data[w * width:(w + 1) * width, :] for w in range(windows)], axis=1)
    parts = dot_nt(jnp.concatenate(split3(values), axis=0), table)
    sums = parts[0:width] + parts[width:2 * width] + parts[2 * width:3 * width]
    center = sums[0:chunks] / per_sensor
    factor = lax.rsqrt(sums[chunks:width] / per_sensor - center * center + EPS)
    both = jnp.concatenate([center, factor], axis=0)
    back = dot(jnp.concatenate(split3(both), axis=0), table)
    back = back[0:width] + back[width:2 * width] + back[2 * width:3 * width]
    rows = jnp.concatenate([back[:, w * LANES:(w + 1) * LANES] for w in range(windows)], axis=0)
    out_ref[...] = rows.T


def stats_call(received, windows, chunks, sensors, per_sensor):
    return pl.pallas_call(
        functools.partial(stats_kernel, windows=windows, chunks=chunks, sensors=sensors, per_sensor=float(per_sensor)),
        out_shape=jax.ShapeDtypeStruct((LANES, LANES), F32),
        compiler_params=pltpu.CompilerParams(vmem_limit_bytes=12 * MIB),
        name="sensor_stats",
    )(received)


def enc1_kernel(perm_ref, log_ref, coef_ref, w_ref, normed_ref, pre_ref, stat_ref, coef, *, cols):
    step = pl.program_id(0)
    all_windows, chunks, frames, _ = log_ref.shape
    quarter = frames // 4
    bins = chunks * LANES
    windows = STEP_WINDOWS
    normed_ref, pre_ref = (step_rows(ref, windows * quarter) for ref in (normed_ref, pre_ref))
    channels = w_ref.shape[1]
    width = 2 * chunks

    @pl.when(step == 0)
    def _():
        coef[...] = coef_ref[...].T

    for w in range(windows):
        start = pl.multiple_of((step * windows + w) * width, width)
        both = coef[pl.ds(start, width), :]
        low, high = w * quarter, (w + 1) * quarter
        for k in range(chunks):
            center = both[k:k + 1, :]
            factor = both[chunks + k:chunks + k + 1, :]
            for i in range(4):
                value = log_ref[step * windows + w, k, pl.ds(i, quarter, stride=4), :]
                normed_ref[i, low:high, k * LANES:(k + 1) * LANES] = ((value - center) * factor).astype(BF16)

    w0, w1, w2, w3 = (w_ref[k * bins:(k + 1) * bins, :] for k in range(4))
    f0, f1, f2, f3 = (normed_ref[i] for i in range(4))
    even = shift_down(dot(f3, w0), quarter) + dot(f0, w1) + dot(f1, w2) + dot(f2, w3)
    odd = dot(f1, w0) + dot(f2, w1) + dot(f3, w2) + shift_up(dot(f0, w3), quarter)
    pre_ref[0] = even
    pre_ref[1] = odd
    for w in range(windows):
        part_e = even[w * quarter:(w + 1) * quarter]
        part_o = odd[w * quarter:(w + 1) * quarter]
        mean = (jnp.sum(part_e, axis=0, keepdims=True) + jnp.sum(part_o, axis=0, keepdims=True)) / (2 * quarter)
        diff_e = part_e - mean
        diff_o = part_o - mean
        spread = (jnp.sum(diff_e * diff_e, axis=0, keepdims=True) + jnp.sum(diff_o * diff_o, axis=0, keepdims=True)) / (2 * quarter)
        place = group_rank(perm_ref, step * windows + w, all_windows, cols)
        stat_ref[pl.ds(place, 1), 0:channels] = mean
        stat_ref[pl.ds(place, 1), channels:2 * channels] = spread


def enc1_call(permutation, logs, coef, w_enc1, cols):
    windows, chunks, frames, _ = logs.shape
    channels = w_enc1.shape[1]
    rows = windows * frames // 4
    grid_spec = pltpu.PrefetchScalarGridSpec(
        num_scalar_prefetch=1,
        grid=(windows // STEP_WINDOWS,),
        in_specs=[ON_CHIP, pl.BlockSpec((LANES, LANES), lambda i, p: (0, 0)), ON_CHIP],
        out_specs=[ON_CHIP] * 3,
        scratch_shapes=[pltpu.VMEM((LANES, LANES), F32)],
    )
    return pl.pallas_call(
        functools.partial(enc1_kernel, cols=cols),
        grid_spec=grid_spec,
        out_shape=[
            pltpu.VMEM((4, rows, chunks * LANES), BF16),
            pltpu.VMEM((2, rows, channels), F32),
            pltpu.VMEM((windows, 2 * channels), F32),
        ],
        compiler_params=pltpu.CompilerParams(vmem_limit_bytes=16 * MIB),
        name="normalize_enc1",
    )(permutation, on_chip(logs), coef, on_chip(w_enc1))


def window_rows(perm_ref, table, step, windows, quarter, all_windows, cols, first, last):
    parts = []
    for w in range(windows):
        place = group_rank(perm_ref, step * windows + w, all_windows, cols)
        parts.append(jnp.broadcast_to(table[pl.ds(place, 1), first:last], (quarter, last - first)))
    return jnp.concatenate(parts, axis=0)


def write_halves(core_ref, grads, own_ref, send_ref, bounds):
    for first, last in zip(bounds[:-1], bounds[1:]):
        half = (last - first) // 2
        at = first // 2
        own = pl.multiple_of(first + core_ref[0] * half, half)
        send = pl.multiple_of(first + (1 - core_ref[0]) * half, half)
        own_ref[at:at + half, :] = grads[pl.ds(own, half), :]
        send_ref[at:at + half, :] = grads[pl.ds(send, half), :]


def middle_kernel(perm_ref, core_ref, normed_ref, pre_ref, stat_ref, v_ref, b_ref, c_ref,
                  own_ref, send_ref, back_ref, moment_ref, sums_ref,
                  grads, moment, *, quarter, cols, total_windows):
    step = pl.program_id(0)
    channels = v_ref.shape[1]
    bins = normed_ref.shape[2]
    windows = STEP_WINDOWS
    normed_ref, pre_ref, back_ref = (step_rows(ref, windows * quarter) for ref in (normed_ref, pre_ref, back_ref))
    all_windows = windows * pl.num_programs(0)
    ch = channels

    @pl.when(step == 0)
    def _():
        means = stat_ref[:, :, 0:ch]
        mean = jnp.mean(means, axis=0)
        diff = means - mean[None]
        variance = jnp.mean(stat_ref[:, :, ch:2 * ch] + diff * diff, axis=0)
        moment[:, 0:ch] = mean
        moment[:, ch:2 * ch] = lax.rsqrt(variance + EPS)
        moment_ref[...] = moment[...]
        grads[...] = jnp.zeros_like(grads)

    mean = window_rows(perm_ref, moment, step, windows, quarter, all_windows, cols, 0, ch)
    inverse = window_rows(perm_ref, moment, step, windows, quarter, all_windows, cols, ch, 2 * ch)
    hat_e = (pre_ref[0] - mean) * inverse
    hat_o = (pre_ref[1] - mean) * inverse
    a_e = (hat_e * sigmoid(hat_e)).astype(BF16)
    a_o = (hat_o * sigmoid(hat_o)).astype(BF16)
    v0, v1, v2, v3 = (v_ref[k * ch:(k + 1) * ch, :] for k in range(4))
    pre2 = shift_down(dot(a_o, v0), quarter) + dot(a_e, v1) + dot(a_o, v2) + shift_up(dot(a_e, v3), quarter)
    gate2 = sigmoid(pre2)
    h32 = (pre2 * gate2).astype(BF16).astype(F32)
    h = h32.astype(BF16)
    b0, b1, b2, b3 = (b_ref[:, k * ch:(k + 1) * ch] for k in range(4))
    d1_e = dot(h, b1) + shift_down(dot(h, b3), quarter)
    d1_o = dot(h, b2) + shift_up(dot(h, b0), quarter)
    gate_e = sigmoid(d1_e)
    gate_o = sigmoid(d1_o)
    de32 = (d1_e * gate_e)
    do32 = (d1_o * gate_o)
    de = de32.astype(BF16)
    do = do32.astype(BF16)
    de_up = shift_up(de32, quarter).astype(BF16)
    do_down = shift_down(do32, quarter).astype(BF16)
    c0, c1, c2, c3 = (c_ref[:, k * bins:(k + 1) * bins] for k in range(4))

    def delta(rebuilt, i):
        return ((rebuilt - normed_ref[i].astype(F32)) / total_windows).astype(BF16)

    g0 = delta(dot(de, c1) + dot(do_down, c3), 0)
    g1 = delta(dot(de, c2) + dot(do, c0), 1)
    g2 = delta(dot(do, c1) + dot(de, c3), 2)
    g3 = delta(dot(do, c2) + dot(de_up, c0), 3)
    halves = bins // ch
    base_b = 4 * bins
    base_v = base_b + 4 * ch

    def add_c(k, value):
        for j in range(halves):
            at = (k * halves + j) * ch
            grads[at:at + ch, :] += value[:, j * ch:(j + 1) * ch]

    add_c(0, dot_tn(de_up, g3) + dot_tn(do, g1))
    add_c(1, dot_tn(de, g0) + dot_tn(do, g2))
    add_c(2, dot_tn(de, g1) + dot_tn(do, g3))
    add_c(3, dot_tn(de, g2) + dot_tn(do_down, g0))
    back_e = shift_down(dot_nt(g3, c0), quarter) + dot_nt(g0, c1) + dot_nt(g1, c2) + dot_nt(g2, c3)
    back_o = dot_nt(g1, c0) + dot_nt(g2, c1) + dot_nt(g3, c2) + shift_up(dot_nt(g0, c3), quarter)
    dd_e = (back_e * (gate_e * (1.0 + d1_e * (1.0 - gate_e)))).astype(BF16)
    dd_o = (back_o * (gate_o * (1.0 + d1_o * (1.0 - gate_o)))).astype(BF16)
    h_up = shift_up(h32, quarter).astype(BF16)
    h_down = shift_down(h32, quarter).astype(BF16)
    grads[base_b:base_b + ch, :] += dot_tn(h_up, dd_o)
    grads[base_b + ch:base_b + 2 * ch, :] += dot_tn(h, dd_e)
    grads[base_b + 2 * ch:base_b + 3 * ch, :] += dot_tn(h, dd_o)
    grads[base_b + 3 * ch:base_b + 4 * ch, :] += dot_tn(h_down, dd_e)
    back2 = shift_down(dot_nt(dd_o, b0), quarter) + dot_nt(dd_e, b1) + dot_nt(dd_o, b2) + shift_up(dot_nt(dd_e, b3), quarter)
    d2_32 = (back2 * (gate2 * (1.0 + pre2 * (1.0 - gate2)))).astype(BF16).astype(F32)
    d2 = d2_32.astype(BF16)
    d2_up = shift_up(d2_32, quarter).astype(BF16)
    d2_down = shift_down(d2_32, quarter).astype(BF16)
    grads[base_v:base_v + ch, :] += dot_tn(a_o, d2_up)
    grads[base_v + ch:base_v + 2 * ch, :] += dot_tn(a_e, d2)
    grads[base_v + 2 * ch:base_v + 3 * ch, :] += dot_tn(a_o, d2)
    grads[base_v + 3 * ch:base_v + 4 * ch, :] += dot_tn(a_e, d2_down)
    fold_e = dot_nt(d2, v1) + shift_down(dot_nt(d2, v3), quarter)
    fold_o = dot_nt(d2, v2) + shift_up(dot_nt(d2, v0), quarter)
    gate_he = sigmoid(hat_e)
    gate_ho = sigmoid(hat_o)
    fold_e = fold_e * (gate_he * (1.0 + hat_e * (1.0 - gate_he)))
    fold_o = fold_o * (gate_ho * (1.0 + hat_o * (1.0 - gate_ho)))
    back_ref[0] = fold_e
    back_ref[1] = fold_o
    cross_e = fold_e * hat_e
    cross_o = fold_o * hat_o
    for w in range(windows):
        low, high = w * quarter, (w + 1) * quarter
        first = jnp.sum(fold_e[low:high] + fold_o[low:high], axis=0, keepdims=True)
        second = jnp.sum(cross_e[low:high] + cross_o[low:high], axis=0, keepdims=True)
        place = group_rank(perm_ref, step * windows + w, all_windows, cols)
        sums_ref[pl.ds(place, 1), 0:ch] = first
        sums_ref[pl.ds(place, 1), ch:2 * ch] = second

    @pl.when(step == pl.num_programs(0) - 1)
    def _():
        write_halves(core_ref, grads, own_ref, send_ref, (0, base_b, base_v, base_v + 4 * ch))


def middle_call(permutation, core, normed, pre, stat, w_enc2, w_dec1, w_dec2, quarter, cols, total_windows):
    bins = normed.shape[2]
    channels = w_enc2.shape[1]
    windows = normed.shape[1] // quarter
    total = 4 * bins + 8 * channels
    whole2 = lambda i, p, c: (0, 0)
    grid_spec = pltpu.PrefetchScalarGridSpec(
        num_scalar_prefetch=2,
        grid=(windows // STEP_WINDOWS,),
        in_specs=[
            ON_CHIP,
            ON_CHIP,
            ON_CHIP,
            ON_CHIP,
            ON_CHIP,
            ON_CHIP,
        ],
        out_specs=[
            ON_CHIP,
            ON_CHIP,
            ON_CHIP,
            pl.BlockSpec((windows, 2 * channels), whole2),
            ON_CHIP,
        ],
        scratch_shapes=[
            pltpu.VMEM((total, channels), F32),
            pltpu.VMEM((windows, 2 * channels), F32),
        ],
    )
    return pl.pallas_call(
        functools.partial(middle_kernel, quarter=quarter, cols=cols, total_windows=float(total_windows)),
        grid_spec=grid_spec,
        out_shape=[
            pltpu.VMEM((total // 2, channels), F32),
            pltpu.VMEM((total // 2, channels), F32),
            pltpu.VMEM(pre.shape, F32),
            jax.ShapeDtypeStruct((windows, 2 * channels), F32),
            pltpu.VMEM((windows, 2 * channels), F32),
        ],
        compiler_params=pltpu.CompilerParams(vmem_limit_bytes=30 * MIB),
        name="middle",
    )(permutation, core, on_chip(normed), on_chip(pre), on_chip(stat), on_chip(w_enc2), on_chip(w_dec1), on_chip(w_dec2))


def tap_grads(normed_ref, delta_ref, out_ref, taps):
    pairs = (((3, 2), (1, 1)), ((0, 0), (2, 1)), ((1, 0), (3, 1)), ((2, 0), (0, 3)))
    bins = normed_ref.shape[2]
    for n, k in enumerate(taps):
        (f0, d0), (f1, d1) = pairs[k]
        out_ref[n * bins:(n + 1) * bins, :] = dot_tn(normed_ref[f0], delta_ref[d0]) + dot_tn(normed_ref[f1], delta_ref[d1])


def send_grad_kernel(perm_ref, core_ref, normed_ref, pre_ref, back_ref, moment_ref, sums_ref, send_ref, delta_ref, scale, *, quarter, cols):
    ch = pre_ref.shape[2]
    windows = pre_ref.shape[1] // quarter
    scale[...] = jnp.sum(sums_ref[...], axis=0) / (2.0 * quarter * cols)
    pick = functools.partial(window_rows, perm_ref, step=0, windows=windows, quarter=quarter, all_windows=windows, cols=cols)
    mean = pick(table=moment_ref, first=0, last=ch)
    inverse = pick(table=moment_ref, first=ch, last=2 * ch)
    first = pick(table=scale, first=0, last=ch)
    second = pick(table=scale, first=ch, last=2 * ch)
    hat_e = (pre_ref[0] - mean) * inverse
    hat_o = (pre_ref[1] - mean) * inverse
    even = (back_ref[0] - first - hat_e * second) * inverse
    odd = (back_ref[1] - first - hat_o * second) * inverse
    delta_ref[0] = even.astype(BF16)
    delta_ref[1] = odd.astype(BF16)
    delta_ref[2] = shift_up(even, quarter).astype(BF16)
    delta_ref[3] = shift_down(odd, quarter).astype(BF16)
    core_taps(core_ref, normed_ref, delta_ref, send_ref, ((2, 3), (0, 1)))


def own_grad_kernel(core_ref, normed_ref, delta_ref, own_ref):
    core_taps(core_ref, normed_ref, delta_ref, own_ref, ((0, 1), (2, 3)))


def core_taps(core_ref, normed_ref, delta_ref, out_ref, taps):
    for core in range(2):
        @pl.when(core_ref[0] == core)
        def _():
            tap_grads(normed_ref, delta_ref, out_ref, taps[core])


def grad_calls(permutation, core, normed, pre, back, moment, sums, quarter, cols):
    _, rows, bins = normed.shape
    channels = pre.shape[2]
    windows = rows // quarter
    half = jax.ShapeDtypeStruct((2 * bins, channels), F32)
    send, deltas = pl.pallas_call(
        functools.partial(send_grad_kernel, quarter=quarter, cols=cols),
        grid_spec=pltpu.PrefetchScalarGridSpec(
            num_scalar_prefetch=2,
            grid=(1,),
            in_specs=[ON_CHIP] * 5,
            out_specs=[ON_CHIP] * 2,
            scratch_shapes=[pltpu.VMEM((windows, 2 * channels), F32)],
        ),
        out_shape=[pltpu.VMEM(half.shape, F32), pltpu.VMEM((4, rows, channels), BF16)],
        compiler_params=pltpu.CompilerParams(vmem_limit_bytes=16 * MIB),
        name="send_grad_enc1",
    )(permutation, core, on_chip(normed), on_chip(pre), on_chip(back), on_chip(moment), on_chip(sums))
    own = pl.pallas_call(
        own_grad_kernel,
        grid_spec=pltpu.PrefetchScalarGridSpec(
            num_scalar_prefetch=1, grid=(1,), in_specs=[ON_CHIP] * 2, out_specs=ON_CHIP),
        out_shape=pltpu.VMEM(half.shape, F32),
        compiler_params=pltpu.CompilerParams(vmem_limit_bytes=12 * MIB),
        cost_estimate=pl.CostEstimate(flops=8 * rows * bins * channels, bytes_accessed=8 * rows * bins, transcendentals=0),
        name="own_grad_enc1",
    )(core, on_chip(normed), on_chip(deltas))
    return own, send


def swap_cores(values):
    return lax.ppermute(values, "core", [(0, 1), (1, 0)])


def exchange(values, axes):
    return lax.all_to_all(values, axes, split_axis=0, concat_axis=0, tiled=True)


def join_kernel(mine_ref, other_ref, out_ref, *, moments):
    mine, other = mine_ref[...], other_ref[...]
    total = mine + other
    width = total.shape[1] // 2
    if moments:
        apart = 0.5 * (mine[:, 0:width] - other[:, 0:width])
        total = jnp.concatenate([0.5 * total[:, 0:width], 0.5 * total[:, width:] + apart * apart], axis=1)
    for d in range(out_ref.shape[0]):
        out_ref[d] = total


def join_cores(mine, chips, moments):
    rows, width = mine.shape
    return pl.pallas_call(
        functools.partial(join_kernel, moments=moments),
        in_specs=[ON_CHIP] * 2,
        out_specs=ON_CHIP,
        out_shape=pltpu.VMEM((chips, rows, width), F32),
        compiler_params=pltpu.CompilerParams(vmem_limit_bytes=2 * MIB),
        name="join_cores",
    )(on_chip(mine), on_chip(swap_cores(mine)))


def exchange_copies(copies):
    return exchange(copies.reshape(-1, copies.shape[2]), "pair").reshape(copies.shape)


def chip_sums(parts, axes, chips):
    total = [(own + swap_cores(send)).astype(BF16).reshape(chips, -1, own.shape[1]) for own, send in parts]
    total = jnp.concatenate(total, axis=1)
    return exchange(total.reshape(-1, total.shape[2]), axes).reshape(total.shape)


def owner_kernel(in_ref, out_ref):
    chips, rows, width = in_ref.shape

    def body(i, total):
        return total + in_ref[i].astype(F32)

    total = lax.fori_loop(0, chips, body, jnp.zeros((rows, width), F32), unroll=4)
    largest = jnp.max(jnp.max(jnp.abs(total), axis=0, keepdims=True), axis=1, keepdims=True)
    exponent = jnp.clip(jnp.ceil(jnp.log2(largest)), -110.0, 126.0)
    total = total * jnp.exp2(14.0 - exponent)
    for k in range(width // LANES):
        out_ref[k * rows:(k + 1) * rows, :] = total[:, k * LANES:(k + 1) * LANES]
    out_ref[width // LANES * rows:, :] = jnp.broadcast_to(exponent, (SCALE_ROWS, LANES))


def owner_call(pieces):
    chips, rows, width = pieces.shape
    return pl.pallas_call(
        owner_kernel,
        out_shape=jax.ShapeDtypeStruct((width // LANES * rows + SCALE_ROWS, LANES), F32),
        compiler_params=pltpu.CompilerParams(vmem_limit_bytes=6 * MIB),
        name="owner_sum",
    )(pieces)


def gather_rows(piece, axes, chips):
    rows, width = piece.shape
    copies = jnp.broadcast_to(piece.astype(jnp.float16)[None], (chips, rows, width))
    return exchange(copies.reshape(-1, width), axes).reshape(chips, rows, width)


def place_kernel(half_ref, blocks_ref, *refs, rows, cut, start, stop):
    grad_w_ref, grad_v_ref, grad_b_ref, grad_c_ref = refs[-4:]
    step = start + pl.program_id(0)
    channels = grad_w_ref.shape[1]
    late = rows - cut
    group = channels // cut

    def copy(out_ref, i, row, column):
        scale = jnp.exp2(blocks_ref[i, 2 * rows:2 * rows + 1, :] - 14.0)
        for k in range(2):
            block = blocks_ref[i, k * rows:(k + 1) * rows, :] * scale
            grad_w_ref[i * late:(i + 1) * late, k * LANES:(k + 1) * LANES] = block[cut:rows]
            out_ref[row:row + cut, column + k * LANES:column + (k + 1) * LANES] = block[0:cut]

    if start < 2:
        @pl.when(step < 2)
        def _():
            for i in range(2 * group):
                copy(grad_c_ref, i, i % group * cut, i // group * channels)

    if stop > 2:
        @pl.when(step == 2)
        def _():
            for i in range(2 * group):
                copy(grad_b_ref, i, i % group * cut, i // group * channels)

        @pl.when(step == 3)
        def _():
            for i in range(2 * group):
                copy(grad_v_ref, i, i * cut, 0)


def place_call(half, blocks, rows, cut, channels, bins, start=0, earlier=()):
    chips, total, _ = blocks.shape
    group = channels // cut
    stop = start + chips // (2 * group)
    untouched = pl.BlockSpec(memory_space=pl.ANY)
    late = rows - cut
    grid_spec = pltpu.PrefetchScalarGridSpec(
        num_scalar_prefetch=1,
        grid=(stop - start,),
        in_specs=[pl.BlockSpec((2 * group, total, LANES), lambda i, h: (i, 0, 0))]
        + [pl.BlockSpec(memory_space=pl.ANY)] * len(earlier),
        out_specs=[
            pl.BlockSpec((2 * group * late, channels), lambda i, h: (h[0] * 4 + start + i, 0)),
            pl.BlockSpec((2 * channels, channels), lambda i, h: (h[0], 0)) if stop > 2 else untouched,
            pl.BlockSpec((channels, 2 * channels), lambda i, h: (0, h[0])) if stop > 2 else untouched,
            pl.BlockSpec((channels, 2 * channels), lambda i, h: (0, h[0] * 2 + jnp.minimum(start + i, 1))) if start < 2 else untouched,
        ],
    )
    return pl.pallas_call(
        functools.partial(place_kernel, rows=rows, cut=cut, start=start, stop=stop),
        grid_spec=grid_spec,
        out_shape=[
            jax.ShapeDtypeStruct((4 * bins, channels), F32),
            jax.ShapeDtypeStruct((4 * channels, channels), F32),
            jax.ShapeDtypeStruct((channels, 4 * channels), F32),
            jax.ShapeDtypeStruct((channels, 4 * bins), F32),
        ],
        input_output_aliases={2 + k: k for k in range(len(earlier))},
        compiler_params=pltpu.CompilerParams(vmem_limit_bytes=16 * MIB),
        cost_estimate=pl.CostEstimate(flops=chips * total * LANES, bytes_accessed=8 * chips * total * LANES, transcendentals=0),
        name="place_gradients",
    )(half, blocks, *earlier)


def local(spectra, sensor_ids, permutation, w_enc1, w_enc2, w_dec1, w_dec2):
    windows, frames, bins = spectra.shape
    channels = w_enc1.shape[1]
    chip_axes = ("row", "pair")
    every = ("row", "pair", "core")
    cols = lax.axis_size("pair") * lax.axis_size("core")
    chips = lax.axis_size("row") * lax.axis_size("pair")
    total_windows = windows * lax.axis_size("row") * cols
    sensors = total_windows // WIN_SENSOR
    chunks = bins // LANES
    quarter = frames // 4
    core_index = lax.axis_index("core")
    core = core_index.astype(jnp.int32).reshape(1)

    logs, sums = sums_call(spectra, sensor_ids)
    sums, core = lax.optimization_barrier((sums, core))
    sums = exchange(sums, every)
    coef = exchange(stats_call(sums, windows, chunks, sensors, WIN_SENSOR * frames), every)
    normed, pre, stat = enc1_call(permutation, logs, coef, w_enc1, cols)
    stat = exchange_copies(join_cores(stat, cols // 2, True))
    own, send, back, moment, moments = middle_call(
        permutation, core, normed, pre, stat, w_enc2, w_dec1, w_dec2, quarter, cols, total_windows)
    moments, send = lax.optimization_barrier((join_cores(moments, cols // 2, False), send))
    moments = exchange_copies(moments)
    late = grad_calls(permutation, core, normed, pre, back, moment, moments, quarter, cols)
    piece = owner_call(chip_sums([(own, send), late], chip_axes, chips))
    mine = gather_rows(piece, chip_axes, chips)
    rows, cut = own.shape[0] // chips + late[0].shape[0] // chips, own.shape[0] // chips
    others = [swap_cores(mine[0:chips // 2]), swap_cores(mine[chips // 2:])]
    placed = place_call(core, mine.astype(F32), rows, cut, channels, bins)
    for n, other in enumerate(others):
        placed = place_call(1 - core, other.astype(F32), rows, cut, channels, bins, 2 * n, placed)
    return tuple(placed)


def solution(mesh):
    rows, cols = mesh.devices.shape
    inner = Mesh(mesh.devices.reshape(rows, cols // 2, 2), ("row", "pair", "core"))
    spread = ("row", "pair", "core")
    return jax.shard_map(
        local,
        mesh=inner,
        in_specs=(P(spread, None, None), P(spread, None), P(spread), P(), P(), P(), P()),
        out_specs=(P(), P(), P(), P()),
        check_vma=False,
    )
```

```python
import functools

import jax
import jax.numpy as jnp
from jax import lax
from jax.experimental import pallas as pl
from jax.experimental.pallas import tpu as pltpu
from jax.sharding import Mesh, PartitionSpec as P

WIN_SENSOR = 8
EPS = 1e-05
F32 = jnp.float32
BF16 = jnp.bfloat16
LANES = 128
STEP_WINDOWS = 16
SORT_WINDOWS = 8
SCALE_ROWS = 8
MIB = 1024 * 1024


ON_CHIP = pl.BlockSpec(memory_space=pltpu.VMEM)


def on_chip(values):
    return pltpu.with_memory_space_constraint(values, pltpu.VMEM)


def in_hbm(values):
    return pltpu.with_memory_space_constraint(values, pltpu.HBM)


def step_rows(ref, rows):
    return ref.at[:, pl.ds(pl.multiple_of(pl.program_id(0) * rows, rows), rows), :]


def dot(left, right):
    return jnp.dot(left, right, preferred_element_type=F32)


def dot_nt(left, right):
    return lax.dot_general(left, right, (((1,), (1,)), ((), ())), preferred_element_type=F32)


def dot_tn(left, right):
    return lax.dot_general(left, right, (((0,), (0,)), ((), ())), preferred_element_type=F32)


def split3(values):
    first = values.astype(BF16)
    rest = values - first.astype(F32)
    second = rest.astype(BF16)
    third = (rest - second.astype(F32)).astype(BF16)
    return first, second, third


def sigmoid(values):
    return 0.5 + 0.5 * jnp.tanh(0.5 * values)


def shift_down(values, period):
    rows = lax.broadcasted_iota(jnp.int32, values.shape, 0) % period
    return jnp.where(rows == 0, 0.0, pltpu.roll(values, 1, 0))


def shift_up(values, period):
    total = values.shape[0]
    rows = lax.broadcasted_iota(jnp.int32, values.shape, 0) % period
    return jnp.where(rows == period - 1, 0.0, pltpu.roll(values, total - 1, 0))


def group_rank(perm_ref, window, window_dev, col_count):
    trainer = perm_ref[window] // window_dev
    per_row = 2
    return (trainer // col_count) * per_row + trainer % per_row


def sums_kernel(ids_ref, spec_ref, log_ref, out_ref, acc, *, chunks, count):
    step = pl.program_id(0)
    windows, frames, bins = spec_ref.shape
    rows = 16

    for w in range(windows):
        def body(i, carry):
            total, square = carry
            start = pl.multiple_of(i * rows, rows)
            value = jnp.log(1.0 + spec_ref[w, pl.ds(start, rows), :].astype(F32))
            for k in range(chunks):
                log_ref[step * windows + w, k, pl.ds(start, rows), :] = value[:, k * LANES:(k + 1) * LANES]
            value_sq = value * value
            return (total + value[0:8] + value[8:16], square + value_sq[0:8] + value_sq[8:16])

        zero = jnp.zeros((8, bins), F32)
        total, square = lax.fori_loop(0, frames // rows, body, (zero, zero), unroll=8)
        total = jnp.sum(total, axis=0, keepdims=True)
        square = jnp.sum(square, axis=0, keepdims=True)
        pieces = [total[:, k * LANES:(k + 1) * LANES] for k in range(chunks)]
        pieces += [square[:, k * LANES:(k + 1) * LANES] for k in range(chunks)]
        start = pl.multiple_of((step * windows + w) * 2 * chunks, 2 * chunks)
        acc[pl.ds(start, 2 * chunks), :] = jnp.concatenate(pieces, axis=0)

    @pl.when(step == pl.num_programs(0) - 1)
    def _():
        acc[LANES:2 * LANES, :] = jnp.zeros((LANES, LANES), F32)
        for w in range(count):
            acc[LANES + w:LANES + w + 1, :] = jnp.full((1, LANES), ids_ref[w], jnp.int32).astype(F32)
        out_ref[pl.ds(0, LANES, stride=2), :] = acc[0:LANES, :].T
        out_ref[pl.ds(1, LANES, stride=2), :] = acc[LANES:2 * LANES, :].T


def sums_call(spectra, sensor_ids):
    windows, frames, bins = spectra.shape
    chunks = bins // LANES
    grid_spec = pltpu.PrefetchScalarGridSpec(
        num_scalar_prefetch=1,
        grid=(windows // SORT_WINDOWS,),
        in_specs=[pl.BlockSpec((SORT_WINDOWS, frames, bins), lambda i, s: (i, 0, 0))],
        out_specs=[ON_CHIP, pl.BlockSpec((2 * LANES, LANES), lambda i, s: (0, 0))],
        scratch_shapes=[pltpu.VMEM((2 * LANES, LANES), F32)],
    )
    return pl.pallas_call(
        functools.partial(sums_kernel, chunks=chunks, count=windows),
        grid_spec=grid_spec,
        out_shape=[
            pltpu.VMEM((windows, chunks, frames, LANES), F32),
            jax.ShapeDtypeStruct((2 * LANES, LANES), F32),
        ],
        compiler_params=pltpu.CompilerParams(vmem_limit_bytes=10 * MIB),
        name="log_and_sum",
    )(in_hbm(sensor_ids.reshape(windows)), in_hbm(spectra))


def stats_kernel(in_ref, out_ref, *, windows, chunks, sensors, per_sensor):
    width = 2 * chunks
    data = in_ref[pl.ds(0, LANES, stride=2), :].T
    labels = in_ref[pl.ds(1, LANES, stride=2), :].T
    sensor_rows = lax.broadcasted_iota(jnp.int32, (sensors, LANES), 0).astype(F32)
    tables = [(sensor_rows == labels[w:w + 1, :]).astype(F32).astype(BF16) for w in range(windows)]
    table = jnp.concatenate(tables, axis=1)
    values = jnp.concatenate([data[w * width:(w + 1) * width, :] for w in range(windows)], axis=1)
    parts = dot_nt(jnp.concatenate(split3(values), axis=0), table)
    sums = parts[0:width] + parts[width:2 * width] + parts[2 * width:3 * width]
    center = sums[0:chunks] / per_sensor
    factor = lax.rsqrt(sums[chunks:width] / per_sensor - center * center + EPS)
    both = jnp.concatenate([center, factor], axis=0)
    back = dot(jnp.concatenate(split3(both), axis=0), table)
    back = back[0:width] + back[width:2 * width] + back[2 * width:3 * width]
    rows = jnp.concatenate([back[:, w * LANES:(w + 1) * LANES] for w in range(windows)], axis=0)
    out_ref[...] = rows.T


def stats_call(received, windows, chunks, sensors, per_sensor):
    return pl.pallas_call(
        functools.partial(stats_kernel, windows=windows, chunks=chunks, sensors=sensors, per_sensor=float(per_sensor)),
        out_shape=jax.ShapeDtypeStruct((LANES, LANES), F32),
        compiler_params=pltpu.CompilerParams(vmem_limit_bytes=12 * MIB),
        name="sensor_stats",
    )(received)


def enc1_kernel(perm_ref, log_ref, coef_ref, w_ref, normed_ref, pre_ref, stat_ref, coef, *, cols):
    step = pl.program_id(0)
    all_windows, chunks, frames, _ = log_ref.shape
    quarter = frames // 4
    bins = chunks * LANES
    windows = STEP_WINDOWS
    normed_ref, pre_ref = (step_rows(ref, windows * quarter) for ref in (normed_ref, pre_ref))
    channels = w_ref.shape[1]
    width = 2 * chunks

    @pl.when(step == 0)
    def _():
        coef[...] = coef_ref[...].T

    for w in range(windows):
        start = pl.multiple_of((step * windows + w) * width, width)
        both = coef[pl.ds(start, width), :]
        low, high = w * quarter, (w + 1) * quarter
        for k in range(chunks):
            center = both[k:k + 1, :]
            factor = both[chunks + k:chunks + k + 1, :]
            for i in range(4):
                value = log_ref[step * windows + w, k, pl.ds(i, quarter, stride=4), :]
                normed_ref[i, low:high, k * LANES:(k + 1) * LANES] = ((value - center) * factor).astype(BF16)

    w0, w1, w2, w3 = (w_ref[k * bins:(k + 1) * bins, :] for k in range(4))
    f0, f1, f2, f3 = (normed_ref[i] for i in range(4))
    even = shift_down(dot(f3, w0), quarter) + dot(f0, w1) + dot(f1, w2) + dot(f2, w3)
    odd = dot(f1, w0) + dot(f2, w1) + dot(f3, w2) + shift_up(dot(f0, w3), quarter)
    pre_ref[0] = even
    pre_ref[1] = odd
    for w in range(windows):
        part_e = even[w * quarter:(w + 1) * quarter]
        part_o = odd[w * quarter:(w + 1) * quarter]
        mean = (jnp.sum(part_e, axis=0, keepdims=True) + jnp.sum(part_o, axis=0, keepdims=True)) / (2 * quarter)
        diff_e = part_e - mean
        diff_o = part_o - mean
        spread = (jnp.sum(diff_e * diff_e, axis=0, keepdims=True) + jnp.sum(diff_o * diff_o, axis=0, keepdims=True)) / (2 * quarter)
        place = group_rank(perm_ref, step * windows + w, all_windows, cols)
        stat_ref[pl.ds(place, 1), 0:channels] = mean
        stat_ref[pl.ds(place, 1), channels:2 * channels] = spread


def enc1_call(permutation, logs, coef, w_enc1, cols):
    windows, chunks, frames, _ = logs.shape
    channels = w_enc1.shape[1]
    rows = windows * frames // 4
    grid_spec = pltpu.PrefetchScalarGridSpec(
        num_scalar_prefetch=1,
        grid=(windows // STEP_WINDOWS,),
        in_specs=[ON_CHIP, pl.BlockSpec((LANES, LANES), lambda i, p: (0, 0)), ON_CHIP],
        out_specs=[ON_CHIP] * 3,
        scratch_shapes=[pltpu.VMEM((LANES, LANES), F32)],
    )
    return pl.pallas_call(
        functools.partial(enc1_kernel, cols=cols),
        grid_spec=grid_spec,
        out_shape=[
            pltpu.VMEM((4, rows, chunks * LANES), BF16),
            pltpu.VMEM((2, rows, channels), F32),
            pltpu.VMEM((windows, 2 * channels), F32),
        ],
        compiler_params=pltpu.CompilerParams(vmem_limit_bytes=16 * MIB),
        name="normalize_enc1",
    )(permutation, on_chip(logs), coef, on_chip(w_enc1))


def window_rows(perm_ref, table, step, windows, quarter, all_windows, cols, first, last):
    parts = []
    for w in range(windows):
        place = group_rank(perm_ref, step * windows + w, all_windows, cols)
        parts.append(jnp.broadcast_to(table[pl.ds(place, 1), first:last], (quarter, last - first)))
    return jnp.concatenate(parts, axis=0)


def write_halves(core_ref, grads, own_ref, send_ref, bounds):
    for first, last in zip(bounds[:-1], bounds[1:]):
        half = (last - first) // 2
        at = first // 2
        own = pl.multiple_of(first + core_ref[0] * half, half)
        send = pl.multiple_of(first + (1 - core_ref[0]) * half, half)
        own_ref[at:at + half, :] = grads[pl.ds(own, half), :]
        send_ref[at:at + half, :] = grads[pl.ds(send, half), :]


def middle_kernel(perm_ref, core_ref, normed_ref, pre_ref, stat_ref, v_ref, b_ref, c_ref,
                  own_ref, send_ref, back_ref, moment_ref, sums_ref,
                  grads, moment, *, quarter, cols, total_windows):
    step = pl.program_id(0)
    channels = v_ref.shape[1]
    bins = normed_ref.shape[2]
    windows = STEP_WINDOWS
    normed_ref, pre_ref, back_ref = (step_rows(ref, windows * quarter) for ref in (normed_ref, pre_ref, back_ref))
    all_windows = windows * pl.num_programs(0)
    ch = channels

    @pl.when(step == 0)
    def _():
        means = stat_ref[:, :, 0:ch]
        mean = jnp.mean(means, axis=0)
        diff = means - mean[None]
        variance = jnp.mean(stat_ref[:, :, ch:2 * ch] + diff * diff, axis=0)
        moment[:, 0:ch] = mean
        moment[:, ch:2 * ch] = lax.rsqrt(variance + EPS)
        moment_ref[...] = moment[...]
        grads[...] = jnp.zeros_like(grads)

    mean = window_rows(perm_ref, moment, step, windows, quarter, all_windows, cols, 0, ch)
    inverse = window_rows(perm_ref, moment, step, windows, quarter, all_windows, cols, ch, 2 * ch)
    hat_e = (pre_ref[0] - mean) * inverse
    hat_o = (pre_ref[1] - mean) * inverse
    a_e = (hat_e * sigmoid(hat_e)).astype(BF16)
    a_o = (hat_o * sigmoid(hat_o)).astype(BF16)
    v0, v1, v2, v3 = (v_ref[k * ch:(k + 1) * ch, :] for k in range(4))
    pre2 = shift_down(dot(a_o, v0), quarter) + dot(a_e, v1) + dot(a_o, v2) + shift_up(dot(a_e, v3), quarter)
    gate2 = sigmoid(pre2)
    h32 = (pre2 * gate2).astype(BF16).astype(F32)
    h = h32.astype(BF16)
    b0, b1, b2, b3 = (b_ref[:, k * ch:(k + 1) * ch] for k in range(4))
    d1_e = dot(h, b1) + shift_down(dot(h, b3), quarter)
    d1_o = dot(h, b2) + shift_up(dot(h, b0), quarter)
    gate_e = sigmoid(d1_e)
    gate_o = sigmoid(d1_o)
    de32 = (d1_e * gate_e)
    do32 = (d1_o * gate_o)
    de = de32.astype(BF16)
    do = do32.astype(BF16)
    de_up = shift_up(de32, quarter).astype(BF16)
    do_down = shift_down(do32, quarter).astype(BF16)
    c0, c1, c2, c3 = (c_ref[:, k * bins:(k + 1) * bins] for k in range(4))

    def delta(rebuilt, i):
        return ((rebuilt - normed_ref[i].astype(F32)) / total_windows).astype(BF16)

    g0 = delta(dot(de, c1) + dot(do_down, c3), 0)
    g1 = delta(dot(de, c2) + dot(do, c0), 1)
    g2 = delta(dot(do, c1) + dot(de, c3), 2)
    g3 = delta(dot(do, c2) + dot(de_up, c0), 3)
    halves = bins // ch
    base_b = 4 * bins
    base_v = base_b + 4 * ch

    def add_c(k, value):
        for j in range(halves):
            at = (k * halves + j) * ch
            grads[at:at + ch, :] += value[:, j * ch:(j + 1) * ch]

    add_c(0, dot_tn(de_up, g3) + dot_tn(do, g1))
    add_c(1, dot_tn(de, g0) + dot_tn(do, g2))
    add_c(2, dot_tn(de, g1) + dot_tn(do, g3))
    add_c(3, dot_tn(de, g2) + dot_tn(do_down, g0))
    back_e = shift_down(dot_nt(g3, c0), quarter) + dot_nt(g0, c1) + dot_nt(g1, c2) + dot_nt(g2, c3)
    back_o = dot_nt(g1, c0) + dot_nt(g2, c1) + dot_nt(g3, c2) + shift_up(dot_nt(g0, c3), quarter)
    dd_e = (back_e * (gate_e * (1.0 + d1_e * (1.0 - gate_e)))).astype(BF16)
    dd_o = (back_o * (gate_o * (1.0 + d1_o * (1.0 - gate_o)))).astype(BF16)
    h_up = shift_up(h32, quarter).astype(BF16)
    h_down = shift_down(h32, quarter).astype(BF16)
    grads[base_b:base_b + ch, :] += dot_tn(h_up, dd_o)
    grads[base_b + ch:base_b + 2 * ch, :] += dot_tn(h, dd_e)
    grads[base_b + 2 * ch:base_b + 3 * ch, :] += dot_tn(h, dd_o)
    grads[base_b + 3 * ch:base_b + 4 * ch, :] += dot_tn(h_down, dd_e)
    back2 = shift_down(dot_nt(dd_o, b0), quarter) + dot_nt(dd_e, b1) + dot_nt(dd_o, b2) + shift_up(dot_nt(dd_e, b3), quarter)
    d2_32 = (back2 * (gate2 * (1.0 + pre2 * (1.0 - gate2)))).astype(BF16).astype(F32)
    d2 = d2_32.astype(BF16)
    d2_up = shift_up(d2_32, quarter).astype(BF16)
    d2_down = shift_down(d2_32, quarter).astype(BF16)
    grads[base_v:base_v + ch, :] += dot_tn(a_o, d2_up)
    grads[base_v + ch:base_v + 2 * ch, :] += dot_tn(a_e, d2)
    grads[base_v + 2 * ch:base_v + 3 * ch, :] += dot_tn(a_o, d2)
    grads[base_v + 3 * ch:base_v + 4 * ch, :] += dot_tn(a_e, d2_down)
    fold_e = dot_nt(d2, v1) + shift_down(dot_nt(d2, v3), quarter)
    fold_o = dot_nt(d2, v2) + shift_up(dot_nt(d2, v0), quarter)
    gate_he = sigmoid(hat_e)
    gate_ho = sigmoid(hat_o)
    fold_e = fold_e * (gate_he * (1.0 + hat_e * (1.0 - gate_he)))
    fold_o = fold_o * (gate_ho * (1.0 + hat_o * (1.0 - gate_ho)))
    back_ref[0] = fold_e
    back_ref[1] = fold_o
    cross_e = fold_e * hat_e
    cross_o = fold_o * hat_o
    for w in range(windows):
        low, high = w * quarter, (w + 1) * quarter
        first = jnp.sum(fold_e[low:high] + fold_o[low:high], axis=0, keepdims=True)
        second = jnp.sum(cross_e[low:high] + cross_o[low:high], axis=0, keepdims=True)
        place = group_rank(perm_ref, step * windows + w, all_windows, cols)
        sums_ref[pl.ds(place, 1), 0:ch] = first
        sums_ref[pl.ds(place, 1), ch:2 * ch] = second

    @pl.when(step == pl.num_programs(0) - 1)
    def _():
        write_halves(core_ref, grads, own_ref, send_ref, (0, base_b, base_v, base_v + 4 * ch))


def middle_call(permutation, core, normed, pre, stat, w_enc2, w_dec1, w_dec2, quarter, cols, total_windows):
    bins = normed.shape[2]
    channels = w_enc2.shape[1]
    windows = normed.shape[1] // quarter
    total = 4 * bins + 8 * channels
    whole2 = lambda i, p, c: (0, 0)
    grid_spec = pltpu.PrefetchScalarGridSpec(
        num_scalar_prefetch=2,
        grid=(windows // STEP_WINDOWS,),
        in_specs=[
            ON_CHIP,
            ON_CHIP,
            ON_CHIP,
            ON_CHIP,
            ON_CHIP,
            ON_CHIP,
        ],
        out_specs=[
            ON_CHIP,
            ON_CHIP,
            ON_CHIP,
            pl.BlockSpec((windows, 2 * channels), whole2),
            ON_CHIP,
        ],
        scratch_shapes=[
            pltpu.VMEM((total, channels), F32),
            pltpu.VMEM((windows, 2 * channels), F32),
        ],
    )
    return pl.pallas_call(
        functools.partial(middle_kernel, quarter=quarter, cols=cols, total_windows=float(total_windows)),
        grid_spec=grid_spec,
        out_shape=[
            pltpu.VMEM((total // 2, channels), F32),
            pltpu.VMEM((total // 2, channels), F32),
            pltpu.VMEM(pre.shape, F32),
            jax.ShapeDtypeStruct((windows, 2 * channels), F32),
            pltpu.VMEM((windows, 2 * channels), F32),
        ],
        compiler_params=pltpu.CompilerParams(vmem_limit_bytes=30 * MIB),
        name="middle",
    )(permutation, core, on_chip(normed), on_chip(pre), on_chip(stat), on_chip(w_enc2), on_chip(w_dec1), on_chip(w_dec2))


def grad_kernel(perm_ref, core_ref, normed_ref, pre_ref, back_ref, moment_ref, sums_ref, own_ref, send_ref, grads, scale, *, quarter, cols):
    step = pl.program_id(0)
    bins = normed_ref.shape[2]
    ch = pre_ref.shape[2]
    windows = STEP_WINDOWS
    rows = windows * quarter
    normed_ref = step_rows(normed_ref, rows)
    pre_ref, back_ref = step_rows(pre_ref, rows), step_rows(back_ref, rows)
    all_windows = windows * pl.num_programs(0)

    @pl.when(step == 0)
    def _():
        scale[...] = jnp.sum(sums_ref[...], axis=0) / (2.0 * quarter * cols)
        grads[...] = jnp.zeros_like(grads)

    pick = functools.partial(window_rows, perm_ref, step=step, windows=windows, quarter=quarter, all_windows=all_windows, cols=cols)
    mean = pick(table=moment_ref, first=0, last=ch)
    inverse = pick(table=moment_ref, first=ch, last=2 * ch)
    first = pick(table=scale, first=0, last=ch)
    second = pick(table=scale, first=ch, last=2 * ch)
    hat_e = (pre_ref[0] - mean) * inverse
    hat_o = (pre_ref[1] - mean) * inverse
    de32 = (back_ref[0] - first - hat_e * second) * inverse
    do32 = (back_ref[1] - first - hat_o * second) * inverse
    de = de32.astype(BF16)
    do = do32.astype(BF16)
    de_up = shift_up(de32, quarter).astype(BF16)
    do_down = shift_down(do32, quarter).astype(BF16)
    f0, f1, f2, f3 = (normed_ref[i] for i in range(4))
    grads[0:bins, :] += dot_tn(f3, de_up) + dot_tn(f1, do)
    grads[bins:2 * bins, :] += dot_tn(f0, de) + dot_tn(f2, do)
    grads[2 * bins:3 * bins, :] += dot_tn(f1, de) + dot_tn(f3, do)
    grads[3 * bins:4 * bins, :] += dot_tn(f2, de) + dot_tn(f0, do_down)

    @pl.when(step == pl.num_programs(0) - 1)
    def _():
        write_halves(core_ref, grads, own_ref, send_ref, (0, 4 * bins))


def grad_call(permutation, core, normed, pre, back, moment, sums, quarter, cols):
    bins = normed.shape[2]
    channels = pre.shape[2]
    windows = normed.shape[1] // quarter
    grid_spec = pltpu.PrefetchScalarGridSpec(
        num_scalar_prefetch=2,
        grid=(windows // STEP_WINDOWS,),
        in_specs=[
            ON_CHIP,
            ON_CHIP,
            ON_CHIP,
            pl.BlockSpec(moment.shape, lambda i, p, c: (0, 0)),
            ON_CHIP,
        ],
        out_specs=[ON_CHIP] * 2,
        scratch_shapes=[pltpu.VMEM((4 * bins, channels), F32), pltpu.VMEM((windows, 2 * channels), F32)],
    )
    return pl.pallas_call(
        functools.partial(grad_kernel, quarter=quarter, cols=cols),
        grid_spec=grid_spec,
        out_shape=[pltpu.VMEM((2 * bins, channels), F32)] * 2,
        compiler_params=pltpu.CompilerParams(vmem_limit_bytes=16 * MIB),
        name="grad_enc1",
    )(permutation, core, on_chip(normed), on_chip(pre), on_chip(back), moment, on_chip(sums))


def swap_cores(values):
    return lax.ppermute(values, "core", [(0, 1), (1, 0)])


def exchange(values, axes):
    return lax.all_to_all(values, axes, split_axis=0, concat_axis=0, tiled=True)


def join_kernel(mine_ref, other_ref, out_ref, *, moments):
    mine, other = mine_ref[...], other_ref[...]
    total = mine + other
    width = total.shape[1] // 2
    if moments:
        apart = 0.5 * (mine[:, 0:width] - other[:, 0:width])
        total = jnp.concatenate([0.5 * total[:, 0:width], 0.5 * total[:, width:] + apart * apart], axis=1)
    for d in range(out_ref.shape[0]):
        out_ref[d] = total


def join_cores(mine, chips, moments):
    rows, width = mine.shape
    return pl.pallas_call(
        functools.partial(join_kernel, moments=moments),
        in_specs=[ON_CHIP] * 2,
        out_specs=ON_CHIP,
        out_shape=pltpu.VMEM((chips, rows, width), F32),
        compiler_params=pltpu.CompilerParams(vmem_limit_bytes=2 * MIB),
        name="join_cores",
    )(on_chip(mine), on_chip(swap_cores(mine)))


def exchange_copies(copies):
    return exchange(copies.reshape(-1, copies.shape[2]), "pair").reshape(copies.shape)


def chip_sums(parts, axes, chips):
    total = [(own + swap_cores(send)).astype(BF16).reshape(chips, -1, own.shape[1]) for own, send in parts]
    total = jnp.concatenate(total, axis=1)
    return exchange(total.reshape(-1, total.shape[2]), axes).reshape(total.shape)


def owner_kernel(in_ref, out_ref):
    chips, rows, width = in_ref.shape

    def body(i, total):
        return total + in_ref[i].astype(F32)

    total = lax.fori_loop(0, chips, body, jnp.zeros((rows, width), F32), unroll=4)
    largest = jnp.max(jnp.max(jnp.abs(total), axis=0, keepdims=True), axis=1, keepdims=True)
    exponent = jnp.clip(jnp.ceil(jnp.log2(largest)), -110.0, 126.0)
    total = total * jnp.exp2(14.0 - exponent)
    for k in range(width // LANES):
        out_ref[k * rows:(k + 1) * rows, :] = total[:, k * LANES:(k + 1) * LANES]
    out_ref[width // LANES * rows:, :] = jnp.broadcast_to(exponent, (SCALE_ROWS, LANES))


def owner_call(pieces):
    chips, rows, width = pieces.shape
    return pl.pallas_call(
        owner_kernel,
        out_shape=jax.ShapeDtypeStruct((width // LANES * rows + SCALE_ROWS, LANES), F32),
        compiler_params=pltpu.CompilerParams(vmem_limit_bytes=6 * MIB),
        name="owner_sum",
    )(pieces)


def gather_rows(piece, axes, chips):
    rows, width = piece.shape
    copies = jnp.broadcast_to(piece.astype(jnp.float16)[None], (chips, rows, width))
    return exchange(copies.reshape(-1, width), axes).reshape(chips, rows, width)


def place_kernel(half_ref, blocks_ref, *refs, rows, cut):
    grad_w_ref, grad_v_ref, grad_b_ref, grad_c_ref = refs[-4:]
    step = pl.program_id(0)
    channels = grad_w_ref.shape[1]
    late = rows - cut
    group = channels // cut

    def copy(out_ref, i, row, column):
        scale = jnp.exp2(blocks_ref[i, 2 * rows:2 * rows + 1, :] - 14.0)
        for k in range(2):
            block = blocks_ref[i, k * rows:(k + 1) * rows, :] * scale
            grad_w_ref[i * late:(i + 1) * late, k * LANES:(k + 1) * LANES] = block[cut:rows]
            out_ref[row:row + cut, column + k * LANES:column + (k + 1) * LANES] = block[0:cut]

    @pl.when(step < 2)
    def _():
        for i in range(2 * group):
            copy(grad_c_ref, i, i % group * cut, i // group * channels)

    @pl.when(step == 2)
    def _():
        for i in range(2 * group):
            copy(grad_b_ref, i, i % group * cut, i // group * channels)

    @pl.when(step == 3)
    def _():
        for i in range(2 * group):
            copy(grad_v_ref, i, i * cut, 0)


def place_call(half, blocks, rows, cut, channels, bins, earlier=()):
    chips, total, _ = blocks.shape
    group = channels // cut
    late = rows - cut
    grid_spec = pltpu.PrefetchScalarGridSpec(
        num_scalar_prefetch=1,
        grid=(4,),
        in_specs=[pl.BlockSpec((2 * group, total, LANES), lambda i, h: (i, 0, 0))]
        + [pl.BlockSpec(memory_space=pl.ANY)] * len(earlier),
        out_specs=[
            pl.BlockSpec((2 * group * late, channels), lambda i, h: (h[0] * 4 + i, 0)),
            pl.BlockSpec((2 * channels, channels), lambda i, h: (h[0], 0)),
            pl.BlockSpec((channels, 2 * channels), lambda i, h: (0, h[0])),
            pl.BlockSpec((channels, 2 * channels), lambda i, h: (0, h[0] * 2 + jnp.minimum(i, 1))),
        ],
    )
    return pl.pallas_call(
        functools.partial(place_kernel, rows=rows, cut=cut),
        grid_spec=grid_spec,
        out_shape=[
            jax.ShapeDtypeStruct((4 * bins, channels), F32),
            jax.ShapeDtypeStruct((4 * channels, channels), F32),
            jax.ShapeDtypeStruct((channels, 4 * channels), F32),
            jax.ShapeDtypeStruct((channels, 4 * bins), F32),
        ],
        input_output_aliases={2 + k: k for k in range(len(earlier))},
        compiler_params=pltpu.CompilerParams(vmem_limit_bytes=16 * MIB),
        cost_estimate=pl.CostEstimate(flops=chips * total * LANES, bytes_accessed=8 * chips * total * LANES, transcendentals=0),
        name="place_gradients",
    )(half, blocks, *earlier)


def local(spectra, sensor_ids, permutation, w_enc1, w_enc2, w_dec1, w_dec2):
    windows, frames, bins = spectra.shape
    channels = w_enc1.shape[1]
    chip_axes = ("row", "pair")
    every = ("row", "pair", "core")
    cols = lax.axis_size("pair") * lax.axis_size("core")
    chips = lax.axis_size("row") * lax.axis_size("pair")
    total_windows = windows * lax.axis_size("row") * cols
    sensors = total_windows // WIN_SENSOR
    chunks = bins // LANES
    quarter = frames // 4
    core_index = lax.axis_index("core")
    core = core_index.astype(jnp.int32).reshape(1)

    logs, sums = sums_call(spectra, sensor_ids)
    sums, core = lax.optimization_barrier((sums, core))
    sums = exchange(sums, every)
    coef = exchange(stats_call(sums, windows, chunks, sensors, WIN_SENSOR * frames), every)
    normed, pre, stat = enc1_call(permutation, logs, coef, w_enc1, cols)
    stat = exchange_copies(join_cores(stat, cols // 2, True))
    own, send, back, moment, moments = middle_call(
        permutation, core, normed, pre, stat, w_enc2, w_dec1, w_dec2, quarter, cols, total_windows)
    moments, send = lax.optimization_barrier((join_cores(moments, cols // 2, False), send))
    moments = exchange_copies(moments)
    late = grad_call(permutation, core, normed, pre, back, moment, moments, quarter, cols)
    piece = owner_call(chip_sums([(own, send), late], chip_axes, chips))
    mine = gather_rows(piece, chip_axes, chips)
    other = swap_cores(mine)
    rows, cut = own.shape[0] // chips + late[0].shape[0] // chips, own.shape[0] // chips
    placed = place_call(core, mine.astype(F32), rows, cut, channels, bins)
    return tuple(place_call(1 - core, other.astype(F32), rows, cut, channels, bins, placed))


def solution(mesh):
    rows, cols = mesh.devices.shape
    inner = Mesh(mesh.devices.reshape(rows, cols // 2, 2), ("row", "pair", "core"))
    spread = ("row", "pair", "core")
    return jax.shard_map(
        local,
        mesh=inner,
        in_specs=(P(spread, None, None), P(spread, None), P(spread), P(), P(), P(), P()),
        out_specs=(P(), P(), P(), P()),
        check_vma=False,
    )
```

```python
import functools

import jax
import jax.numpy as jnp
from jax import lax
from jax.experimental import pallas as pl
from jax.experimental.pallas import tpu as pltpu
from jax.sharding import Mesh, PartitionSpec as P

WIN_SENSOR = 8
EPS = 1e-05
F32 = jnp.float32
BF16 = jnp.bfloat16
LANES = 128
STEP_WINDOWS = 16
SORT_WINDOWS = 8
SCALE_ROWS = 8
MIB = 1024 * 1024


ON_CHIP = pl.BlockSpec(memory_space=pltpu.VMEM)


def on_chip(values):
    return pltpu.with_memory_space_constraint(values, pltpu.VMEM)


def in_hbm(values):
    return pltpu.with_memory_space_constraint(values, pltpu.HBM)


def step_rows(ref, rows):
    return ref.at[:, pl.ds(pl.multiple_of(pl.program_id(0) * rows, rows), rows), :]


def dot(left, right):
    return jnp.dot(left, right, preferred_element_type=F32)


def dot_nt(left, right):
    return lax.dot_general(left, right, (((1,), (1,)), ((), ())), preferred_element_type=F32)


def dot_tn(left, right):
    return lax.dot_general(left, right, (((0,), (0,)), ((), ())), preferred_element_type=F32)


def split3(values):
    first = values.astype(BF16)
    rest = values - first.astype(F32)
    second = rest.astype(BF16)
    third = (rest - second.astype(F32)).astype(BF16)
    return first, second, third


def sigmoid(values):
    return 1.0 / (1.0 + jnp.exp(-values))


def shift_down(values, period):
    rows = lax.broadcasted_iota(jnp.int32, values.shape, 0) % period
    return jnp.where(rows == 0, 0.0, pltpu.roll(values, 1, 0))


def shift_up(values, period):
    total = values.shape[0]
    rows = lax.broadcasted_iota(jnp.int32, values.shape, 0) % period
    return jnp.where(rows == period - 1, 0.0, pltpu.roll(values, total - 1, 0))


def group_rank(perm_ref, window, window_dev, col_count):
    trainer = perm_ref[window] // window_dev
    per_row = 2
    return (trainer // col_count) * per_row + trainer % per_row


def sums_kernel(ids_ref, spec_ref, log_ref, out_ref, acc, *, chunks, count):
    step = pl.program_id(0)
    windows, frames, bins = spec_ref.shape
    rows = 16

    for w in range(windows):
        def body(i, carry):
            total, square = carry
            start = pl.multiple_of(i * rows, rows)
            value = jnp.log(1.0 + spec_ref[w, pl.ds(start, rows), :].astype(F32))
            for k in range(chunks):
                log_ref[step * windows + w, k, pl.ds(start, rows), :] = value[:, k * LANES:(k + 1) * LANES]
            value_sq = value * value
            return (total + value[0:8] + value[8:16], square + value_sq[0:8] + value_sq[8:16])

        zero = jnp.zeros((8, bins), F32)
        total, square = lax.fori_loop(0, frames // rows, body, (zero, zero), unroll=8)
        total = jnp.sum(total, axis=0, keepdims=True)
        square = jnp.sum(square, axis=0, keepdims=True)
        pieces = [total[:, k * LANES:(k + 1) * LANES] for k in range(chunks)]
        pieces += [square[:, k * LANES:(k + 1) * LANES] for k in range(chunks)]
        start = pl.multiple_of((step * windows + w) * 2 * chunks, 2 * chunks)
        acc[pl.ds(start, 2 * chunks), :] = jnp.concatenate(pieces, axis=0)

    @pl.when(step == pl.num_programs(0) - 1)
    def _():
        acc[LANES:2 * LANES, :] = jnp.zeros((LANES, LANES), F32)
        for w in range(count):
            acc[LANES + w:LANES + w + 1, :] = jnp.full((1, LANES), ids_ref[w], jnp.int32).astype(F32)
        out_ref[pl.ds(0, LANES, stride=2), :] = acc[0:LANES, :].T
        out_ref[pl.ds(1, LANES, stride=2), :] = acc[LANES:2 * LANES, :].T


def sums_call(spectra, sensor_ids):
    windows, frames, bins = spectra.shape
    chunks = bins // LANES
    grid_spec = pltpu.PrefetchScalarGridSpec(
        num_scalar_prefetch=1,
        grid=(windows // SORT_WINDOWS,),
        in_specs=[pl.BlockSpec((SORT_WINDOWS, frames, bins), lambda i, s: (i, 0, 0))],
        out_specs=[ON_CHIP, pl.BlockSpec((2 * LANES, LANES), lambda i, s: (0, 0))],
        scratch_shapes=[pltpu.VMEM((2 * LANES, LANES), F32)],
    )
    return pl.pallas_call(
        functools.partial(sums_kernel, chunks=chunks, count=windows),
        grid_spec=grid_spec,
        out_shape=[
            pltpu.VMEM((windows, chunks, frames, LANES), F32),
            jax.ShapeDtypeStruct((2 * LANES, LANES), F32),
        ],
        compiler_params=pltpu.CompilerParams(vmem_limit_bytes=10 * MIB),
        name="log_and_sum",
    )(in_hbm(sensor_ids.reshape(windows)), in_hbm(spectra))


def stats_kernel(in_ref, out_ref, *, windows, chunks, sensors, per_sensor):
    width = 2 * chunks
    data = in_ref[pl.ds(0, LANES, stride=2), :].T
    labels = in_ref[pl.ds(1, LANES, stride=2), :].T
    sensor_rows = lax.broadcasted_iota(jnp.int32, (sensors, LANES), 0).astype(F32)
    tables = [(sensor_rows == labels[w:w + 1, :]).astype(F32).astype(BF16) for w in range(windows)]
    table = jnp.concatenate(tables, axis=1)
    values = jnp.concatenate([data[w * width:(w + 1) * width, :] for w in range(windows)], axis=1)
    parts = dot_nt(jnp.concatenate(split3(values), axis=0), table)
    sums = parts[0:width] + parts[width:2 * width] + parts[2 * width:3 * width]
    center = sums[0:chunks] / per_sensor
    factor = lax.rsqrt(sums[chunks:width] / per_sensor - center * center + EPS)
    both = jnp.concatenate([center, factor], axis=0)
    back = dot(jnp.concatenate(split3(both), axis=0), table)
    back = back[0:width] + back[width:2 * width] + back[2 * width:3 * width]
    rows = jnp.concatenate([back[:, w * LANES:(w + 1) * LANES] for w in range(windows)], axis=0)
    out_ref[...] = rows.T


def stats_call(received, windows, chunks, sensors, per_sensor):
    return pl.pallas_call(
        functools.partial(stats_kernel, windows=windows, chunks=chunks, sensors=sensors, per_sensor=float(per_sensor)),
        out_shape=jax.ShapeDtypeStruct((LANES, LANES), F32),
        compiler_params=pltpu.CompilerParams(vmem_limit_bytes=12 * MIB),
        name="sensor_stats",
    )(received)


def enc1_kernel(perm_ref, log_ref, coef_ref, w_ref, normed_ref, pre_ref, stat_ref, coef, *, cols):
    step = pl.program_id(0)
    all_windows, chunks, frames, _ = log_ref.shape
    quarter = frames // 4
    bins = chunks * LANES
    windows = STEP_WINDOWS
    normed_ref, pre_ref = (step_rows(ref, windows * quarter) for ref in (normed_ref, pre_ref))
    channels = w_ref.shape[1]
    width = 2 * chunks

    @pl.when(step == 0)
    def _():
        coef[...] = coef_ref[...].T

    for w in range(windows):
        start = pl.multiple_of((step * windows + w) * width, width)
        both = coef[pl.ds(start, width), :]
        low, high = w * quarter, (w + 1) * quarter
        for k in range(chunks):
            center = both[k:k + 1, :]
            factor = both[chunks + k:chunks + k + 1, :]
            for i in range(4):
                value = log_ref[step * windows + w, k, pl.ds(i, quarter, stride=4), :]
                normed_ref[i, low:high, k * LANES:(k + 1) * LANES] = ((value - center) * factor).astype(BF16)

    w0, w1, w2, w3 = (w_ref[k * bins:(k + 1) * bins, :] for k in range(4))
    f0, f1, f2, f3 = (normed_ref[i] for i in range(4))
    even = shift_down(dot(f3, w0), quarter) + dot(f0, w1) + dot(f1, w2) + dot(f2, w3)
    odd = dot(f1, w0) + dot(f2, w1) + dot(f3, w2) + shift_up(dot(f0, w3), quarter)
    pre_ref[0] = even
    pre_ref[1] = odd
    for w in range(windows):
        part_e = even[w * quarter:(w + 1) * quarter]
        part_o = odd[w * quarter:(w + 1) * quarter]
        mean = (jnp.sum(part_e, axis=0, keepdims=True) + jnp.sum(part_o, axis=0, keepdims=True)) / (2 * quarter)
        diff_e = part_e - mean
        diff_o = part_o - mean
        spread = (jnp.sum(diff_e * diff_e, axis=0, keepdims=True) + jnp.sum(diff_o * diff_o, axis=0, keepdims=True)) / (2 * quarter)
        place = group_rank(perm_ref, step * windows + w, all_windows, cols)
        stat_ref[pl.ds(place, 1), 0:channels] = mean
        stat_ref[pl.ds(place, 1), channels:2 * channels] = spread


def enc1_call(permutation, logs, coef, w_enc1, cols):
    windows, chunks, frames, _ = logs.shape
    channels = w_enc1.shape[1]
    rows = windows * frames // 4
    grid_spec = pltpu.PrefetchScalarGridSpec(
        num_scalar_prefetch=1,
        grid=(windows // STEP_WINDOWS,),
        in_specs=[ON_CHIP, pl.BlockSpec((LANES, LANES), lambda i, p: (0, 0)), ON_CHIP],
        out_specs=[ON_CHIP] * 3,
        scratch_shapes=[pltpu.VMEM((LANES, LANES), F32)],
    )
    return pl.pallas_call(
        functools.partial(enc1_kernel, cols=cols),
        grid_spec=grid_spec,
        out_shape=[
            pltpu.VMEM((4, rows, chunks * LANES), BF16),
            pltpu.VMEM((2, rows, channels), F32),
            pltpu.VMEM((windows, 2 * channels), F32),
        ],
        compiler_params=pltpu.CompilerParams(vmem_limit_bytes=16 * MIB),
        name="normalize_enc1",
    )(permutation, on_chip(logs), coef, on_chip(w_enc1))


def window_rows(perm_ref, table, step, windows, quarter, all_windows, cols, first, last):
    parts = []
    for w in range(windows):
        place = group_rank(perm_ref, step * windows + w, all_windows, cols)
        parts.append(jnp.broadcast_to(table[pl.ds(place, 1), first:last], (quarter, last - first)))
    return jnp.concatenate(parts, axis=0)


def write_halves(core_ref, grads, own_ref, send_ref, bounds):
    for first, last in zip(bounds[:-1], bounds[1:]):
        half = (last - first) // 2
        at = first // 2
        own = pl.multiple_of(first + core_ref[0] * half, half)
        send = pl.multiple_of(first + (1 - core_ref[0]) * half, half)
        own_ref[at:at + half, :] = grads[pl.ds(own, half), :]
        send_ref[at:at + half, :] = grads[pl.ds(send, half), :]


def middle_kernel(perm_ref, core_ref, normed_ref, pre_ref, stat_ref, v_ref, b_ref, c_ref,
                  own_ref, send_ref, back_ref, moment_ref, sums_ref,
                  grads, moment, *, quarter, cols, total_windows):
    step = pl.program_id(0)
    channels = v_ref.shape[1]
    bins = normed_ref.shape[2]
    windows = STEP_WINDOWS
    normed_ref, pre_ref, back_ref = (step_rows(ref, windows * quarter) for ref in (normed_ref, pre_ref, back_ref))
    all_windows = windows * pl.num_programs(0)
    ch = channels

    @pl.when(step == 0)
    def _():
        means = stat_ref[:, :, 0:ch]
        mean = jnp.mean(means, axis=0)
        diff = means - mean[None]
        variance = jnp.mean(stat_ref[:, :, ch:2 * ch] + diff * diff, axis=0)
        moment[:, 0:ch] = mean
        moment[:, ch:2 * ch] = lax.rsqrt(variance + EPS)
        moment_ref[...] = moment[...]
        grads[...] = jnp.zeros_like(grads)

    mean = window_rows(perm_ref, moment, step, windows, quarter, all_windows, cols, 0, ch)
    inverse = window_rows(perm_ref, moment, step, windows, quarter, all_windows, cols, ch, 2 * ch)
    hat_e = (pre_ref[0] - mean) * inverse
    hat_o = (pre_ref[1] - mean) * inverse
    a_e = (hat_e * sigmoid(hat_e)).astype(BF16)
    a_o = (hat_o * sigmoid(hat_o)).astype(BF16)
    v0, v1, v2, v3 = (v_ref[k * ch:(k + 1) * ch, :] for k in range(4))
    pre2 = shift_down(dot(a_o, v0), quarter) + dot(a_e, v1) + dot(a_o, v2) + shift_up(dot(a_e, v3), quarter)
    gate2 = sigmoid(pre2)
    h32 = (pre2 * gate2).astype(BF16).astype(F32)
    h = h32.astype(BF16)
    b0, b1, b2, b3 = (b_ref[:, k * ch:(k + 1) * ch] for k in range(4))
    d1_e = dot(h, b1) + shift_down(dot(h, b3), quarter)
    d1_o = dot(h, b2) + shift_up(dot(h, b0), quarter)
    gate_e = sigmoid(d1_e)
    gate_o = sigmoid(d1_o)
    de32 = (d1_e * gate_e)
    do32 = (d1_o * gate_o)
    de = de32.astype(BF16)
    do = do32.astype(BF16)
    de_up = shift_up(de32, quarter).astype(BF16)
    do_down = shift_down(do32, quarter).astype(BF16)
    c0, c1, c2, c3 = (c_ref[:, k * bins:(k + 1) * bins] for k in range(4))

    def delta(rebuilt, i):
        return ((rebuilt - normed_ref[i].astype(F32)) / total_windows).astype(BF16)

    g0 = delta(dot(de, c1) + dot(do_down, c3), 0)
    g1 = delta(dot(de, c2) + dot(do, c0), 1)
    g2 = delta(dot(do, c1) + dot(de, c3), 2)
    g3 = delta(dot(do, c2) + dot(de_up, c0), 3)
    halves = bins // ch
    base_b = 4 * bins
    base_v = base_b + 4 * ch

    def add_c(k, value):
        for j in range(halves):
            at = (k * halves + j) * ch
            grads[at:at + ch, :] += value[:, j * ch:(j + 1) * ch]

    add_c(0, dot_tn(de_up, g3) + dot_tn(do, g1))
    add_c(1, dot_tn(de, g0) + dot_tn(do, g2))
    add_c(2, dot_tn(de, g1) + dot_tn(do, g3))
    add_c(3, dot_tn(de, g2) + dot_tn(do_down, g0))
    back_e = shift_down(dot_nt(g3, c0), quarter) + dot_nt(g0, c1) + dot_nt(g1, c2) + dot_nt(g2, c3)
    back_o = dot_nt(g1, c0) + dot_nt(g2, c1) + dot_nt(g3, c2) + shift_up(dot_nt(g0, c3), quarter)
    dd_e = (back_e * (gate_e * (1.0 + d1_e * (1.0 - gate_e)))).astype(BF16)
    dd_o = (back_o * (gate_o * (1.0 + d1_o * (1.0 - gate_o)))).astype(BF16)
    h_up = shift_up(h32, quarter).astype(BF16)
    h_down = shift_down(h32, quarter).astype(BF16)
    grads[base_b:base_b + ch, :] += dot_tn(h_up, dd_o)
    grads[base_b + ch:base_b + 2 * ch, :] += dot_tn(h, dd_e)
    grads[base_b + 2 * ch:base_b + 3 * ch, :] += dot_tn(h, dd_o)
    grads[base_b + 3 * ch:base_b + 4 * ch, :] += dot_tn(h_down, dd_e)
    back2 = shift_down(dot_nt(dd_o, b0), quarter) + dot_nt(dd_e, b1) + dot_nt(dd_o, b2) + shift_up(dot_nt(dd_e, b3), quarter)
    d2_32 = (back2 * (gate2 * (1.0 + pre2 * (1.0 - gate2)))).astype(BF16).astype(F32)
    d2 = d2_32.astype(BF16)
    d2_up = shift_up(d2_32, quarter).astype(BF16)
    d2_down = shift_down(d2_32, quarter).astype(BF16)
    grads[base_v:base_v + ch, :] += dot_tn(a_o, d2_up)
    grads[base_v + ch:base_v + 2 * ch, :] += dot_tn(a_e, d2)
    grads[base_v + 2 * ch:base_v + 3 * ch, :] += dot_tn(a_o, d2)
    grads[base_v + 3 * ch:base_v + 4 * ch, :] += dot_tn(a_e, d2_down)
    fold_e = dot_nt(d2, v1) + shift_down(dot_nt(d2, v3), quarter)
    fold_o = dot_nt(d2, v2) + shift_up(dot_nt(d2, v0), quarter)
    gate_he = sigmoid(hat_e)
    gate_ho = sigmoid(hat_o)
    fold_e = fold_e * (gate_he * (1.0 + hat_e * (1.0 - gate_he)))
    fold_o = fold_o * (gate_ho * (1.0 + hat_o * (1.0 - gate_ho)))
    back_ref[0] = fold_e
    back_ref[1] = fold_o
    cross_e = fold_e * hat_e
    cross_o = fold_o * hat_o
    for w in range(windows):
        low, high = w * quarter, (w + 1) * quarter
        first = jnp.sum(fold_e[low:high] + fold_o[low:high], axis=0, keepdims=True)
        second = jnp.sum(cross_e[low:high] + cross_o[low:high], axis=0, keepdims=True)
        place = group_rank(perm_ref, step * windows + w, all_windows, cols)
        sums_ref[pl.ds(place, 1), 0:ch] = first
        sums_ref[pl.ds(place, 1), ch:2 * ch] = second

    @pl.when(step == pl.num_programs(0) - 1)
    def _():
        write_halves(core_ref, grads, own_ref, send_ref, (0, base_b, base_v, base_v + 4 * ch))


def middle_call(permutation, core, normed, pre, stat, w_enc2, w_dec1, w_dec2, quarter, cols, total_windows):
    bins = normed.shape[2]
    channels = w_enc2.shape[1]
    windows = normed.shape[1] // quarter
    total = 4 * bins + 8 * channels
    whole2 = lambda i, p, c: (0, 0)
    grid_spec = pltpu.PrefetchScalarGridSpec(
        num_scalar_prefetch=2,
        grid=(windows // STEP_WINDOWS,),
        in_specs=[
            ON_CHIP,
            ON_CHIP,
            ON_CHIP,
            ON_CHIP,
            ON_CHIP,
            ON_CHIP,
        ],
        out_specs=[
            ON_CHIP,
            ON_CHIP,
            ON_CHIP,
            pl.BlockSpec((windows, 2 * channels), whole2),
            ON_CHIP,
        ],
        scratch_shapes=[
            pltpu.VMEM((total, channels), F32),
            pltpu.VMEM((windows, 2 * channels), F32),
        ],
    )
    return pl.pallas_call(
        functools.partial(middle_kernel, quarter=quarter, cols=cols, total_windows=float(total_windows)),
        grid_spec=grid_spec,
        out_shape=[
            pltpu.VMEM((total // 2, channels), F32),
            pltpu.VMEM((total // 2, channels), F32),
            pltpu.VMEM(pre.shape, F32),
            jax.ShapeDtypeStruct((windows, 2 * channels), F32),
            pltpu.VMEM((windows, 2 * channels), F32),
        ],
        compiler_params=pltpu.CompilerParams(vmem_limit_bytes=30 * MIB),
        name="middle",
    )(permutation, core, on_chip(normed), on_chip(pre), on_chip(stat), on_chip(w_enc2), on_chip(w_dec1), on_chip(w_dec2))


def grad_kernel(perm_ref, core_ref, normed_ref, pre_ref, back_ref, moment_ref, sums_ref, own_ref, send_ref, grads, scale, *, quarter, cols):
    step = pl.program_id(0)
    bins = normed_ref.shape[2]
    ch = pre_ref.shape[2]
    windows = STEP_WINDOWS
    rows = windows * quarter
    normed_ref = step_rows(normed_ref, rows)
    pre_ref, back_ref = step_rows(pre_ref, rows), step_rows(back_ref, rows)
    all_windows = windows * pl.num_programs(0)

    @pl.when(step == 0)
    def _():
        scale[...] = jnp.sum(sums_ref[...], axis=0) / (2.0 * quarter * cols)
        grads[...] = jnp.zeros_like(grads)

    pick = functools.partial(window_rows, perm_ref, step=step, windows=windows, quarter=quarter, all_windows=all_windows, cols=cols)
    mean = pick(table=moment_ref, first=0, last=ch)
    inverse = pick(table=moment_ref, first=ch, last=2 * ch)
    first = pick(table=scale, first=0, last=ch)
    second = pick(table=scale, first=ch, last=2 * ch)
    hat_e = (pre_ref[0] - mean) * inverse
    hat_o = (pre_ref[1] - mean) * inverse
    de32 = (back_ref[0] - first - hat_e * second) * inverse
    do32 = (back_ref[1] - first - hat_o * second) * inverse
    de = de32.astype(BF16)
    do = do32.astype(BF16)
    de_up = shift_up(de32, quarter).astype(BF16)
    do_down = shift_down(do32, quarter).astype(BF16)
    f0, f1, f2, f3 = (normed_ref[i] for i in range(4))
    grads[0:bins, :] += dot_tn(f3, de_up) + dot_tn(f1, do)
    grads[bins:2 * bins, :] += dot_tn(f0, de) + dot_tn(f2, do)
    grads[2 * bins:3 * bins, :] += dot_tn(f1, de) + dot_tn(f3, do)
    grads[3 * bins:4 * bins, :] += dot_tn(f2, de) + dot_tn(f0, do_down)

    @pl.when(step == pl.num_programs(0) - 1)
    def _():
        write_halves(core_ref, grads, own_ref, send_ref, (0, 4 * bins))


def grad_call(permutation, core, normed, pre, back, moment, sums, quarter, cols):
    bins = normed.shape[2]
    channels = pre.shape[2]
    windows = normed.shape[1] // quarter
    grid_spec = pltpu.PrefetchScalarGridSpec(
        num_scalar_prefetch=2,
        grid=(windows // STEP_WINDOWS,),
        in_specs=[
            ON_CHIP,
            ON_CHIP,
            ON_CHIP,
            pl.BlockSpec(moment.shape, lambda i, p, c: (0, 0)),
            ON_CHIP,
        ],
        out_specs=[ON_CHIP] * 2,
        scratch_shapes=[pltpu.VMEM((4 * bins, channels), F32), pltpu.VMEM((windows, 2 * channels), F32)],
    )
    return pl.pallas_call(
        functools.partial(grad_kernel, quarter=quarter, cols=cols),
        grid_spec=grid_spec,
        out_shape=[pltpu.VMEM((2 * bins, channels), F32)] * 2,
        compiler_params=pltpu.CompilerParams(vmem_limit_bytes=16 * MIB),
        name="grad_enc1",
    )(permutation, core, on_chip(normed), on_chip(pre), on_chip(back), moment, on_chip(sums))


def swap_cores(values):
    return lax.ppermute(values, "core", [(0, 1), (1, 0)])


def exchange(values, axes):
    return lax.all_to_all(values, axes, split_axis=0, concat_axis=0, tiled=True)


def join_kernel(mine_ref, other_ref, out_ref, *, moments):
    mine, other = mine_ref[...], other_ref[...]
    total = mine + other
    width = total.shape[1] // 2
    if moments:
        apart = 0.5 * (mine[:, 0:width] - other[:, 0:width])
        total = jnp.concatenate([0.5 * total[:, 0:width], 0.5 * total[:, width:] + apart * apart], axis=1)
    for d in range(out_ref.shape[0]):
        out_ref[d] = total


def join_cores(mine, chips, moments):
    rows, width = mine.shape
    return pl.pallas_call(
        functools.partial(join_kernel, moments=moments),
        in_specs=[ON_CHIP] * 2,
        out_specs=ON_CHIP,
        out_shape=pltpu.VMEM((chips, rows, width), F32),
        compiler_params=pltpu.CompilerParams(vmem_limit_bytes=2 * MIB),
        name="join_cores",
    )(on_chip(mine), on_chip(swap_cores(mine)))


def exchange_copies(copies):
    return exchange(copies.reshape(-1, copies.shape[2]), "pair").reshape(copies.shape)


def chip_sums(parts, axes, chips):
    total = [(own + swap_cores(send)).astype(BF16).reshape(chips, -1, own.shape[1]) for own, send in parts]
    total = jnp.concatenate(total, axis=1)
    return exchange(total.reshape(-1, total.shape[2]), axes).reshape(total.shape)


def owner_kernel(in_ref, out_ref):
    chips, rows, width = in_ref.shape

    def body(i, total):
        return total + in_ref[i].astype(F32)

    total = lax.fori_loop(0, chips, body, jnp.zeros((rows, width), F32), unroll=4)
    largest = jnp.max(jnp.max(jnp.abs(total), axis=0, keepdims=True), axis=1, keepdims=True)
    exponent = jnp.clip(jnp.ceil(jnp.log2(largest)), -110.0, 126.0)
    total = total * jnp.exp2(14.0 - exponent)
    for k in range(width // LANES):
        out_ref[k * rows:(k + 1) * rows, :] = total[:, k * LANES:(k + 1) * LANES]
    out_ref[width // LANES * rows:, :] = jnp.broadcast_to(exponent, (SCALE_ROWS, LANES))


def owner_call(pieces):
    chips, rows, width = pieces.shape
    return pl.pallas_call(
        owner_kernel,
        out_shape=jax.ShapeDtypeStruct((width // LANES * rows + SCALE_ROWS, LANES), F32),
        compiler_params=pltpu.CompilerParams(vmem_limit_bytes=6 * MIB),
        name="owner_sum",
    )(pieces)


def gather_rows(piece, axes, chips):
    rows, width = piece.shape
    copies = jnp.broadcast_to(piece.astype(jnp.float16)[None], (chips, rows, width))
    return exchange(copies.reshape(-1, width), axes).reshape(chips, rows, width)


def place_kernel(half_ref, blocks_ref, *refs, rows, cut):
    grad_w_ref, grad_v_ref, grad_b_ref, grad_c_ref = refs[-4:]
    step = pl.program_id(0)
    channels = grad_w_ref.shape[1]
    late = rows - cut
    group = channels // cut

    def copy(out_ref, i, row, column):
        scale = jnp.exp2(blocks_ref[i, 2 * rows:2 * rows + 1, :] - 14.0)
        for k in range(2):
            block = blocks_ref[i, k * rows:(k + 1) * rows, :] * scale
            grad_w_ref[i * late:(i + 1) * late, k * LANES:(k + 1) * LANES] = block[cut:rows]
            out_ref[row:row + cut, column + k * LANES:column + (k + 1) * LANES] = block[0:cut]

    @pl.when(step < 2)
    def _():
        for i in range(2 * group):
            copy(grad_c_ref, i, i % group * cut, i // group * channels)

    @pl.when(step == 2)
    def _():
        for i in range(2 * group):
            copy(grad_b_ref, i, i % group * cut, i // group * channels)

    @pl.when(step == 3)
    def _():
        for i in range(2 * group):
            copy(grad_v_ref, i, i * cut, 0)


def place_call(half, blocks, rows, cut, channels, bins, earlier=()):
    chips, total, _ = blocks.shape
    group = channels // cut
    late = rows - cut
    grid_spec = pltpu.PrefetchScalarGridSpec(
        num_scalar_prefetch=1,
        grid=(4,),
        in_specs=[pl.BlockSpec((2 * group, total, LANES), lambda i, h: (i, 0, 0))]
        + [pl.BlockSpec(memory_space=pl.ANY)] * len(earlier),
        out_specs=[
            pl.BlockSpec((2 * group * late, channels), lambda i, h: (h[0] * 4 + i, 0)),
            pl.BlockSpec((2 * channels, channels), lambda i, h: (h[0], 0)),
            pl.BlockSpec((channels, 2 * channels), lambda i, h: (0, h[0])),
            pl.BlockSpec((channels, 2 * channels), lambda i, h: (0, h[0] * 2 + jnp.minimum(i, 1))),
        ],
    )
    return pl.pallas_call(
        functools.partial(place_kernel, rows=rows, cut=cut),
        grid_spec=grid_spec,
        out_shape=[
            jax.ShapeDtypeStruct((4 * bins, channels), F32),
            jax.ShapeDtypeStruct((4 * channels, channels), F32),
            jax.ShapeDtypeStruct((channels, 4 * channels), F32),
            jax.ShapeDtypeStruct((channels, 4 * bins), F32),
        ],
        input_output_aliases={2 + k: k for k in range(len(earlier))},
        compiler_params=pltpu.CompilerParams(vmem_limit_bytes=16 * MIB),
        cost_estimate=pl.CostEstimate(flops=chips * total * LANES, bytes_accessed=8 * chips * total * LANES, transcendentals=0),
        name="place_gradients",
    )(half, blocks, *earlier)


def local(spectra, sensor_ids, permutation, w_enc1, w_enc2, w_dec1, w_dec2):
    windows, frames, bins = spectra.shape
    channels = w_enc1.shape[1]
    chip_axes = ("row", "pair")
    every = ("row", "pair", "core")
    cols = lax.axis_size("pair") * lax.axis_size("core")
    chips = lax.axis_size("row") * lax.axis_size("pair")
    total_windows = windows * lax.axis_size("row") * cols
    sensors = total_windows // WIN_SENSOR
    chunks = bins // LANES
    quarter = frames // 4
    core_index = lax.axis_index("core")
    core = core_index.astype(jnp.int32).reshape(1)

    logs, sums = sums_call(spectra, sensor_ids)
    sums, core = lax.optimization_barrier((sums, core))
    sums = exchange(sums, every)
    coef = exchange(stats_call(sums, windows, chunks, sensors, WIN_SENSOR * frames), every)
    normed, pre, stat = enc1_call(permutation, logs, coef, w_enc1, cols)
    stat = exchange_copies(join_cores(stat, cols // 2, True))
    own, send, back, moment, moments = middle_call(
        permutation, core, normed, pre, stat, w_enc2, w_dec1, w_dec2, quarter, cols, total_windows)
    moments, send = lax.optimization_barrier((join_cores(moments, cols // 2, False), send))
    moments = exchange_copies(moments)
    late = grad_call(permutation, core, normed, pre, back, moment, moments, quarter, cols)
    piece = owner_call(chip_sums([(own, send), late], chip_axes, chips))
    mine = gather_rows(piece, chip_axes, chips)
    other = swap_cores(mine)
    rows, cut = own.shape[0] // chips + late[0].shape[0] // chips, own.shape[0] // chips
    placed = place_call(core, mine.astype(F32), rows, cut, channels, bins)
    return tuple(place_call(1 - core, other.astype(F32), rows, cut, channels, bins, placed))


def solution(mesh):
    rows, cols = mesh.devices.shape
    inner = Mesh(mesh.devices.reshape(rows, cols // 2, 2), ("row", "pair", "core"))
    spread = ("row", "pair", "core")
    return jax.shard_map(
        local,
        mesh=inner,
        in_specs=(P(spread, None, None), P(spread, None), P(spread), P(), P(), P(), P()),
        out_specs=(P(), P(), P(), P()),
        check_vma=False,
    )
```
